32 devices in a mesh: ctx: 8 (over y, x, core), fsdp: 4 (over z).
Axes of the slice: x: 2, y: 2, z: 4, core: 2. Of those that a mesh axis runs over, the one named last changes fastest.
Arguments:
- tokens: bfloat16 [4, 2048, 1024], P('fsdp', 'ctx'), may hold values from -6 to 6
- encoded: bfloat16 [4, 2048, 1024], P('fsdp', 'ctx'), may hold values from -6 to 6
- cotangent: bfloat16 [4, 2048, 1024], P('fsdp', 'ctx'), may hold values from -6 to 6
- target_segments: int32 [4, 2048], P('fsdp'), may hold values from 0 to 15, never falling along the last dimension, each value on 1 to 512 neighbouring positions
- source_segments: int32 [4, 2048], P('fsdp'), may hold values from 0 to 15, never falling along the last dimension, each value on 1 to 512 neighbouring positions
- block_order: int32 [4, 16], P('fsdp'), may hold values from 0 to 15, each once within a row
- norm_gain: bfloat16 [3, 1024], P(None, 'fsdp'), may hold values from 0.099609375 to 1.8984375
- norm_shift: bfloat16 [3, 1024], P(None, 'fsdp'), may hold values from -4 to 4
- inward: bfloat16 [2, 1024, 3072], P(None, 'fsdp'), may hold values from -0.1875 to 0.1875
- inbias: bfloat16 [2, 2, 1024], P(None, None, 'fsdp'), may hold values from -6 to 6
- outward: bfloat16 [2, 1024, 1024], P(None, 'fsdp'), may hold values from -0.75 to 0.75
- outbias: bfloat16 [2, 1024], P(None, 'fsdp'), may hold values from -4 to 4
- upward: bfloat16 [1024, 4096], P('fsdp'), may hold values from -0.1875 to 0.1875
- upbias: bfloat16 [4096], P('fsdp'), may hold values from -4 to 4
- downward: bfloat16 [4096, 1024], P('fsdp'), may hold values from -0.09375 to 0.09375
- downbias: bfloat16 [1024], P('fsdp'), may hold values from -4 to 4
Outputs:
- layer_out: bfloat16 [4, 2048, 1024], P('fsdp', 'ctx')
- tokens_grad: float32 [4, 2048, 1024], P('fsdp', 'ctx')
- encoded_grad: float32 [4, 2048, 1024], P('fsdp', 'ctx')
- gain_grad: float32 [3, 1024], P(None, 'fsdp')
- shift_grad: float32 [3, 1024], P(None, 'fsdp')
- inward_grad: float32 [2, 1024, 3072], P(None, 'fsdp')
- inbias_grad: float32 [2, 2, 1024], P(None, None, 'fsdp')
- outward_grad: float32 [2, 1024, 1024], P(None, 'fsdp')
- outbias_grad: float32 [2, 1024], P(None, 'fsdp')
- upward_grad: float32 [1024, 4096], P('fsdp')
- upbias_grad: float32 [4096], P('fsdp')
- downward_grad: float32 [4096, 1024], P('fsdp')
- downbias_grad: float32 [1024], P('fsdp')
The draws below stay inside these ranges and needn't reach their ends.
Inputs may be any that keep to these rules, and one draw needn't show every extreme that they name: `target_segments`: within each sequence the numbers never fall; each of the 16 documents has 1 to 512 target positions, one exactly that many. `source_segments`: within each sequence the numbers never fall; each of the 16 documents has 1 to 512 source tokens, one exactly that many. Each row is a permutation; stored block b of a sequence holds target positions block_order[b] * 128 to block_order[b] * 128 + 127.
All inputs are finite; a program needn't handle non-finite values.
Results may differ from the reference program's by a relative error of at most 0.03.
Values may be sent and summed in bfloat16 or wider, within the bound.
No kernel may reach another device: no remote copies, remote signals or barrier semaphores. Data moves between devices by JAX's collectives and lax.ppermute only.
A program may use at most 320 MiB of HBM per device.

```python
import math
import jax
import jax.numpy as jnp
import numpy as np
from jax import lax

D = 1024
HEADS = 16
HEAD_DIM = 64
FF = 4096
BLOCK = 128
TOK_DEV = 256
SEGS = 16
NSEQ = 4
LEN = 2048
SLEN = 2048
NBLK = 16


def shard_levels(stream_key, dims, shards, low, top_value):
    def one(dim, parts):
        draws = jax.random.uniform(jax.random.fold_in(jax.random.fold_in(stream_key, 6), dim), (parts,), jnp.float32, low / len(shards), top_value / len(shards))
        return jnp.repeat(jnp.exp(draws), dims[dim] // parts).reshape((-1,) + (1,) * (len(dims) - dim - 1))

    factor_of = one(*shards[0])
    for cut in shards[1:]:
        factor_of = factor_of * one(*cut)
    return factor_of


def split_up(amount, total, bound, lean):
    loads = [(1 << 20) // math.isqrt(rank ** lean) + 1 for rank in range(2, amount + 1)]
    spare, holding = total - bound - (amount - 1), [1] * (amount - 1)
    while spare > 0:
        free = [i for i in range(amount - 1) if holding[i] < bound]
        whole, left = sum([loads[i] for i in free]), spare
        for i in free:
            more = min(bound - holding[i], max(1, left * loads[i] // whole), spare)
            holding[i] = holding[i] + more
            spare = spare - more
    return np.array([bound] + holding)


def ragged_sizes(stream_key, amount, total, bound, lean):
    if amount == 2:
        one = jax.random.randint(stream_key, (), max(1, total - bound), min(bound, total - 1) + 1)
        return jnp.stack([one, total - one])
    lengths = jnp.asarray(split_up(amount, total, bound, lean), jnp.int32)
    pairs = (amount - 1) // 2
    source_of, sink = lengths[1:1 + 2 * pairs:2], lengths[2:2 + 2 * pairs:2]
    slack = jnp.minimum(source_of - 1, bound - sink)
    moved = jax.random.randint(jax.random.fold_in(stream_key, 1), (pairs,), 0, 1 << 20) % (slack + 1)
    lengths = lengths.at[1:1 + 2 * pairs:2].set(source_of - moved).at[2:2 + 2 * pairs:2].set(sink + moved)
    return lengths[jax.random.permutation(jax.random.fold_in(stream_key, 2), amount)]


def bell_draw(key, dims, spread, reach, split=(), held_as=jnp.bfloat16):
    loudness = shard_levels(key, dims, split, -0.22, 0.18) if split else 1.0
    values = jax.random.normal(key, dims, jnp.float32) * spread * loudness
    return jnp.minimum(jnp.maximum(values, -reach), reach).astype(held_as)


def setup_inputs(seed: int = 0) -> dict:
    key_of = jax.random.split(jax.random.key(seed), 17)
    return {
        "tokens": bell_draw(key_of[0], (NSEQ, LEN, D), 1.0, 6.0, ((0, 4), (1, 8))),
        "encoded": bell_draw(key_of[1], (NSEQ, SLEN, D), 1.0, 6.0, ((0, 4), (1, 8))),
        "cotangent": bell_draw(key_of[2], (NSEQ, LEN, D), 1.0, 6.0, ((0, 4), (1, 8))),
        "target_segments": jax.vmap(lambda own: jnp.searchsorted(jnp.cumsum(ragged_sizes(own, SEGS, LEN, LEN // 4, 2)), jnp.arange(LEN), side="right"))(jax.random.split(key_of[3], NSEQ)).reshape((NSEQ, LEN)).astype(jnp.int32),
        "source_segments": jax.vmap(lambda own: jnp.searchsorted(jnp.cumsum(ragged_sizes(own, SEGS, SLEN, SLEN // 4, 2)), jnp.arange(SLEN), side="right"))(jax.random.split(key_of[4], NSEQ)).reshape((NSEQ, SLEN)).astype(jnp.int32),
        "block_order": jax.vmap(lambda own: jax.random.permutation(own, NBLK))(jax.random.split(key_of[5], NSEQ)).reshape((NSEQ, NBLK)).astype(jnp.int32),
        "norm_gain": jnp.clip(1.0 + 0.18 * jax.random.normal(key_of[6], (3, D), jnp.float32), 0.099609375, 1.8984375).astype(jnp.bfloat16),
        "norm_shift": bell_draw(key_of[7], (3, D), 0.3, 4.0, ((1, 4),)),
        "inward": bell_draw(key_of[8], (2, D, 3 * D), D ** -0.5, 0.1875, ((1, 4),)),
        "inbias": bell_draw(key_of[9], (2, 2, D), 0.5, 6.0, ((2, 4),)),
        "outward": bell_draw(key_of[10], (2, D, D), (D // 16) ** -0.5, 0.75, ((1, 4),)),
        "outbias": bell_draw(key_of[11], (2, D), 0.3, 4.0, ((1, 4),)),
        "upward": bell_draw(key_of[12], (D, FF), D ** -0.5, 0.1875, ((0, 4),)),
        "upbias": bell_draw(key_of[13], (FF,), 0.3, 4.0, ((0, 4),)),
        "downward": bell_draw(key_of[14], (FF, D), FF ** -0.5, 0.09375, ((0, 4),)),
        "downbias": bell_draw(key_of[15], (D,), 0.3, 4.0, ((0, 4),)),
    }


epsilon = 1e-05

@jax.custom_vjp
def low(v):
    return lax.optimization_barrier(v.astype(jnp.bfloat16)).astype(jnp.float32)

@jax.custom_vjp
def low_back(v):
    return v

def low_keep(v):
    return (low(v), None)

def low_pass(kept, grad):
    return (grad,)

def back_keep(v):
    return (v, None)

def back_low(kept, grad):
    return (low(grad),)
low.defvjp(low_keep, low_pass)
low_back.defvjp(back_keep, back_low)

def product(left_side, right_side):
    return jnp.dot(left_side, right_side, precision=lax.Precision.HIGHEST)

def layer_norm(values, gain_row, shift_row):
    centre = lax.optimization_barrier(jnp.mean(values, axis=-1, keepdims=True))
    centred = values - centre
    variance = lax.optimization_barrier(jnp.mean(centred * centred, axis=-1, keepdims=True))
    return centred * lax.rsqrt(variance + epsilon) * gain_row + shift_row

def attention(query, key_rows, value_rows, query_seg, query_pos, key_seg, key_pos, causal):
    row_count = query.shape[0]
    key_heads = key_rows.reshape(-1, HEADS, HEAD_DIM)
    value_heads = value_rows.reshape(-1, HEADS, HEAD_DIM)

    def one_block(inputs):
        block_query, block_seg, block_pos = inputs
        scores = jnp.einsum('qhd,khd->hqk', block_query.reshape(-1, HEADS, HEAD_DIM), key_heads, precision=lax.Precision.HIGHEST) * HEAD_DIM ** (-0.5)
        scores = low_back(scores)
        allowed = block_seg[:, None] == key_seg[None, :]
        if causal:
            allowed = allowed & (key_pos[None, :] <= block_pos[:, None])
        weights = jnp.where(allowed[None], jnp.exp(scores), 0.0)
        row_total = lax.optimization_barrier(jnp.sum(weights, axis=2))
        summed = jnp.einsum('hqk,khd->qhd', low(weights), value_heads, precision=lax.Precision.HIGHEST)
        summed = low_back(summed)
        return (summed / row_total.T[:, :, None]).reshape(block_query.shape[0], -1)
    blocks = row_count // TOK_DEV
    mixed_rows = lax.map(jax.checkpoint(one_block), (query.reshape(blocks, TOK_DEV, -1), query_seg.reshape(blocks, TOK_DEV), query_pos.reshape(blocks, TOK_DEV)))
    return mixed_rows.reshape(row_count, -1)

def layer(params, tokens, encoded, target_seg, target_pos, source_seg):
    norm_gain, norm_shift, inward, inbias, outward, outbias, upward, upbias, downward, downbias = params
    normed_one = low(layer_norm(tokens, norm_gain[0], norm_shift[0]))
    query_one = low(low_back(product(normed_one, inward[0][:, :D]) + inbias[0, 0]))
    keys_one = low(low_back(product(normed_one, inward[0][:, D:2 * D])))
    values_one = low(low_back(product(normed_one, inward[0][:, 2 * D:]) + inbias[0, 1]))
    mixed_one = low(attention(query_one, keys_one, values_one, target_seg, target_pos, target_seg, target_pos, True))
    after_self = tokens + low_back(product(mixed_one, outward[0]) + outbias[0])
    normed_two = low(layer_norm(after_self, norm_gain[1], norm_shift[1]))
    query_two = low(low_back(product(normed_two, inward[1][:, :D]) + inbias[1, 0]))
    keys_two = low(low_back(product(encoded, inward[1][:, D:2 * D])))
    values_two = low(low_back(product(encoded, inward[1][:, 2 * D:]) + inbias[1, 1]))
    mixed_two = low(attention(query_two, keys_two, values_two, target_seg, target_pos, source_seg, None, False))
    after_cross = after_self + low_back(product(mixed_two, outward[1]) + outbias[1])
    normed_three = low(layer_norm(after_cross, norm_gain[2], norm_shift[2]))
    hidden = low(jax.nn.gelu(low_back(product(normed_three, upward) + upbias), approximate=True))
    return after_cross + low_back(product(hidden, downward) + downbias)

def reference(tokens, encoded, cotangent, target_segments, source_segments, block_order, norm_gain, norm_shift, inward, inbias, outward, outbias, upward, upbias, downward, downbias):
    params = (norm_gain.astype(jnp.float32), norm_shift.astype(jnp.float32), inward.astype(jnp.float32), inbias.astype(jnp.float32), outward.astype(jnp.float32), outbias.astype(jnp.float32), upward.astype(jnp.float32), upbias.astype(jnp.float32), downward.astype(jnp.float32), downbias.astype(jnp.float32))
    within_block = jnp.arange(BLOCK, dtype=jnp.int32)
    positions = (block_order[:, :, None] * BLOCK + within_block[None, None, :]).reshape(block_order.shape[0], -1)
    positions = positions.astype(jnp.int32)
    row_segments = jnp.take_along_axis(target_segments, positions, axis=1)

    def one_sequence(accumulated, inputs):
        sequence_tokens, sequence_encoded, sequence_cotangent, sequence_segments, sequence_positions, sequence_source = inputs

        def forward(weights, token_values, encoded_values):
            return layer(weights, token_values, encoded_values, sequence_segments, sequence_positions, sequence_source)
        result, pullback = jax.vjp(forward, params, sequence_tokens.astype(jnp.float32), sequence_encoded.astype(jnp.float32))
        weight_grads, token_grads, encoded_grads = pullback(sequence_cotangent.astype(jnp.float32))
        accumulated = jax.tree.map(jnp.add, accumulated, weight_grads)
        return (accumulated, (result.astype(jnp.bfloat16), token_grads, encoded_grads))
    initial = jax.tree.map(jnp.zeros_like, params)
    totals, (layer_out, tokens_grad, encoded_grad) = lax.scan(one_sequence, initial, (tokens, encoded, cotangent, row_segments, positions, source_segments))
    return (layer_out, tokens_grad, encoded_grad, totals[0], totals[1], totals[2], totals[3], totals[4], totals[5], totals[6], totals[7], totals[8], totals[9])
```

```python
import jax
import jax.numpy as jnp
from jax import lax
from jax.experimental import pallas as pl
from jax.experimental.pallas import tpu as pltpu
from jax.sharding import PartitionSpec as P

HEADS = 16
HEAD_DIM = 64
BLOCK = 128
DOCS = 16
QB = 256
KB = 256

epsilon = 1e-05
f32 = jnp.float32
bf16 = jnp.bfloat16
i32 = jnp.int32
VMEM_BYTES = 56 << 20
TIMES = {
    "cut_weights": 8, "assemble_a": 8, "project_self": 36, "attend_self": 40, "project_cross": 5, "attend_cross": 11,
    "mix_self": 5, "mix_cross": 4, "feed": 16, "feed_weights": 44, "feed_out": 5, "unmix_cross": 5, "unmix_self": 6,
    "attend_cross_back": 15, "attend_self_back": 14, "source_back": 5, "source_weights": 5, "self_back": 8,
    "unmix_tokens": 4, "feed_outputs": 6, "spread_rest": 6,
}


def cost(name):
    return pl.CostEstimate(
        flops=int(1.1e9 * TIMES.get(name, 4)), transcendentals=0, bytes_accessed=int(3.5e6 * TIMES.get(name, 4)))


def product(left, right):
    return jnp.dot(left, right, preferred_element_type=f32)


def contract_rows(left, right):
    return lax.dot_general(left, right, (((0,), (0,)), ((), ())), preferred_element_type=f32)


def times_transpose(left, right):
    return lax.dot_general(left, right, (((1,), (1,)), ((), ())), preferred_element_type=f32)


def normalise(values):
    centre = jnp.mean(values, axis=-1, keepdims=True)
    centred = values - centre
    inverse = lax.rsqrt(jnp.mean(centred * centred, axis=-1, keepdims=True) + epsilon)
    return centred * inverse, inverse


def norm_backward(upstream, scaled, inverse, gain_row):
    weighted = upstream * gain_row
    first_mean = jnp.mean(weighted, axis=-1, keepdims=True)
    second_mean = jnp.mean(weighted * scaled, axis=-1, keepdims=True)
    return inverse * (weighted - first_mean - scaled * second_mean)


def vmem():
    return pl.BlockSpec(memory_space=pltpu.VMEM)


def smem():
    return pl.BlockSpec(memory_space=pltpu.SMEM)


def project(pieces, weight, first, vectors, biases, me, norm, table, widths, padded, name):
    counts = [p.shape[0] for p in pieces]
    rows = sum(counts)
    depth = weight.shape[0]
    extra = [BLOCK if pad else 0 for pad in padded]
    n_in = len(pieces)
    total = sum(widths)
    aligned = widths[0] % 128 == 0
    if not aligned:
        own = [
            jnp.zeros((w,), f32) if b is None else lax.dynamic_slice_in_dim(vectors[b], me * w, w)
            for b, w in zip(biases, widths)
        ]
        own = jnp.concatenate(own)[None]

    def kernel(*refs):
        table_ref, me_ref = refs[:2]
        x_refs = refs[2 : 2 + n_in]
        w_ref, v_ref = refs[2 + n_in], refs[3 + n_in]
        at = 4 + n_in
        if not aligned:
            own_ref = refs[at]
            at += 1
        outs = refs[at : at + len(widths)]
        if norm:
            normed_ref = refs[at + len(widths)]
        bias = []
        left = 0
        for b, w in zip(biases, widths):
            if not aligned:
                bias.append(own_ref[0:1, left : left + w])
            elif b is not None:
                bias.append(v_ref[b : b + 1, pl.ds(pl.multiple_of(me_ref[0] * w, 128), w)])
            else:
                bias.append(None)
            left += w
        base = 0
        for x_ref, count in zip(x_refs, counts):
            step = min(count, 256)
            for sub in range(0, count, step):
                x = x_ref[sub : sub + step, :depth]
                if norm:
                    scaled, _ = normalise(x.astype(f32))
                    x = (scaled * v_ref[norm[0] : norm[0] + 1, :] + v_ref[norm[1] : norm[1] + 1, :]).astype(bf16)
                    normed_ref[base + sub : base + sub + step, :] = x
                y = product(x, w_ref[:, first : first + total])
                left = 0
                for out, width, row in zip(outs, widths, bias):
                    cut = y[:, left : left + width]
                    cut = (cut if row is None else cut + row).astype(bf16)
                    for part in range(0, step, BLOCK):
                        place = pl.multiple_of(table_ref[(base + sub + part) // BLOCK] * BLOCK, BLOCK)
                        out[pl.ds(place, BLOCK), :] = cut[part : part + BLOCK, :]
                    left += width
            base += count
        for out, width, more in zip(outs, widths, extra):
            if more:
                out[rows : rows + more, :] = jnp.zeros((more, width), bf16)

    out_shape = [jax.ShapeDtypeStruct((rows + more, width), bf16) for width, more in zip(widths, extra)]
    if norm:
        out_shape.append(jax.ShapeDtypeStruct((rows, depth), bf16))
    args = [table, me.reshape(1), *pieces, weight, vectors] + ([] if aligned else [own])
    return call(kernel, args, out_shape, [], name)


def split_rows(rows, heads):
    if heads == 1:
        return rows
    lane = lax.broadcasted_iota(i32, rows.shape, 1)
    zero = jnp.zeros_like(rows)
    parts = [
        jnp.where((lane >= h * HEAD_DIM) & (lane < (h + 1) * HEAD_DIM), rows, zero)
        for h in range(heads)
    ]
    return jnp.concatenate(parts, axis=0)


def own_rows(stacked, heads):
    if heads == 1:
        return stacked
    width = stacked.shape[1] // heads
    return jnp.concatenate(
        [
            stacked[h * HEAD_DIM : (h + 1) * HEAD_DIM, h * width : (h + 1) * width]
            for h in range(heads)
        ],
        axis=0,
    )


def load_blocks(ref, table_ref, block):
    parts = []
    for k in range(QB // BLOCK):
        place = pl.multiple_of(table_ref[block * (QB // BLOCK) + k] * BLOCK, BLOCK)
        parts.append(ref[pl.ds(place, BLOCK), :])
    return jnp.concatenate(parts, axis=0)


def store_blocks(ref, table_ref, block, values, left):
    width = values.shape[1]
    for k in range(QB // BLOCK):
        place = pl.multiple_of(table_ref[block * (QB // BLOCK) + k] * BLOCK, BLOCK)
        ref[pl.ds(place, BLOCK), left : left + width] = values[k * BLOCK : (k + 1) * BLOCK, :]


def key_weights(keys, query_rows, low, high, start, heads):
    scores = times_transpose(keys, query_rows)
    place = start + lax.broadcasted_iota(i32, (KB, QB), 0)
    allowed = (place >= low) & (place < high)
    parts = [
        jnp.where(allowed, jnp.exp(scores[:, h * QB : (h + 1) * QB]), 0.0) for h in range(heads)
    ]
    return jnp.concatenate(parts, axis=1) if heads > 1 else parts[0]


def attend(tables, query, keys, values, low, high, name):
    first, last, query_table, out_table = tables
    rows, width = query.shape
    heads = width // HEAD_DIM
    key_rows = keys.shape[0]
    tall = width + 16

    def kernel(
        first_ref, last_ref, qt_ref, ot_ref, q_ref, k_ref, v_ref, lo_ref, hi_ref,
        mixed_ref, wide_ref, inv_ref, vt_ref, acc_ref,
    ):
        for c in range(0, key_rows, BLOCK):
            vt_ref[0:width, c : c + BLOCK] = v_ref[c : c + BLOCK, :].T
        vt_ref[width:tall, :] = jnp.ones((16, key_rows), bf16)

        def one(i, carry):
            q = split_rows(load_blocks(q_ref, qt_ref, i) * jnp.asarray(HEAD_DIM ** (-0.5), bf16), heads)
            lo = lo_ref[pl.ds(i, 1), :]
            hi = hi_ref[pl.ds(i, 1), :]
            acc_ref[...] = jnp.zeros_like(acc_ref)
            begin = first_ref[i]

            def step(j, c):
                start = pl.multiple_of((begin + j * (KB // BLOCK)) * BLOCK, BLOCK)
                w = key_weights(k_ref[pl.ds(start, KB), :], q, lo, hi, start, heads)
                acc_ref[...] += product(vt_ref[:, pl.ds(start, KB)], w.astype(bf16))
                return c

            lax.fori_loop(0, (last_ref[i] - begin + KB // BLOCK - 1) // (KB // BLOCK), step, 0)
            acc = acc_ref[...]
            inverse = 1.0 / acc[width : width + 1, :]
            mixed = own_rows(acc[0:width, :] * inverse, heads).T
            inv = own_rows(jnp.broadcast_to(inverse, (width, heads * QB)), heads).T
            wide_ref[pl.ds(pl.multiple_of(i * QB, QB), QB), :] = mixed
            inv_ref[pl.ds(pl.multiple_of(i * QB, QB), QB), :] = inv
            store_blocks(mixed_ref, ot_ref, i, mixed.astype(bf16), 0)
            return carry

        lax.fori_loop(0, rows // QB, one, 0)

    return pl.pallas_call(
        kernel,
        out_shape=[
            jax.ShapeDtypeStruct((rows, width), bf16),
            jax.ShapeDtypeStruct((rows, width), f32),
            jax.ShapeDtypeStruct((rows, width), f32),
        ],
        in_specs=[smem()] * 4 + [vmem()] * 5,
        out_specs=[vmem()] * 3,
        scratch_shapes=[pltpu.VMEM((tall, key_rows), bf16), pltpu.VMEM((tall, heads * QB), f32)],
        compiler_params=pltpu.CompilerParams(vmem_limit_bytes=VMEM_BYTES),
        cost_estimate=cost(name),
        name=name,
    )(first, last, query_table, out_table, query, keys, values, low, high)


def attend_back(tables, query, keys, values, low, high, upstream, wide, inverse, joined, name):
    first, last, query_table, up_table, dq_table, dk_table = tables
    rows, width = query.shape
    heads = width // HEAD_DIM
    key_rows = keys.shape[0]
    held = key_rows - BLOCK
    scale = HEAD_DIM ** (-0.5)

    def kernel(
        first_ref, last_ref, qt_ref, ut_ref, dqt_ref, dkt_ref,
        q_ref, k_ref, v_ref, lo_ref, hi_ref, up_ref, wide_ref, inv_ref, *rest,
    ):
        if joined:
            dq_ref, kt_ref, dk_acc, dv_acc, dq_acc = rest
            dkv_ref = dq_ref
            left = width
        else:
            dq_ref, dkv_ref, kt_ref, dk_acc, dv_acc, dq_acc = rest
            left = 0
        for c in range(0, key_rows, BLOCK):
            kt_ref[:, c : c + BLOCK] = k_ref[c : c + BLOCK, :].T
        dk_acc[...] = jnp.zeros_like(dk_acc)
        dv_acc[...] = jnp.zeros_like(dv_acc)

        def one(i, carry):
            here = pl.ds(pl.multiple_of(i * QB, QB), QB)
            q = split_rows(load_blocks(q_ref, qt_ref, i) * jnp.asarray(scale, bf16), heads)
            shared = load_blocks(up_ref, ut_ref, i)[:, :width].astype(f32) * inv_ref[here, :]
            total = -(shared * wide_ref[here, :]).T
            total = [
                jnp.sum(total[h * HEAD_DIM : (h + 1) * HEAD_DIM, :], axis=0, keepdims=True)
                for h in range(heads)
            ]
            total = jnp.concatenate(total, axis=1) if heads > 1 else total[0]
            shared = split_rows(shared.astype(bf16), heads)
            lo = lo_ref[pl.ds(i, 1), :]
            hi = hi_ref[pl.ds(i, 1), :]
            dq_acc[...] = jnp.zeros_like(dq_acc)
            begin = first_ref[i]

            def step(j, c):
                start = pl.multiple_of((begin + j * (KB // BLOCK)) * BLOCK, BLOCK)
                some = pl.ds(start, KB)
                w = key_weights(k_ref[some, :], q, lo, hi, start, heads)
                grad = times_transpose(v_ref[some, :], shared)
                ds = (w * (grad + total)).astype(bf16)
                dv_acc[some, :] += product(w.astype(bf16), shared)
                dk_acc[some, :] += product(ds, q)
                dq_acc[...] += product(kt_ref[:, some], ds)
                return c

            lax.fori_loop(0, (last_ref[i] - begin + KB // BLOCK - 1) // (KB // BLOCK), step, 0)
            dq = own_rows(dq_acc[...] * scale, heads).T.astype(bf16)
            store_blocks(dq_ref, dqt_ref, i, dq, 0)
            return carry

        lax.fori_loop(0, rows // QB, one, 0)

        def flush(b, carry):
            here = pl.ds(pl.multiple_of(b * BLOCK, BLOCK), BLOCK)
            there = pl.ds(pl.multiple_of(dkt_ref[b] * BLOCK, BLOCK), BLOCK)
            dkv_ref[there, left : left + width] = dk_acc[here, :].astype(bf16)
            dkv_ref[there, left + width : left + 2 * width] = dv_acc[here, :].astype(bf16)
            return carry

        lax.fori_loop(0, held // BLOCK, flush, 0)

    if joined:
        out_shape = [jax.ShapeDtypeStruct((rows, 3 * width), bf16)]
    else:
        out_shape = [
            jax.ShapeDtypeStruct((rows, width), bf16),
            jax.ShapeDtypeStruct((held, 2 * width), bf16),
        ]
    return pl.pallas_call(
        kernel,
        out_shape=out_shape,
        in_specs=[smem()] * 6 + [vmem()] * 8,
        out_specs=[vmem()] * len(out_shape),
        scratch_shapes=[
            pltpu.VMEM((width, key_rows), bf16),
            pltpu.VMEM((key_rows, width), f32),
            pltpu.VMEM((key_rows, width), f32),
            pltpu.VMEM((width, heads * QB), f32),
        ],
        compiler_params=pltpu.CompilerParams(vmem_limit_bytes=VMEM_BYTES),
        cost_estimate=cost(name),
        name=name,
    )(first, last, query_table, up_table, dq_table, dk_table,
      query, keys, values, low, high, upstream, wide, inverse)


def cut_weights(inward, outward, upward, downward, small, me, width, units, parts, name):
    depth, D = outward.shape[1:]
    stride = upward.shape[1] // parts

    F = parts * units
    tall, wide = small.shape

    def kernel(me_ref, small_ref, in_ref, out_ref, up_ref, down_ref, a_ref, b_ref, sems):
        at = pl.multiple_of(me_ref[0] * width, 128)
        unit = pl.multiple_of(me_ref[0] * units, 128)
        plan = []
        for k in range(3):
            plan.append((in_ref.at[0, :, pl.ds(k * D + at, width)], a_ref.at[0:depth, pl.ds(k * width, width)]))
        plan.append((out_ref.at[0, :, pl.ds(at, width)], a_ref.at[0:depth, pl.ds(3 * width, width)]))
        plan.append((in_ref.at[1, :, pl.ds(at, width)], a_ref.at[0:depth, pl.ds(4 * width, width)]))
        for k in range(2):
            plan.append((in_ref.at[1, :, pl.ds((k + 1) * D + at, width)], b_ref.at[:, pl.ds(k * width, width)]))
        plan.append((out_ref.at[1, :, pl.ds(at, width)], b_ref.at[:, pl.ds(2 * width, width)]))
        for k in range(parts):
            plan.append((up_ref.at[:, pl.ds(k * stride + unit, units)],
                         b_ref.at[:, pl.ds(3 * width + k * units, units)]))
        for q in range(D // F):
            plan.append((down_ref.at[pl.ds(unit, units), q * F : (q + 1) * F],
                         b_ref.at[q * units : (q + 1) * units, pl.ds(3 * width + F, F)]))
        copies = [pltpu.make_async_copy(src, dst, sems.at[k]) for k, (src, dst) in enumerate(plan)]
        for c in copies:
            c.start()
        a_ref[depth : depth + tall, 0:wide] = small_ref[...]
        a_ref[depth : depth + tall, wide : 5 * width] = jnp.zeros((tall, 5 * width - wide), bf16)
        for c in copies:
            c.wait()

    return pl.pallas_call(
        kernel,
        out_shape=[
            jax.ShapeDtypeStruct((depth + tall, 5 * width), bf16),
            jax.ShapeDtypeStruct((depth, 3 * width + 2 * F), bf16),
        ],
        in_specs=[smem(), vmem()] + [pl.BlockSpec(memory_space=pl.ANY)] * 4,
        out_specs=[vmem()] * 2,
        scratch_shapes=[pltpu.SemaphoreType.DMA((8 + parts + D // F,))],
        compiler_params=pltpu.CompilerParams(vmem_limit_bytes=VMEM_BYTES),
        cost_estimate=cost(name),
        name=name,
    )(me.reshape(1), small, inward, outward, upward, downward)


def assemble(pieces, places, widths, tall, name):
    depth = pieces[0].shape[0] - tall
    count = len(pieces)

    def kernel(*refs):
        place_ref, parts, outs = refs[0], refs[1 : 1 + count], refs[1 + count :]
        for d, part in enumerate(parts):
            at = pl.multiple_of(place_ref[d] * depth, depth)
            left = 0
            for out, width in zip(outs, widths):
                out[pl.ds(at, depth), :] = part[0:depth, left : left + width]
                left += width
            for k in range(2):
                outs[-1][k * tall : (k + 1) * tall, pl.ds(at, depth)] = part[
                    depth : depth + tall, k * depth : (k + 1) * depth].astype(f32)

    shapes = [jax.ShapeDtypeStruct((count * depth, w), bf16) for w in widths]
    shapes.append(jax.ShapeDtypeStruct((2 * tall, count * depth), f32))
    return call(kernel, [places, *pieces], shapes, [], name)


def spread_columns(pieces, near, plan, shapes, dtype, name):
    stacked = [len(group) == 1 for group in pieces]
    counts = [len(group) for group in pieces]
    flat = [p for group in pieces for p in group]

    def kernel(*refs):
        near_ref, parts, outs = refs[0], refs[1 : 1 + len(flat)], refs[1 + len(flat) :]
        for group, first, width, out, lead, base in plan:
            skip = sum(counts[:group])
            for r in range(near.shape[0]):
                there = pl.ds(pl.multiple_of(base + near_ref[r] * width, 128), width)
                part = parts[skip].at[r] if stacked[group] else parts[skip + r]
                value = part[: shapes[out][-2], first : first + width].astype(dtype)
                if lead is None:
                    outs[out][:, there] = value
                else:
                    outs[out][lead, :, there] = value

    return pl.pallas_call(
        kernel,
        out_shape=[jax.ShapeDtypeStruct(shape, dtype) for shape in shapes],
        in_specs=[smem()] + [vmem()] * len(flat),
        out_specs=[vmem()] * len(shapes),
        compiler_params=pltpu.CompilerParams(vmem_limit_bytes=VMEM_BYTES),
        cost_estimate=cost(name),
        name=name,
    )(near, *flat)


def call(kernel, args, out_shape, scratch, name):
    small = [a.ndim == 1 and a.dtype == i32 for a in args]
    return pl.pallas_call(
        kernel,
        out_shape=out_shape,
        in_specs=[smem() if is_small else vmem() for is_small in small],
        out_specs=[vmem()] * len(out_shape),
        scratch_shapes=scratch,
        compiler_params=pltpu.CompilerParams(vmem_limit_bytes=VMEM_BYTES),
        cost_estimate=cost(name),
        name=name,
    )(*args)


def columns_at(order_ref, fixed, r, width):
    if fixed:
        return pl.ds(r * width, width)
    return pl.ds(pl.multiple_of(order_ref[r] * width, 128), width)


def block_at(order_ref, fixed, r):
    return r if fixed else order_ref[r]


def mix(received, pieces, order, fixed, residual, rows, first, width, query, name):
    C, T = received.shape[:2]
    D = residual.shape[1]
    stacked = len(pieces) == 1

    def kernel(*refs):
        order_ref, rec_ref = refs[:2]
        parts = refs[2 : 2 + len(pieces)]
        res_ref, rows_ref, after_ref, kept_ref, last_ref, y_ref = refs[2 + len(pieces) :]

        def weights(r, left):
            part = parts[0].at[r] if stacked else parts[r]
            return part[:, left : left + width]

        def pairs(x, left):
            for r in range(0, C, 2):
                both = product(x, jnp.concatenate([weights(r, left), weights(r + 1, left)], axis=1))
                yield r, both[:, :width]
                yield r + 1, both[:, width:]

        mixed = jnp.concatenate([rec_ref[c] for c in range(C)], axis=1)
        kept_ref[:, 0:D] = mixed
        for r, value in pairs(mixed, first):
            y_ref[:, columns_at(order_ref, fixed, r, width)] = value
        values = res_ref[...].astype(f32) + (y_ref[...] + rows_ref[0:1, :])
        after_ref[...] = values
        scaled, _ = normalise(values)
        normed = (scaled * rows_ref[1:2, :] + rows_ref[2:3, :]).astype(bf16)
        if not query:
            last_ref[...] = normed
        else:
            kept_ref[:, D : 2 * D] = normed
            for r, value in pairs(normed, first + width):
                bias = rows_ref[3:4, columns_at(order_ref, fixed, r, width)]
                last_ref[block_at(order_ref, fixed, r)] = (value + bias).astype(bf16)

    shapes = [
        jax.ShapeDtypeStruct((T, D), f32),
        jax.ShapeDtypeStruct((T, 2 * D if query else D), bf16),
        jax.ShapeDtypeStruct((C, T, width) if query else (T, D), bf16),
    ]
    return call(kernel, [order, received, *pieces, residual, rows], shapes,
                [pltpu.VMEM((T, D), f32)], name)


def unmix(grads, query_grads, query_pieces, pieces, order, fixed, firsts, upstream, values, gain, width, name):
    T, D = upstream.shape
    C = D // width
    joined = query_pieces is pieces and pieces is not None
    lists = [list(grads)]
    lists.append([query_grads] if query_grads is not None else [])
    lists.append(list(query_pieces) if query_pieces is not None and not joined else [])
    lists.append(list(pieces) if pieces is not None else [])
    flat = [a for part in lists for a in part]
    low_out = pieces is not None

    def kernel(*refs):
        order_ref = refs[0]
        at = 1
        got = []
        for part in lists:
            got.append(refs[at : at + len(part)])
            at += len(part)
        up_ref, val_ref, gain_ref = refs[at : at + 3]
        at += 3
        if low_out:
            grad_ref, m_ref, sums_ref = refs[at : at + 3]
        else:
            grad_ref, sums_ref = refs[at : at + 2]
        ws = got[3]
        qs = ws if joined else got[2]

        def weights(parts, r, left):
            part = parts[0].at[r] if len(parts) == 1 else parts[r]
            return part[:, left : left + width]

        def back(columns, parts, left):
            total = None
            for r in range(0, C, 2):
                cols = jnp.concatenate([columns(r), columns(r + 1)], axis=1)
                both = jnp.concatenate([weights(parts, r, left), weights(parts, r + 1, left)], axis=1)
                part = times_transpose(cols, both)
                total = part if total is None else total + part
            return total

        sums_ref[...] = jnp.zeros_like(sums_ref)
        if query_grads is not None:
            dq_ref = got[1][0]
            grad = back(lambda r: dq_ref[block_at(order_ref, fixed, r)], qs, firsts[0])
            for c in range(C):
                sums_ref[3:4, c * width : (c + 1) * width] = jnp.sum(
                    dq_ref[c].astype(f32), axis=0, keepdims=True)
        else:
            grad = got[0][0][...].astype(f32)
            for g in got[0][1:]:
                grad = grad + g[...].astype(f32)
        scaled, inverse = normalise(val_ref[...].astype(f32))
        sums_ref[0:1, :] = jnp.sum(grad * scaled, axis=0, keepdims=True)
        sums_ref[1:2, :] = jnp.sum(grad, axis=0, keepdims=True)
        upstream_values = up_ref[...].astype(f32)
        if query_grads is None:
            sums_ref[3:4, :] = jnp.sum(upstream_values, axis=0, keepdims=True)
        result = upstream_values + norm_backward(grad, scaled, inverse, gain_ref[...])
        grad_ref[...] = result
        if low_out:
            low = result.astype(bf16)
            for c in range(C):
                m_ref[c, :, width : 2 * width] = low[:, c * width : (c + 1) * width]
            sums_ref[2:3, :] = jnp.sum(low.astype(f32), axis=0, keepdims=True)
            m = back(lambda r: m_ref[block_at(order_ref, fixed, r), :, width : 2 * width], ws, firsts[1])
            for c in range(C):
                m_ref[c, :, 0:width] = m[:, c * width : (c + 1) * width].astype(bf16)

    shapes = [jax.ShapeDtypeStruct((T, D), f32)]
    if low_out:
        shapes.append(jax.ShapeDtypeStruct((C, T, 2 * width), bf16))
    shapes.append(jax.ShapeDtypeStruct((8, D), f32))
    return call(kernel, [order, *flat, upstream, values, gain], shapes, [], name)


def parts_shapes(cube, C, T, D):
    if cube:
        return [jax.ShapeDtypeStruct((T, D), bf16)] * 5 + [jax.ShapeDtypeStruct((3, T, D), bf16)]
    return [jax.ShapeDtypeStruct((C, T, D), bf16)]


def store_part(cube, refs, r, value):
    if not cube:
        refs[0][r] = value
    elif r < 4:
        refs[r][...] = value
    elif r == 7:
        refs[4][...] = value
    else:
        refs[5][r - 4] = value


ROOT = 0.7978845608028654


def feed(normed, cotangent, order, fixed, up, first, down, up_bias, cube, name):
    C = len(normed)
    T, D = normed[0].shape
    F = down.shape[0]

    def kernel(*refs):
        order_ref = refs[0]
        n_refs = refs[1 : 1 + C]
        cot_ref, up_ref, down_ref, bias_ref = refs[1 + C : 5 + C]
        hidden_ref, grad_ref, sum_ref = refs[5 + C : 8 + C]
        part_refs = refs[8 + C :]
        total = jnp.zeros((1, F), f32)
        for r in range(C):
            pre = product(n_refs[r][...], up_ref[:, first : first + F]) + bias_ref[...]
            square = pre * pre
            inner = jnp.tanh(ROOT * pre * (1.0 + 0.044715 * square))
            half = 0.5 * (1.0 + inner)
            rows = slice(r * T, (r + 1) * T)
            hidden_ref[rows, :] = (pre * half).astype(bf16)
            slope = half + 0.5 * pre * (1.0 - inner * inner) * (ROOT * (1.0 + 3 * 0.044715 * square))
            cot = cot_ref[block_at(order_ref, fixed, r)]
            low = (times_transpose(cot, down_ref[...]) * slope).astype(bf16)
            grad_ref[rows, :] = low
            total = total + jnp.sum(low.astype(f32), axis=0, keepdims=True)
            store_part(cube, part_refs, r, times_transpose(low, up_ref[:, first : first + F]).astype(bf16))
        sum_ref[...] = total

    shapes = [
        jax.ShapeDtypeStruct((C * T, F), bf16),
        jax.ShapeDtypeStruct((C * T, F), bf16),
        jax.ShapeDtypeStruct((1, F), f32),
    ] + parts_shapes(cube, C, T, D)
    return call(kernel, [order, *normed, cotangent, up, down, up_bias], shapes, [], name)


def feed_weights(normed, cotangent, order, fixed, hidden, up_grad, parts, name):
    C = len(normed)
    T, D = normed[0].shape
    F = hidden.shape[1]
    depth, units = D // parts, F // parts

    def kernel(*refs):
        order_ref = refs[0]
        n_refs = refs[1 : 1 + C]
        cot_ref, hid_ref, grad_ref, out_ref, up_acc, down_acc = refs[1 + C :]
        for r in range(C):
            rows = slice(r * T, (r + 1) * T)
            up = contract_rows(n_refs[r][...], grad_ref[rows, :])
            down = contract_rows(hid_ref[rows, :], cot_ref[block_at(order_ref, fixed, r)])
            if r == 0:
                up_acc[...] = up
                down_acc[...] = down
            else:
                up_acc[...] += up
                down_acc[...] += down
        for z in range(parts):
            out_ref[z, 0:depth, :] = up_acc[z * depth : (z + 1) * depth, :].astype(bf16)
            for q in range(D // F):
                out_ref[z, depth + q * units : depth + (q + 1) * units, :] = down_acc[
                    z * units : (z + 1) * units, q * F : (q + 1) * F].astype(bf16)

    return call(kernel, [order, *normed, cotangent, hidden, up_grad],
                [jax.ShapeDtypeStruct((parts, 2 * depth, F), bf16)],
                [pltpu.VMEM((D, F), f32), pltpu.VMEM((F, D), f32)], name)[0]


def feed_outputs(gathered, parts, D, name):
    C, _, F = gathered.shape
    depth, units = D // parts, F // parts
    FF, FZ = C * F, C * units

    def kernel(x_ref, up_ref, down_ref):
        for c in range(C):
            for z in range(parts):
                at = z * FZ + c * units
                up_ref[:, at : at + units] = x_ref[c, 0:depth, z * units : (z + 1) * units].astype(f32)
            for q in range(D // F):
                down_ref[c * units : (c + 1) * units, q * F : (q + 1) * F] = x_ref[
                    c, depth + q * units : depth + (q + 1) * units, :].astype(f32)

    return call(kernel, [gathered], [
        jax.ShapeDtypeStruct((depth, FF), f32), jax.ShapeDtypeStruct((FZ, D), f32)], [], name)


def times_weight(x, weight, columns, turned, order, ordered, cube, C, name):
    T = x.shape[0] // C
    D = weight.shape[0] if turned else columns

    def kernel(order_ref, x_ref, w_ref, *outs):
        for r in range(C):
            rows = x_ref[r * T : (r + 1) * T, :]
            some = w_ref[:, :columns]
            value = times_transpose(rows, some) if turned else product(rows, some)
            if ordered:
                outs[0][order_ref[r]] = value.astype(bf16)
            else:
                store_part(cube, outs, r, value.astype(bf16))

    shapes = [jax.ShapeDtypeStruct((C, T, D), bf16)] if ordered else parts_shapes(cube, C, T, D)
    return call(kernel, [order, x, weight], shapes, [], name)


def self_back(tokens, grads, weight, sums, me, cube, name):
    C = len(tokens)
    T, D = tokens[0].shape
    Z = sums.shape[0]
    DZ = D // Z
    width = weight.shape[1] // 3

    def kernel(me_ref, *refs):
        x_refs, (g_ref, w_ref, sums_ref, out_ref), outs = refs[:C], refs[C : C + 4], refs[C + 4 :]
        first = jnp.zeros((1, D), f32)
        second = jnp.zeros((1, D), f32)
        bias = jnp.zeros((1, 3 * width), f32)
        for r in range(C):
            rows = g_ref[r * T : (r + 1) * T, :]
            grad = times_transpose(rows, w_ref[...])
            store_part(cube, outs, r, grad.astype(bf16))
            scaled, _ = normalise(x_refs[r][...].astype(f32))
            first = first + jnp.sum(grad * scaled, axis=0, keepdims=True)
            second = second + jnp.sum(grad, axis=0, keepdims=True)
            bias = bias + jnp.sum(rows.astype(f32), axis=0, keepdims=True)
        lane = lax.broadcasted_iota(i32, (1, D), 1)
        spot = (lane >= me_ref[0] * width) & (lane < (me_ref[0] + 1) * width)

        def at_own(row):
            return jnp.where(spot, jnp.concatenate([row] * C, axis=1), 0.0)

        late = {0: first, 3: second, 6: at_own(bias[:, :width]), 7: at_own(bias[:, 2 * width :])}
        for z in range(Z):
            block = sums_ref[z]
            place = lax.broadcasted_iota(i32, block.shape, 0)
            for k, row in late.items():
                cut = row[:, z * DZ : (z + 1) * DZ]
                cut = jnp.concatenate([cut, jnp.zeros_like(cut)], axis=1)
                block = block + jnp.where(place == k, cut, 0.0)
            out_ref[z] = block.astype(bf16)

    shapes = [jax.ShapeDtypeStruct(sums.shape, bf16)] + parts_shapes(cube, C, T, D)
    return call(kernel, [me.reshape(1), *tokens, grads, weight, sums], shapes, [], name)


def contract_pieces(pieces, grads, name):
    C = len(pieces)
    T, D = pieces[0].shape
    N = grads.shape[1]

    def kernel(*refs):
        x_refs, (g_ref, out_ref, acc_ref) = refs[:C], refs[C:]
        for r in range(C):
            part = contract_rows(x_refs[r][...], g_ref[r * T : (r + 1) * T, :])
            if r == 0:
                acc_ref[...] = part
            else:
                acc_ref[...] += part
        out_ref[...] = acc_ref[...].astype(bf16)

    return call(kernel, [*pieces, grads], [jax.ShapeDtypeStruct((D, N), bf16)],
                [pltpu.VMEM((D, N), f32)], name)[0]


def after(x, *others):
    return lax.optimization_barrier((x, *others))[0]


def together(many, *others):
    return lax.optimization_barrier((*many, *others))[: len(many)]


def make_body(C, Z):
    cube = C == 8
    relative = [0, 2, 4, 6, 1, 3, 5, 7] if cube else list(range(C))

    def hop(x, bit):
        return lax.ppermute(x, "ctx", [(i, i ^ bit) for i in range(C)])

    def hop_diag(x):
        return lax.ppermute(x, "ctx", [(i, i ^ (4 if i & 1 else 2)) for i in range(C)])

    def gather_halves(x):
        if not cube:
            return [x, x, x], lambda hold: gather_steps(x, hold)
        odd = lax.axis_index("ctx") & 1
        own, ex, wy = hop(x, 1), hop(x, 2), hop(x, 4)

        def rest(hold):
            one, two = (ex, wy) if hold is None else together((ex, wy), hold)
            chosen = jnp.where(odd == 1, one, two)
            diag = hop_diag(chosen)
            first = [x, ex, wy, diag, own, hop(one, 1), hop(two, 1)]
            return first, chosen, lambda held: first + [hop(diag if held is None else after(diag, held), 1)]

        return [own, ex, wy], rest

    def gather_steps(x, hold):
        if not cube:
            whole = lax.all_gather(x, "ctx", axis=0, tiled=False)
            blocks = [whole[r] for r in range(C)]
            return blocks, x, lambda held: blocks
        return gather_halves(x)[1](hold)

    def gather_rows(x, hold=None):
        return gather_steps(x, hold)[2](None)

    def scatter_parts(parts):
        if not cube:
            done = lax.psum_scatter(parts[0], "ctx", scatter_dimension=0, tiled=False)
            return [done], done, done
        odd = lax.axis_index("ctx") & 1
        even, other_diag, others = parts[:4], parts[4], parts[5]
        got_diag = hop(other_diag, 1)
        got = hop(others, 1)
        second = (even[3].astype(f32) + got_diag.astype(f32)).astype(bf16)
        passed = hop_diag(second).astype(f32)
        ex = even[1].astype(f32) + got[1].astype(f32) + jnp.where(odd == 1, passed, 0.0)
        wy = even[2].astype(f32) + got[2].astype(f32) + jnp.where(odd == 1, 0.0, passed)
        third = wy.astype(bf16)
        got_x = hop(ex.astype(bf16), 2)
        got_y = hop(third, 4)
        return [even[0], got[0], got_x, got_y], second, third

    def tree_sum(blocks):
        parts = [blocks[relative.index(r)] for r in range(C)]
        while len(parts) > 1:
            parts = [parts[k] + parts[k + 1] for k in range(0, len(parts), 2)]
        return parts[0]

    def exchange(x):
        return lax.all_to_all(x, "ctx", split_axis=0, concat_axis=0, tiled=True)

    def zhop(x, d):
        return lax.ppermute(x, "fsdp", [(i, (i + d) % Z) for i in range(Z)])

    far_first = sorted(range(1, Z), key=lambda d: -min(d, Z - d))

    def zgather(x):
        got = {d: zhop(x, d) for d in far_first}
        return [x] + [got[d] for d in range(1, Z)]

    def zscatter(blocks, hold=None):
        got = lax.all_to_all(blocks, "fsdp", split_axis=0, concat_axis=0, tiled=True)
        if hold is not None:
            got = after(got, hold)
        return jnp.sum(got.astype(f32), axis=0)

    def body(
        tokens, encoded, cotangent, target_segments, source_segments, block_order,
        norm_gain, norm_shift, inward, inbias, outward, outbias, upward, upbias, downward, downbias,
    ):
        T, D = tokens.shape[1:]
        S = encoded.shape[1]
        L = C * T
        DZ = norm_gain.shape[1]
        FZ = downward.shape[0]
        FF = FZ * Z
        U = FZ // C
        width = D // C
        lanes = width % 128 == 0 and U % 128 == 0
        me = lax.axis_index("ctx")
        zi = lax.axis_index("fsdp")
        near = jnp.array(relative, i32)
        if cube:
            near = near ^ me
        zplace = (zi - jnp.arange(Z, dtype=i32)) % Z
        fixed = not cube
        steady = jnp.arange(C, dtype=i32)

        def mine(x, dims, axis):
            return lax.dynamic_index_in_dim(x.reshape(dims), me, axis, keepdims=False)

        def columns(groups, plan, shapes, dtype, name):
            if lanes:
                return spread_columns(groups, near, plan, shapes, dtype, name)
            outs = [[None] * (shape[0] if len(shape) == 3 else 1) for shape in shapes]
            for group, first, w, out, lead, base in sorted(plan, key=lambda p: p[5]):
                stacked = jnp.stack(groups[group])[:, : shapes[out][-2], first : first + w].astype(dtype)
                part = stacked.transpose(1, 0, 2).reshape(stacked.shape[1], -1)
                k = lead or 0
                outs[out][k] = part if outs[out][k] is None else jnp.concatenate([outs[out][k], part], axis=1)
            return [o[0] if len(shape) == 2 else jnp.stack(o) for o, shape in zip(outs, shapes)]

        small = jnp.concatenate(
            [norm_gain, norm_shift, inbias.reshape(4, DZ), outbias, downbias.reshape(1, DZ),
             upbias.reshape(FZ // DZ, DZ), jnp.zeros((19 - FZ // DZ, DZ), bf16)], axis=0)
        small = jnp.concatenate([small[:16], small[16:]], axis=1)
        F = Z * U
        if lanes:
            cut_a, cut_b = cut_weights(
                inward, outward, upward, downward, small, me, width, U, Z, "cut_weights")
        else:
            in_one = mine(inward[0], (DZ, 3, C, width), 2).reshape(DZ, 3 * width)
            in_two = mine(inward[1], (DZ, 3, C, width), 2).reshape(DZ, 3 * width)
            outs = mine(outward, (2, DZ, C, width), 2)
            cut_a = jnp.concatenate([in_one, outs[0], in_two[:, :width]], axis=1)
            cut_a = jnp.concatenate([cut_a, jnp.pad(small, ((0, 0), (0, 5 * width - 2 * DZ)))], axis=0)
            cut_up = mine(upward, (DZ, Z, C, U), 2).reshape(DZ, F)
            cut_down = mine(downward, (C, U, D), 0).reshape(U, D // F, F).transpose(1, 0, 2).reshape(DZ, F)
            cut_b = jnp.concatenate([in_two[:, width:], outs[1], cut_up, cut_down], axis=1)

        pieces_a = zgather(cut_a)
        token_start, token_chosen, token_join = gather_steps(after(tokens[0], cut_a), pieces_a[Z // 2])
        source_start, source_chosen, source_join = gather_steps(after(encoded[0], token_chosen), None)
        w_self, w_pair, vectors = assemble(
            list(together(pieces_a, token_chosen)), zplace, [3 * width, 2 * width], 16, "assemble_a")
        token_pieces = token_join(w_self)
        pair_start, pair_rest = gather_halves(w_pair)
        w_b = lax.all_gather(after(cut_b, w_self), "fsdp", axis=0, tiled=True)
        w_down = w_b[:, 3 * width + F :].reshape(Z, D // F, U, F).transpose(0, 2, 1, 3).reshape(F, D)
        w_out = w_b[:, 2 * width : 3 * width]
        gains, shifts = vectors[0:3], vectors[3:6]
        outb, downb = vectors[10:12], vectors[12]
        upb = vectors[13 : 13 + FZ // DZ].reshape(FZ // DZ, Z, DZ).transpose(1, 0, 2)
        upb = mine(upb.reshape(FF), (Z, C, U), 1).reshape(F)

        blocks = T // BLOCK
        index = jnp.arange(C * blocks, dtype=i32)
        order = block_order[0]
        by_device = order.reshape(1, C, blocks)
        near_order = jnp.sum(
            jnp.where(near[:, None, None] == jnp.arange(C, dtype=i32)[None, :, None], by_device, 0), axis=1
        ).reshape(-1)

        def inverted(table):
            return jnp.sum(jnp.where(table[None, :] == index[:, None], index[None, :], 0), axis=1)

        source_table = (near[:, None] * blocks + jnp.arange(blocks, dtype=i32)).reshape(-1)
        near_source = inverted(source_table)
        stored = inverted(order)
        near_stored = inverted(near_order)
        seg = target_segments[0]
        docs = jnp.arange(DOCS, dtype=i32)[:, None]
        own_doc = seg[None, :] == docs
        t_start = jnp.sum((seg[None, :] < docs).astype(i32), axis=1)
        s_start = jnp.sum((source_segments[0][None, :] < docs).astype(i32), axis=1)
        s_end = jnp.sum((source_segments[0][None, :] <= docs).astype(i32), axis=1)

        def per_row(table):
            return jnp.sum(jnp.where(own_doc, table[:, None], 0), axis=0).reshape(L // QB, QB)

        self_low = per_row(t_start)
        self_high = jnp.arange(1, L + 1, dtype=i32).reshape(L // QB, QB)
        cross_low, cross_high = per_row(s_start), per_row(s_end)
        self_first = self_low[:, 0] // BLOCK
        self_last = self_high[:, -1] // BLOCK
        cross_first = cross_low[:, 0] // BLOCK
        cross_last = (cross_high[:, -1] + BLOCK - 1) // BLOCK

        q1, k1, v1, normed_one = project(
            token_pieces, after(w_self, source_chosen, pair_start[0]), 0, vectors, [6, None, 7], me, (0, 3),
            near_order, [width] * 3, [False, True, True], "project_self")
        source_pieces = source_join(None)
        mixed1, wide1, inv1 = attend(
            (self_first, self_last, index, stored), after(q1, source_start[3]), k1, v1, self_low, self_high,
            "attend_self")
        pair = pair_rest(q1)[2](None)
        cot = lax.all_gather(after(cotangent[0], q1), "ctx", axis=0, tiled=False)
        mixed_one = exchange(mixed1.reshape(C, T, width))

        after_self, kept_self, q2_own = mix(
            mixed_one, pair, near, fixed, tokens[0],
            jnp.stack([outb[0], gains[1], shifts[1], vectors[8]]), 0, width, True, "mix_self")
        q2 = exchange(q2_own).reshape(L, width)
        k2, v2 = project(
            source_pieces, after(w_b, q2_own), 0, vectors, [None, 9], me, None, source_table,
            [width] * 2, [True, True], "project_cross")
        mixed2, wide2, inv2 = attend(
            (cross_first, cross_last, stored, stored), q2, k2, v2, cross_low, cross_high,
            "attend_cross")
        kept_self = lax.all_gather(kept_self, "ctx", axis=0, tiled=True)
        out_two = gather_rows(after(w_out, q2_own), mixed2)
        mixed_two = exchange(mixed2.reshape(C, T, width))
        after_cross, kept_cross, normed_three = mix(
            mixed_two, out_two, near, fixed, after_self,
            jnp.stack([outb[1], gains[2], shifts[2]]), 0, width, False, "mix_cross")

        kept_cross = lax.all_gather(after(kept_cross, kept_self), "ctx", axis=0, tiled=True)

        n3 = gather_rows(normed_three)
        hidden, up_grad, upb_tp, *parts = feed(
            n3, cot, near, fixed, w_b, 3 * width, w_down, upb[None], cube, "feed")
        back_three, _, _ = scatter_parts(parts)
        feed_dw = feed_weights(
            n3, cot, near, fixed, hidden, after(up_grad, parts[0]), Z, "feed_weights")
        out_parts = times_weight(
            hidden, after(w_down, feed_dw), D, False, near, False, cube, C, "feed_out")
        feed_sum = lax.psum_scatter(feed_dw, "fsdp", scatter_dimension=0, tiled=False)

        out_terms, out_second, out_third = scatter_parts(out_parts)

        cross_grad, m2_own, sums_three = unmix(
            back_three, None, None, out_two, near, fixed, (0, 0), after(cotangent[0], feed_dw, out_second), after_cross,
            gains[2:3], width, "unmix_cross")
        m2 = exchange(m2_own).reshape(L, 2 * width)
        dq2, dkv2 = attend_back(
            (cross_first, cross_last, stored, stored, stored, near_source),
            q2, k2, v2, cross_low, cross_high, after(m2, out_third), wide2, inv2, False, "attend_cross_back")
        feed_all = lax.all_gather(after(feed_sum, dq2), "ctx", axis=0, tiled=False)
        layer_out = (after_cross + (sum(t.astype(f32) for t in together(out_terms, dq2)) + downb)).astype(bf16)
        dq2_own = exchange(dq2.reshape(C, T, width))
        (source_part,) = times_weight(dkv2, w_b, 2 * width, True, near, True, cube, C, "source_back")
        encoded_grad = lax.psum_scatter(source_part, "ctx", scatter_dimension=0, tiled=False).astype(f32)
        self_grad, m1_own, sums_two = unmix(
            [], dq2_own, pair, pair, near, fixed, (width, 0), after(cross_grad, source_part), after_self,
            gains[1:2], width, "unmix_self")

        m1 = exchange(m1_own).reshape(L, 2 * width)
        group_one = jnp.concatenate([
            contract_rows(kept_self[:, D:], after(dq2, m1_own)).astype(bf16),
            contract_rows(kept_cross, after(m2, m1_own)[:, width:]).astype(bf16),
            contract_pieces(source_pieces, after(dkv2, m1_own), "source_weights"),
        ], axis=1).reshape(Z, DZ, 4 * width)
        m1 = after(m1, group_one, layer_out)
        group_one = zscatter(group_one).astype(bf16)
        (dqkv,) = attend_back(
            (self_first, self_last, index, stored, near_stored, near_stored),
            q1, k1, v1, self_low, self_high, m1, wide1, inv1, True, "attend_self_back")
        def placed(part, count):
            part = part.reshape(count, 1, -1)
            spot = lax.broadcasted_iota(i32, (count, C, part.shape[2]), 1) == me
            return jnp.where(spot, part, 0.0)

        dkv2_sum = placed(jnp.sum(dkv2[:, width:].astype(f32), axis=0), 1).reshape(D)
        upb_rows = placed(upb_tp, Z).reshape(Z, FZ // DZ, DZ)
        none = jnp.zeros((D,), f32)
        sums = jnp.stack([
            none, sums_two[0], sums_three[0], none, sums_two[1], sums_three[1],
            none, none, sums_two[3], dkv2_sum, sums_two[2], sums_three[2], sums_three[3],
        ])
        count = 13 + FZ // DZ
        sums = jnp.concatenate([
            sums.reshape(13, Z, DZ).transpose(1, 0, 2), upb_rows, jnp.zeros((Z, 32 - count, DZ), f32)], axis=1)
        sums = jnp.concatenate([sums[:, :16], sums[:, 16:]], axis=2)
        sums, *parts_one = self_back(
            token_pieces, dqkv, w_self, after(sums, m1), me, cube, "self_back")
        back_one, _, back_third = scatter_parts(parts_one)
        group_two = jnp.concatenate([
            contract_rows(kept_self[:, :D], m1[:, width:]).astype(bf16),
            contract_rows(normed_one, dqkv).astype(bf16),
        ], axis=1)
        group_two = jnp.concatenate([group_two.reshape(Z, DZ, 4 * width), sums], axis=1)
        group_two = zscatter(after(group_two, group_one), back_third).astype(bf16)
        one_start, one_chosen, one_join = gather_steps(after(group_one, parts_one[0]), back_third)
        group_one = one_join(None)
        upward_grad, down_grad = feed_outputs(after(feed_all, back_third), Z, D, "feed_outputs")
        tokens_grad, _ = unmix(
            back_one, None, None, None, near, fixed, (0, 0),
            after(self_grad, upward_grad, encoded_grad, one_chosen, group_two), tokens[0], gains[0:1], width, "unmix_tokens")
        group_two = gather_rows(after(group_two, tokens_grad))
        part = tree_sum([g[DZ:].astype(f32) for g in group_two])
        part = jnp.concatenate([part[:, :DZ], part[:, DZ:]], axis=0)[:count]

        inward_grad, outward_grad = columns(
            [group_one, group_two],
            [(1, (k + 1) * width, width, 0, 0, k * D) for k in range(3)]
            + [(0, 0, width, 0, 1, 0)]
            + [(0, (k + 2) * width, width, 0, 1, (k + 1) * D) for k in range(2)]
            + [(1, 0, width, 1, 0, 0), (0, width, width, 1, 1, 0)],
            [(2, DZ, 3 * D), (2, DZ, D)], f32, "spread_rest")

        return (
            layer_out[None], tokens_grad[None], encoded_grad[None],
            part[0:3], part[3:6], inward_grad, part[6:10].reshape(2, 2, DZ), outward_grad,
            part[10:12], upward_grad, part[13:].reshape(FZ), down_grad, part[12],
        )

    return body


def solution(mesh):
    rows = P("fsdp", "ctx", None)
    placed = (
        rows, rows, rows, P("fsdp", None), P("fsdp", None), P("fsdp", None),
        P(None, "fsdp"), P(None, "fsdp"), P(None, "fsdp", None), P(None, None, "fsdp"),
        P(None, "fsdp", None), P(None, "fsdp"), P("fsdp", None), P("fsdp"), P("fsdp", None), P("fsdp"),
    )
    return jax.shard_map(
        make_body(mesh.shape["ctx"], mesh.shape["fsdp"]),
        mesh=mesh,
        in_specs=placed,
        out_specs=(
            rows, rows, rows, P(None, "fsdp"), P(None, "fsdp"), P(None, "fsdp", None),
            P(None, None, "fsdp"), P(None, "fsdp", None), P(None, "fsdp"), P("fsdp", None),
            P("fsdp"), P("fsdp", None), P("fsdp"),
        ),
        check_vma=False,
    )
```

```python
import jax
import jax.numpy as jnp
from jax import lax
from jax.experimental import pallas as pl
from jax.experimental.pallas import tpu as pltpu
from jax.sharding import PartitionSpec as P

HEADS = 16
HEAD_DIM = 64
BLOCK = 128
DOCS = 16
QB = 256
KB = 256

epsilon = 1e-05
f32 = jnp.float32
bf16 = jnp.bfloat16
i32 = jnp.int32
VMEM_BYTES = 56 << 20
TIMES = {
    "cut_weights": 20, "assemble_a": 20, "project_self": 90, "attend_self": 100, "project_cross": 5, "attend_cross": 11,
    "mix_self": 5, "mix_cross": 4, "feed": 16, "feed_weights": 11, "feed_out": 5, "unmix_cross": 5, "unmix_self": 6,
    "attend_cross_back": 15, "attend_self_back": 14, "source_back": 5, "source_weights": 5, "self_back": 8,
    "unmix_tokens": 4, "feed_outputs": 6, "spread_rest": 6,
}


def cost(name):
    return pl.CostEstimate(
        flops=int(1.1e9 * TIMES.get(name, 4)), transcendentals=0, bytes_accessed=int(3.5e6 * TIMES.get(name, 4)))


def product(left, right):
    return jnp.dot(left, right, preferred_element_type=f32)


def contract_rows(left, right):
    return lax.dot_general(left, right, (((0,), (0,)), ((), ())), preferred_element_type=f32)


def times_transpose(left, right):
    return lax.dot_general(left, right, (((1,), (1,)), ((), ())), preferred_element_type=f32)


def normalise(values):
    centre = jnp.mean(values, axis=-1, keepdims=True)
    centred = values - centre
    inverse = lax.rsqrt(jnp.mean(centred * centred, axis=-1, keepdims=True) + epsilon)
    return centred * inverse, inverse


def norm_backward(upstream, scaled, inverse, gain_row):
    weighted = upstream * gain_row
    first_mean = jnp.mean(weighted, axis=-1, keepdims=True)
    second_mean = jnp.mean(weighted * scaled, axis=-1, keepdims=True)
    return inverse * (weighted - first_mean - scaled * second_mean)


def vmem():
    return pl.BlockSpec(memory_space=pltpu.VMEM)


def smem():
    return pl.BlockSpec(memory_space=pltpu.SMEM)


def project(pieces, weight, first, vectors, biases, me, norm, table, widths, padded, name):
    counts = [p.shape[0] for p in pieces]
    rows = sum(counts)
    depth = weight.shape[0]
    extra = [BLOCK if pad else 0 for pad in padded]
    n_in = len(pieces)
    total = sum(widths)
    aligned = widths[0] % 128 == 0
    if not aligned:
        own = [
            jnp.zeros((w,), f32) if b is None else lax.dynamic_slice_in_dim(vectors[b], me * w, w)
            for b, w in zip(biases, widths)
        ]
        own = jnp.concatenate(own)[None]

    def kernel(*refs):
        table_ref, me_ref = refs[:2]
        x_refs = refs[2 : 2 + n_in]
        w_ref, v_ref = refs[2 + n_in], refs[3 + n_in]
        at = 4 + n_in
        if not aligned:
            own_ref = refs[at]
            at += 1
        outs = refs[at : at + len(widths)]
        if norm:
            normed_ref = refs[at + len(widths)]
        bias = []
        left = 0
        for b, w in zip(biases, widths):
            if not aligned:
                bias.append(own_ref[0:1, left : left + w])
            elif b is not None:
                bias.append(v_ref[b : b + 1, pl.ds(pl.multiple_of(me_ref[0] * w, 128), w)])
            else:
                bias.append(None)
            left += w
        base = 0
        for x_ref, count in zip(x_refs, counts):
            step = min(count, 256)
            for sub in range(0, count, step):
                x = x_ref[sub : sub + step, :depth]
                if norm:
                    scaled, _ = normalise(x.astype(f32))
                    x = (scaled * v_ref[norm[0] : norm[0] + 1, :] + v_ref[norm[1] : norm[1] + 1, :]).astype(bf16)
                    normed_ref[base + sub : base + sub + step, :] = x
                y = product(x, w_ref[:, first : first + total])
                left = 0
                for out, width, row in zip(outs, widths, bias):
                    cut = y[:, left : left + width]
                    cut = (cut if row is None else cut + row).astype(bf16)
                    for part in range(0, step, BLOCK):
                        place = pl.multiple_of(table_ref[(base + sub + part) // BLOCK] * BLOCK, BLOCK)
                        out[pl.ds(place, BLOCK), :] = cut[part : part + BLOCK, :]
                    left += width
            base += count
        for out, width, more in zip(outs, widths, extra):
            if more:
                out[rows : rows + more, :] = jnp.zeros((more, width), bf16)

    out_shape = [jax.ShapeDtypeStruct((rows + more, width), bf16) for width, more in zip(widths, extra)]
    if norm:
        out_shape.append(jax.ShapeDtypeStruct((rows, depth), bf16))
    args = [table, me.reshape(1), *pieces, weight, vectors] + ([] if aligned else [own])
    return call(kernel, args, out_shape, [], name)


def split_rows(rows, heads):
    if heads == 1:
        return rows
    lane = lax.broadcasted_iota(i32, rows.shape, 1)
    zero = jnp.zeros_like(rows)
    parts = [
        jnp.where((lane >= h * HEAD_DIM) & (lane < (h + 1) * HEAD_DIM), rows, zero)
        for h in range(heads)
    ]
    return jnp.concatenate(parts, axis=0)


def own_rows(stacked, heads):
    if heads == 1:
        return stacked
    width = stacked.shape[1] // heads
    return jnp.concatenate(
        [
            stacked[h * HEAD_DIM : (h + 1) * HEAD_DIM, h * width : (h + 1) * width]
            for h in range(heads)
        ],
        axis=0,
    )


def load_blocks(ref, table_ref, block):
    parts = []
    for k in range(QB // BLOCK):
        place = pl.multiple_of(table_ref[block * (QB // BLOCK) + k] * BLOCK, BLOCK)
        parts.append(ref[pl.ds(place, BLOCK), :])
    return jnp.concatenate(parts, axis=0)


def store_blocks(ref, table_ref, block, values, left):
    width = values.shape[1]
    for k in range(QB // BLOCK):
        place = pl.multiple_of(table_ref[block * (QB // BLOCK) + k] * BLOCK, BLOCK)
        ref[pl.ds(place, BLOCK), left : left + width] = values[k * BLOCK : (k + 1) * BLOCK, :]


def key_weights(keys, query_rows, low, high, start, heads):
    scores = times_transpose(keys, query_rows)
    place = start + lax.broadcasted_iota(i32, (KB, QB), 0)
    allowed = (place >= low) & (place < high)
    parts = [
        jnp.where(allowed, jnp.exp(scores[:, h * QB : (h + 1) * QB]), 0.0) for h in range(heads)
    ]
    return jnp.concatenate(parts, axis=1) if heads > 1 else parts[0]


def attend(tables, query, keys, values, low, high, name):
    first, last, query_table, out_table = tables
    rows, width = query.shape
    heads = width // HEAD_DIM
    key_rows = keys.shape[0]
    tall = width + 16

    def kernel(
        first_ref, last_ref, qt_ref, ot_ref, q_ref, k_ref, v_ref, lo_ref, hi_ref,
        mixed_ref, wide_ref, inv_ref, vt_ref, acc_ref,
    ):
        for c in range(0, key_rows, BLOCK):
            vt_ref[0:width, c : c + BLOCK] = v_ref[c : c + BLOCK, :].T
        vt_ref[width:tall, :] = jnp.ones((16, key_rows), bf16)

        def one(i, carry):
            q = split_rows(load_blocks(q_ref, qt_ref, i) * jnp.asarray(HEAD_DIM ** (-0.5), bf16), heads)
            lo = lo_ref[pl.ds(i, 1), :]
            hi = hi_ref[pl.ds(i, 1), :]
            acc_ref[...] = jnp.zeros_like(acc_ref)
            begin = first_ref[i]

            def step(j, c):
                start = pl.multiple_of((begin + j * (KB // BLOCK)) * BLOCK, BLOCK)
                w = key_weights(k_ref[pl.ds(start, KB), :], q, lo, hi, start, heads)
                acc_ref[...] += product(vt_ref[:, pl.ds(start, KB)], w.astype(bf16))
                return c

            lax.fori_loop(0, (last_ref[i] - begin + KB // BLOCK - 1) // (KB // BLOCK), step, 0)
            acc = acc_ref[...]
            inverse = 1.0 / acc[width : width + 1, :]
            mixed = own_rows(acc[0:width, :] * inverse, heads).T
            inv = own_rows(jnp.broadcast_to(inverse, (width, heads * QB)), heads).T
            wide_ref[pl.ds(pl.multiple_of(i * QB, QB), QB), :] = mixed
            inv_ref[pl.ds(pl.multiple_of(i * QB, QB), QB), :] = inv
            store_blocks(mixed_ref, ot_ref, i, mixed.astype(bf16), 0)
            return carry

        lax.fori_loop(0, rows // QB, one, 0)

    return pl.pallas_call(
        kernel,
        out_shape=[
            jax.ShapeDtypeStruct((rows, width), bf16),
            jax.ShapeDtypeStruct((rows, width), f32),
            jax.ShapeDtypeStruct((rows, width), f32),
        ],
        in_specs=[smem()] * 4 + [vmem()] * 5,
        out_specs=[vmem()] * 3,
        scratch_shapes=[pltpu.VMEM((tall, key_rows), bf16), pltpu.VMEM((tall, heads * QB), f32)],
        compiler_params=pltpu.CompilerParams(vmem_limit_bytes=VMEM_BYTES),
        cost_estimate=cost(name),
        name=name,
    )(first, last, query_table, out_table, query, keys, values, low, high)


def attend_back(tables, query, keys, values, low, high, upstream, wide, inverse, joined, name):
    first, last, query_table, up_table, dq_table, dk_table = tables
    rows, width = query.shape
    heads = width // HEAD_DIM
    key_rows = keys.shape[0]
    held = key_rows - BLOCK
    scale = HEAD_DIM ** (-0.5)

    def kernel(
        first_ref, last_ref, qt_ref, ut_ref, dqt_ref, dkt_ref,
        q_ref, k_ref, v_ref, lo_ref, hi_ref, up_ref, wide_ref, inv_ref, *rest,
    ):
        if joined:
            dq_ref, kt_ref, dk_acc, dv_acc, dq_acc = rest
            dkv_ref = dq_ref
            left = width
        else:
            dq_ref, dkv_ref, kt_ref, dk_acc, dv_acc, dq_acc = rest
            left = 0
        for c in range(0, key_rows, BLOCK):
            kt_ref[:, c : c + BLOCK] = k_ref[c : c + BLOCK, :].T
        dk_acc[...] = jnp.zeros_like(dk_acc)
        dv_acc[...] = jnp.zeros_like(dv_acc)

        def one(i, carry):
            here = pl.ds(pl.multiple_of(i * QB, QB), QB)
            q = split_rows(load_blocks(q_ref, qt_ref, i) * jnp.asarray(scale, bf16), heads)
            shared = load_blocks(up_ref, ut_ref, i)[:, :width].astype(f32) * inv_ref[here, :]
            total = -(shared * wide_ref[here, :]).T
            total = [
                jnp.sum(total[h * HEAD_DIM : (h + 1) * HEAD_DIM, :], axis=0, keepdims=True)
                for h in range(heads)
            ]
            total = jnp.concatenate(total, axis=1) if heads > 1 else total[0]
            shared = split_rows(shared.astype(bf16), heads)
            lo = lo_ref[pl.ds(i, 1), :]
            hi = hi_ref[pl.ds(i, 1), :]
            dq_acc[...] = jnp.zeros_like(dq_acc)
            begin = first_ref[i]

            def step(j, c):
                start = pl.multiple_of((begin + j * (KB // BLOCK)) * BLOCK, BLOCK)
                some = pl.ds(start, KB)
                w = key_weights(k_ref[some, :], q, lo, hi, start, heads)
                grad = times_transpose(v_ref[some, :], shared)
                ds = (w * (grad + total)).astype(bf16)
                dv_acc[some, :] += product(w.astype(bf16), shared)
                dk_acc[some, :] += product(ds, q)
                dq_acc[...] += product(kt_ref[:, some], ds)
                return c

            lax.fori_loop(0, (last_ref[i] - begin + KB // BLOCK - 1) // (KB // BLOCK), step, 0)
            dq = own_rows(dq_acc[...] * scale, heads).T.astype(bf16)
            store_blocks(dq_ref, dqt_ref, i, dq, 0)
            return carry

        lax.fori_loop(0, rows // QB, one, 0)

        def flush(b, carry):
            here = pl.ds(pl.multiple_of(b * BLOCK, BLOCK), BLOCK)
            there = pl.ds(pl.multiple_of(dkt_ref[b] * BLOCK, BLOCK), BLOCK)
            dkv_ref[there, left : left + width] = dk_acc[here, :].astype(bf16)
            dkv_ref[there, left + width : left + 2 * width] = dv_acc[here, :].astype(bf16)
            return carry

        lax.fori_loop(0, held // BLOCK, flush, 0)

    if joined:
        out_shape = [jax.ShapeDtypeStruct((rows, 3 * width), bf16)]
    else:
        out_shape = [
            jax.ShapeDtypeStruct((rows, width), bf16),
            jax.ShapeDtypeStruct((held, 2 * width), bf16),
        ]
    return pl.pallas_call(
        kernel,
        out_shape=out_shape,
        in_specs=[smem()] * 6 + [vmem()] * 8,
        out_specs=[vmem()] * len(out_shape),
        scratch_shapes=[
            pltpu.VMEM((width, key_rows), bf16),
            pltpu.VMEM((key_rows, width), f32),
            pltpu.VMEM((key_rows, width), f32),
            pltpu.VMEM((width, heads * QB), f32),
        ],
        compiler_params=pltpu.CompilerParams(vmem_limit_bytes=VMEM_BYTES),
        cost_estimate=cost(name),
        name=name,
    )(first, last, query_table, up_table, dq_table, dk_table,
      query, keys, values, low, high, upstream, wide, inverse)


def cut_weights(inward, outward, upward, downward, small, me, width, units, parts, name):
    depth, D = outward.shape[1:]
    stride = upward.shape[1] // parts

    F = parts * units
    tall, wide = small.shape

    def kernel(me_ref, small_ref, in_ref, out_ref, up_ref, down_ref, a_ref, b_ref, sems):
        at = pl.multiple_of(me_ref[0] * width, 128)
        unit = pl.multiple_of(me_ref[0] * units, 128)
        plan = []
        for k in range(3):
            plan.append((in_ref.at[0, :, pl.ds(k * D + at, width)], a_ref.at[0:depth, pl.ds(k * width, width)]))
        plan.append((out_ref.at[0, :, pl.ds(at, width)], a_ref.at[0:depth, pl.ds(3 * width, width)]))
        plan.append((in_ref.at[1, :, pl.ds(at, width)], a_ref.at[0:depth, pl.ds(4 * width, width)]))
        for k in range(2):
            plan.append((in_ref.at[1, :, pl.ds((k + 1) * D + at, width)], b_ref.at[:, pl.ds(k * width, width)]))
        plan.append((out_ref.at[1, :, pl.ds(at, width)], b_ref.at[:, pl.ds(2 * width, width)]))
        for k in range(parts):
            plan.append((up_ref.at[:, pl.ds(k * stride + unit, units)],
                         b_ref.at[:, pl.ds(3 * width + k * units, units)]))
        for q in range(D // F):
            plan.append((down_ref.at[pl.ds(unit, units), q * F : (q + 1) * F],
                         b_ref.at[q * units : (q + 1) * units, pl.ds(3 * width + F, F)]))
        copies = [pltpu.make_async_copy(src, dst, sems.at[k]) for k, (src, dst) in enumerate(plan)]
        for c in copies:
            c.start()
        a_ref[depth : depth + tall, 0:wide] = small_ref[...]
        a_ref[depth : depth + tall, wide : 5 * width] = jnp.zeros((tall, 5 * width - wide), bf16)
        for c in copies:
            c.wait()

    return pl.pallas_call(
        kernel,
        out_shape=[
            jax.ShapeDtypeStruct((depth + tall, 5 * width), bf16),
            jax.ShapeDtypeStruct((depth, 3 * width + 2 * F), bf16),
        ],
        in_specs=[smem(), vmem()] + [pl.BlockSpec(memory_space=pl.ANY)] * 4,
        out_specs=[vmem()] * 2,
        scratch_shapes=[pltpu.SemaphoreType.DMA((8 + parts + D // F,))],
        compiler_params=pltpu.CompilerParams(vmem_limit_bytes=VMEM_BYTES),
        cost_estimate=cost(name),
        name=name,
    )(me.reshape(1), small, inward, outward, upward, downward)


def assemble(pieces, places, widths, tall, name):
    depth = pieces[0].shape[0] - tall
    count = len(pieces)

    def kernel(*refs):
        place_ref, parts, outs = refs[0], refs[1 : 1 + count], refs[1 + count :]
        for d, part in enumerate(parts):
            at = pl.multiple_of(place_ref[d] * depth, depth)
            left = 0
            for out, width in zip(outs, widths):
                out[pl.ds(at, depth), :] = part[0:depth, left : left + width]
                left += width
            for k in range(2):
                outs[-1][k * tall : (k + 1) * tall, pl.ds(at, depth)] = part[
                    depth : depth + tall, k * depth : (k + 1) * depth].astype(f32)

    shapes = [jax.ShapeDtypeStruct((count * depth, w), bf16) for w in widths]
    shapes.append(jax.ShapeDtypeStruct((2 * tall, count * depth), f32))
    return call(kernel, [places, *pieces], shapes, [], name)


def spread_columns(pieces, near, plan, shapes, dtype, name):
    stacked = [len(group) == 1 for group in pieces]
    counts = [len(group) for group in pieces]
    flat = [p for group in pieces for p in group]

    def kernel(*refs):
        near_ref, parts, outs = refs[0], refs[1 : 1 + len(flat)], refs[1 + len(flat) :]
        for group, first, width, out, lead, base in plan:
            skip = sum(counts[:group])
            for r in range(near.shape[0]):
                there = pl.ds(pl.multiple_of(base + near_ref[r] * width, 128), width)
                part = parts[skip].at[r] if stacked[group] else parts[skip + r]
                value = part[: shapes[out][-2], first : first + width].astype(dtype)
                if lead is None:
                    outs[out][:, there] = value
                else:
                    outs[out][lead, :, there] = value

    return pl.pallas_call(
        kernel,
        out_shape=[jax.ShapeDtypeStruct(shape, dtype) for shape in shapes],
        in_specs=[smem()] + [vmem()] * len(flat),
        out_specs=[vmem()] * len(shapes),
        compiler_params=pltpu.CompilerParams(vmem_limit_bytes=VMEM_BYTES),
        cost_estimate=cost(name),
        name=name,
    )(near, *flat)


def call(kernel, args, out_shape, scratch, name):
    small = [a.ndim == 1 and a.dtype == i32 for a in args]
    return pl.pallas_call(
        kernel,
        out_shape=out_shape,
        in_specs=[smem() if is_small else vmem() for is_small in small],
        out_specs=[vmem()] * len(out_shape),
        scratch_shapes=scratch,
        compiler_params=pltpu.CompilerParams(vmem_limit_bytes=VMEM_BYTES),
        cost_estimate=cost(name),
        name=name,
    )(*args)


def columns_at(order_ref, fixed, r, width):
    if fixed:
        return pl.ds(r * width, width)
    return pl.ds(pl.multiple_of(order_ref[r] * width, 128), width)


def block_at(order_ref, fixed, r):
    return r if fixed else order_ref[r]


def mix(received, pieces, order, fixed, residual, rows, first, width, query, name):
    C, T = received.shape[:2]
    D = residual.shape[1]
    stacked = len(pieces) == 1

    def kernel(*refs):
        order_ref, rec_ref = refs[:2]
        parts = refs[2 : 2 + len(pieces)]
        res_ref, rows_ref, after_ref, kept_ref, last_ref, y_ref = refs[2 + len(pieces) :]

        def weights(r, left):
            part = parts[0].at[r] if stacked else parts[r]
            return part[:, left : left + width]

        def pairs(x, left):
            for r in range(0, C, 2):
                both = product(x, jnp.concatenate([weights(r, left), weights(r + 1, left)], axis=1))
                yield r, both[:, :width]
                yield r + 1, both[:, width:]

        mixed = jnp.concatenate([rec_ref[c] for c in range(C)], axis=1)
        kept_ref[:, 0:D] = mixed
        for r, value in pairs(mixed, first):
            y_ref[:, columns_at(order_ref, fixed, r, width)] = value
        values = res_ref[...].astype(f32) + (y_ref[...] + rows_ref[0:1, :])
        after_ref[...] = values
        scaled, _ = normalise(values)
        normed = (scaled * rows_ref[1:2, :] + rows_ref[2:3, :]).astype(bf16)
        if not query:
            last_ref[...] = normed
        else:
            kept_ref[:, D : 2 * D] = normed
            for r, value in pairs(normed, first + width):
                bias = rows_ref[3:4, columns_at(order_ref, fixed, r, width)]
                last_ref[block_at(order_ref, fixed, r)] = (value + bias).astype(bf16)

    shapes = [
        jax.ShapeDtypeStruct((T, D), f32),
        jax.ShapeDtypeStruct((T, 2 * D if query else D), bf16),
        jax.ShapeDtypeStruct((C, T, width) if query else (T, D), bf16),
    ]
    return call(kernel, [order, received, *pieces, residual, rows], shapes,
                [pltpu.VMEM((T, D), f32)], name)


def unmix(grads, query_grads, query_pieces, pieces, order, fixed, firsts, upstream, values, gain, width, name):
    T, D = upstream.shape
    C = D // width
    joined = query_pieces is pieces and pieces is not None
    lists = [list(grads)]
    lists.append([query_grads] if query_grads is not None else [])
    lists.append(list(query_pieces) if query_pieces is not None and not joined else [])
    lists.append(list(pieces) if pieces is not None else [])
    flat = [a for part in lists for a in part]
    low_out = pieces is not None

    def kernel(*refs):
        order_ref = refs[0]
        at = 1
        got = []
        for part in lists:
            got.append(refs[at : at + len(part)])
            at += len(part)
        up_ref, val_ref, gain_ref = refs[at : at + 3]
        at += 3
        if low_out:
            grad_ref, m_ref, sums_ref = refs[at : at + 3]
        else:
            grad_ref, sums_ref = refs[at : at + 2]
        ws = got[3]
        qs = ws if joined else got[2]

        def weights(parts, r, left):
            part = parts[0].at[r] if len(parts) == 1 else parts[r]
            return part[:, left : left + width]

        def back(columns, parts, left):
            total = None
            for r in range(0, C, 2):
                cols = jnp.concatenate([columns(r), columns(r + 1)], axis=1)
                both = jnp.concatenate([weights(parts, r, left), weights(parts, r + 1, left)], axis=1)
                part = times_transpose(cols, both)
                total = part if total is None else total + part
            return total

        sums_ref[...] = jnp.zeros_like(sums_ref)
        if query_grads is not None:
            dq_ref = got[1][0]
            grad = back(lambda r: dq_ref[block_at(order_ref, fixed, r)], qs, firsts[0])
            for c in range(C):
                sums_ref[3:4, c * width : (c + 1) * width] = jnp.sum(
                    dq_ref[c].astype(f32), axis=0, keepdims=True)
        else:
            grad = got[0][0][...].astype(f32)
            for g in got[0][1:]:
                grad = grad + g[...].astype(f32)
        scaled, inverse = normalise(val_ref[...].astype(f32))
        sums_ref[0:1, :] = jnp.sum(grad * scaled, axis=0, keepdims=True)
        sums_ref[1:2, :] = jnp.sum(grad, axis=0, keepdims=True)
        upstream_values = up_ref[...].astype(f32)
        if query_grads is None:
            sums_ref[3:4, :] = jnp.sum(upstream_values, axis=0, keepdims=True)
        result = upstream_values + norm_backward(grad, scaled, inverse, gain_ref[...])
        grad_ref[...] = result
        if low_out:
            low = result.astype(bf16)
            for c in range(C):
                m_ref[c, :, width : 2 * width] = low[:, c * width : (c + 1) * width]
            sums_ref[2:3, :] = jnp.sum(low.astype(f32), axis=0, keepdims=True)
            m = back(lambda r: m_ref[block_at(order_ref, fixed, r), :, width : 2 * width], ws, firsts[1])
            for c in range(C):
                m_ref[c, :, 0:width] = m[:, c * width : (c + 1) * width].astype(bf16)

    shapes = [jax.ShapeDtypeStruct((T, D), f32)]
    if low_out:
        shapes.append(jax.ShapeDtypeStruct((C, T, 2 * width), bf16))
    shapes.append(jax.ShapeDtypeStruct((8, D), f32))
    return call(kernel, [order, *flat, upstream, values, gain], shapes, [], name)


def parts_shapes(cube, C, T, D):
    if cube:
        return [jax.ShapeDtypeStruct((T, D), bf16)] * 5 + [jax.ShapeDtypeStruct((3, T, D), bf16)]
    return [jax.ShapeDtypeStruct((C, T, D), bf16)]


def store_part(cube, refs, r, value):
    if not cube:
        refs[0][r] = value
    elif r < 4:
        refs[r][...] = value
    elif r == 7:
        refs[4][...] = value
    else:
        refs[5][r - 4] = value


ROOT = 0.7978845608028654


def feed(normed, cotangent, order, fixed, up, first, down, up_bias, cube, name):
    C = len(normed)
    T, D = normed[0].shape
    F = down.shape[0]

    def kernel(*refs):
        order_ref = refs[0]
        n_refs = refs[1 : 1 + C]
        cot_ref, up_ref, down_ref, bias_ref = refs[1 + C : 5 + C]
        hidden_ref, grad_ref, sum_ref = refs[5 + C : 8 + C]
        part_refs = refs[8 + C :]
        total = jnp.zeros((1, F), f32)
        for r in range(C):
            pre = product(n_refs[r][...], up_ref[:, first : first + F]) + bias_ref[...]
            square = pre * pre
            inner = jnp.tanh(ROOT * pre * (1.0 + 0.044715 * square))
            half = 0.5 * (1.0 + inner)
            rows = slice(r * T, (r + 1) * T)
            hidden_ref[rows, :] = (pre * half).astype(bf16)
            slope = half + 0.5 * pre * (1.0 - inner * inner) * (ROOT * (1.0 + 3 * 0.044715 * square))
            cot = cot_ref[block_at(order_ref, fixed, r)]
            low = (times_transpose(cot, down_ref[...]) * slope).astype(bf16)
            grad_ref[rows, :] = low
            total = total + jnp.sum(low.astype(f32), axis=0, keepdims=True)
            store_part(cube, part_refs, r, times_transpose(low, up_ref[:, first : first + F]).astype(bf16))
        sum_ref[...] = total

    shapes = [
        jax.ShapeDtypeStruct((C * T, F), bf16),
        jax.ShapeDtypeStruct((C * T, F), bf16),
        jax.ShapeDtypeStruct((1, F), f32),
    ] + parts_shapes(cube, C, T, D)
    return call(kernel, [order, *normed, cotangent, up, down, up_bias], shapes, [], name)


def feed_weights(normed, cotangent, order, fixed, hidden, up_grad, parts, name):
    C = len(normed)
    T, D = normed[0].shape
    F = hidden.shape[1]
    depth, units = D // parts, F // parts

    def kernel(*refs):
        order_ref = refs[0]
        n_refs = refs[1 : 1 + C]
        cot_ref, hid_ref, grad_ref, out_ref, up_acc, down_acc = refs[1 + C :]
        for r in range(C):
            rows = slice(r * T, (r + 1) * T)
            up = contract_rows(n_refs[r][...], grad_ref[rows, :])
            down = contract_rows(hid_ref[rows, :], cot_ref[block_at(order_ref, fixed, r)])
            if r == 0:
                up_acc[...] = up
                down_acc[...] = down
            else:
                up_acc[...] += up
                down_acc[...] += down
        for z in range(parts):
            out_ref[z, 0:depth, :] = up_acc[z * depth : (z + 1) * depth, :].astype(bf16)
            for q in range(D // F):
                out_ref[z, depth + q * units : depth + (q + 1) * units, :] = down_acc[
                    z * units : (z + 1) * units, q * F : (q + 1) * F].astype(bf16)

    return call(kernel, [order, *normed, cotangent, hidden, up_grad],
                [jax.ShapeDtypeStruct((parts, 2 * depth, F), bf16)],
                [pltpu.VMEM((D, F), f32), pltpu.VMEM((F, D), f32)], name)[0]


def feed_outputs(gathered, parts, D, name):
    C, _, F = gathered.shape
    depth, units = D // parts, F // parts
    FF, FZ = C * F, C * units

    def kernel(x_ref, up_ref, down_ref):
        for c in range(C):
            for z in range(parts):
                at = z * FZ + c * units
                up_ref[:, at : at + units] = x_ref[c, 0:depth, z * units : (z + 1) * units].astype(f32)
            for q in range(D // F):
                down_ref[c * units : (c + 1) * units, q * F : (q + 1) * F] = x_ref[
                    c, depth + q * units : depth + (q + 1) * units, :].astype(f32)

    return call(kernel, [gathered], [
        jax.ShapeDtypeStruct((depth, FF), f32), jax.ShapeDtypeStruct((FZ, D), f32)], [], name)


def times_weight(x, weight, columns, turned, order, ordered, cube, C, name):
    T = x.shape[0] // C
    D = weight.shape[0] if turned else columns

    def kernel(order_ref, x_ref, w_ref, *outs):
        for r in range(C):
            rows = x_ref[r * T : (r + 1) * T, :]
            some = w_ref[:, :columns]
            value = times_transpose(rows, some) if turned else product(rows, some)
            if ordered:
                outs[0][order_ref[r]] = value.astype(bf16)
            else:
                store_part(cube, outs, r, value.astype(bf16))

    shapes = [jax.ShapeDtypeStruct((C, T, D), bf16)] if ordered else parts_shapes(cube, C, T, D)
    return call(kernel, [order, x, weight], shapes, [], name)


def self_back(tokens, grads, weight, sums, me, cube, name):
    C = len(tokens)
    T, D = tokens[0].shape
    Z = sums.shape[0]
    DZ = D // Z
    width = weight.shape[1] // 3

    def kernel(me_ref, *refs):
        x_refs, (g_ref, w_ref, sums_ref, out_ref), outs = refs[:C], refs[C : C + 4], refs[C + 4 :]
        first = jnp.zeros((1, D), f32)
        second = jnp.zeros((1, D), f32)
        bias = jnp.zeros((1, 3 * width), f32)
        for r in range(C):
            rows = g_ref[r * T : (r + 1) * T, :]
            grad = times_transpose(rows, w_ref[...])
            store_part(cube, outs, r, grad.astype(bf16))
            scaled, _ = normalise(x_refs[r][...].astype(f32))
            first = first + jnp.sum(grad * scaled, axis=0, keepdims=True)
            second = second + jnp.sum(grad, axis=0, keepdims=True)
            bias = bias + jnp.sum(rows.astype(f32), axis=0, keepdims=True)
        lane = lax.broadcasted_iota(i32, (1, D), 1)
        spot = (lane >= me_ref[0] * width) & (lane < (me_ref[0] + 1) * width)

        def at_own(row):
            return jnp.where(spot, jnp.concatenate([row] * C, axis=1), 0.0)

        late = {0: first, 3: second, 6: at_own(bias[:, :width]), 7: at_own(bias[:, 2 * width :])}
        for z in range(Z):
            block = sums_ref[z]
            place = lax.broadcasted_iota(i32, block.shape, 0)
            for k, row in late.items():
                cut = row[:, z * DZ : (z + 1) * DZ]
                cut = jnp.concatenate([cut, jnp.zeros_like(cut)], axis=1)
                block = block + jnp.where(place == k, cut, 0.0)
            out_ref[z] = block.astype(bf16)

    shapes = [jax.ShapeDtypeStruct(sums.shape, bf16)] + parts_shapes(cube, C, T, D)
    return call(kernel, [me.reshape(1), *tokens, grads, weight, sums], shapes, [], name)


def contract_pieces(pieces, grads, name):
    C = len(pieces)
    T, D = pieces[0].shape
    N = grads.shape[1]

    def kernel(*refs):
        x_refs, (g_ref, out_ref, acc_ref) = refs[:C], refs[C:]
        for r in range(C):
            part = contract_rows(x_refs[r][...], g_ref[r * T : (r + 1) * T, :])
            if r == 0:
                acc_ref[...] = part
            else:
                acc_ref[...] += part
        out_ref[...] = acc_ref[...].astype(bf16)

    return call(kernel, [*pieces, grads], [jax.ShapeDtypeStruct((D, N), bf16)],
                [pltpu.VMEM((D, N), f32)], name)[0]


def after(x, *others):
    return lax.optimization_barrier((x, *others))[0]


def together(many, *others):
    return lax.optimization_barrier((*many, *others))[: len(many)]


def make_body(C, Z):
    cube = C == 8
    relative = [0, 2, 4, 6, 1, 3, 5, 7] if cube else list(range(C))

    def hop(x, bit):
        return lax.ppermute(x, "ctx", [(i, i ^ bit) for i in range(C)])

    def hop_diag(x):
        return lax.ppermute(x, "ctx", [(i, i ^ (4 if i & 1 else 2)) for i in range(C)])

    def gather_halves(x):
        if not cube:
            return [x, x, x], lambda hold: gather_steps(x, hold)
        odd = lax.axis_index("ctx") & 1
        own, ex, wy = hop(x, 1), hop(x, 2), hop(x, 4)

        def rest(hold):
            one, two = (ex, wy) if hold is None else together((ex, wy), hold)
            chosen = jnp.where(odd == 1, one, two)
            diag = hop_diag(chosen)
            first = [x, ex, wy, diag, own, hop(one, 1), hop(two, 1)]
            return first, chosen, lambda held: first + [hop(diag if held is None else after(diag, held), 1)]

        return [own, ex, wy], rest

    def gather_steps(x, hold):
        if not cube:
            whole = lax.all_gather(x, "ctx", axis=0, tiled=False)
            blocks = [whole[r] for r in range(C)]
            return blocks, x, lambda held: blocks
        return gather_halves(x)[1](hold)

    def gather_rows(x, hold=None):
        return gather_steps(x, hold)[2](None)

    def scatter_parts(parts):
        if not cube:
            done = lax.psum_scatter(parts[0], "ctx", scatter_dimension=0, tiled=False)
            return [done], done, done
        odd = lax.axis_index("ctx") & 1
        even, other_diag, others = parts[:4], parts[4], parts[5]
        got_diag = hop(other_diag, 1)
        got = hop(others, 1)
        second = (even[3].astype(f32) + got_diag.astype(f32)).astype(bf16)
        passed = hop_diag(second).astype(f32)
        ex = even[1].astype(f32) + got[1].astype(f32) + jnp.where(odd == 1, passed, 0.0)
        wy = even[2].astype(f32) + got[2].astype(f32) + jnp.where(odd == 1, 0.0, passed)
        third = wy.astype(bf16)
        got_x = hop(ex.astype(bf16), 2)
        got_y = hop(third, 4)
        return [even[0], got[0], got_x, got_y], second, third

    def tree_sum(blocks):
        parts = [blocks[relative.index(r)] for r in range(C)]
        while len(parts) > 1:
            parts = [parts[k] + parts[k + 1] for k in range(0, len(parts), 2)]
        return parts[0]

    def exchange(x):
        return lax.all_to_all(x, "ctx", split_axis=0, concat_axis=0, tiled=True)

    def zhop(x, d):
        return lax.ppermute(x, "fsdp", [(i, (i + d) % Z) for i in range(Z)])

    far_first = sorted(range(1, Z), key=lambda d: -min(d, Z - d))

    def zgather(x):
        got = {d: zhop(x, d) for d in far_first}
        return [x] + [got[d] for d in range(1, Z)]

    def zscatter(blocks, hold=None):
        got = lax.all_to_all(blocks, "fsdp", split_axis=0, concat_axis=0, tiled=True)
        if hold is not None:
            got = after(got, hold)
        return jnp.sum(got.astype(f32), axis=0)

    def body(
        tokens, encoded, cotangent, target_segments, source_segments, block_order,
        norm_gain, norm_shift, inward, inbias, outward, outbias, upward, upbias, downward, downbias,
    ):
        T, D = tokens.shape[1:]
        S = encoded.shape[1]
        L = C * T
        DZ = norm_gain.shape[1]
        FZ = downward.shape[0]
        FF = FZ * Z
        U = FZ // C
        width = D // C
        lanes = width % 128 == 0 and U % 128 == 0
        me = lax.axis_index("ctx")
        zi = lax.axis_index("fsdp")
        near = jnp.array(relative, i32)
        if cube:
            near = near ^ me
        zplace = (zi - jnp.arange(Z, dtype=i32)) % Z
        fixed = not cube
        steady = jnp.arange(C, dtype=i32)

        def mine(x, dims, axis):
            return lax.dynamic_index_in_dim(x.reshape(dims), me, axis, keepdims=False)

        def columns(groups, plan, shapes, dtype, name):
            if lanes:
                return spread_columns(groups, near, plan, shapes, dtype, name)
            outs = [[None] * (shape[0] if len(shape) == 3 else 1) for shape in shapes]
            for group, first, w, out, lead, base in sorted(plan, key=lambda p: p[5]):
                stacked = jnp.stack(groups[group])[:, : shapes[out][-2], first : first + w].astype(dtype)
                part = stacked.transpose(1, 0, 2).reshape(stacked.shape[1], -1)
                k = lead or 0
                outs[out][k] = part if outs[out][k] is None else jnp.concatenate([outs[out][k], part], axis=1)
            return [o[0] if len(shape) == 2 else jnp.stack(o) for o, shape in zip(outs, shapes)]

        small = jnp.concatenate(
            [norm_gain, norm_shift, inbias.reshape(4, DZ), outbias, downbias.reshape(1, DZ),
             upbias.reshape(FZ // DZ, DZ), jnp.zeros((19 - FZ // DZ, DZ), bf16)], axis=0)
        small = jnp.concatenate([small[:16], small[16:]], axis=1)
        F = Z * U
        if lanes:
            cut_a, cut_b = cut_weights(
                inward, outward, upward, downward, small, me, width, U, Z, "cut_weights")
        else:
            in_one = mine(inward[0], (DZ, 3, C, width), 2).reshape(DZ, 3 * width)
            in_two = mine(inward[1], (DZ, 3, C, width), 2).reshape(DZ, 3 * width)
            outs = mine(outward, (2, DZ, C, width), 2)
            cut_a = jnp.concatenate([in_one, outs[0], in_two[:, :width]], axis=1)
            cut_a = jnp.concatenate([cut_a, jnp.pad(small, ((0, 0), (0, 5 * width - 2 * DZ)))], axis=0)
            cut_up = mine(upward, (DZ, Z, C, U), 2).reshape(DZ, F)
            cut_down = mine(downward, (C, U, D), 0).reshape(U, D // F, F).transpose(1, 0, 2).reshape(DZ, F)
            cut_b = jnp.concatenate([in_two[:, width:], outs[1], cut_up, cut_down], axis=1)

        pieces_a = zgather(cut_a)
        token_start, token_chosen, token_join = gather_steps(after(tokens[0], cut_a), None)
        source_start, source_chosen, source_join = gather_steps(after(encoded[0], token_chosen), None)
        w_self, w_pair, vectors = assemble(
            list(together(pieces_a, token_chosen)), zplace, [3 * width, 2 * width], 16, "assemble_a")
        token_pieces = token_join(w_self)
        pair_start, pair_rest = gather_halves(w_pair)
        w_b = lax.all_gather(after(cut_b, w_self), "fsdp", axis=0, tiled=True)
        w_down = w_b[:, 3 * width + F :].reshape(Z, D // F, U, F).transpose(0, 2, 1, 3).reshape(F, D)
        w_out = w_b[:, 2 * width : 3 * width]
        gains, shifts = vectors[0:3], vectors[3:6]
        outb, downb = vectors[10:12], vectors[12]
        upb = vectors[13 : 13 + FZ // DZ].reshape(FZ // DZ, Z, DZ).transpose(1, 0, 2)
        upb = mine(upb.reshape(FF), (Z, C, U), 1).reshape(F)

        blocks = T // BLOCK
        index = jnp.arange(C * blocks, dtype=i32)
        order = block_order[0]
        by_device = order.reshape(1, C, blocks)
        near_order = jnp.sum(
            jnp.where(near[:, None, None] == jnp.arange(C, dtype=i32)[None, :, None], by_device, 0), axis=1
        ).reshape(-1)

        def inverted(table):
            return jnp.sum(jnp.where(table[None, :] == index[:, None], index[None, :], 0), axis=1)

        source_table = (near[:, None] * blocks + jnp.arange(blocks, dtype=i32)).reshape(-1)
        near_source = inverted(source_table)
        stored = inverted(order)
        near_stored = inverted(near_order)
        seg = target_segments[0]
        docs = jnp.arange(DOCS, dtype=i32)[:, None]
        own_doc = seg[None, :] == docs
        t_start = jnp.sum((seg[None, :] < docs).astype(i32), axis=1)
        s_start = jnp.sum((source_segments[0][None, :] < docs).astype(i32), axis=1)
        s_end = jnp.sum((source_segments[0][None, :] <= docs).astype(i32), axis=1)

        def per_row(table):
            return jnp.sum(jnp.where(own_doc, table[:, None], 0), axis=0).reshape(L // QB, QB)

        self_low = per_row(t_start)
        self_high = jnp.arange(1, L + 1, dtype=i32).reshape(L // QB, QB)
        cross_low, cross_high = per_row(s_start), per_row(s_end)
        self_first = self_low[:, 0] // BLOCK
        self_last = self_high[:, -1] // BLOCK
        cross_first = cross_low[:, 0] // BLOCK
        cross_last = (cross_high[:, -1] + BLOCK - 1) // BLOCK

        q1, k1, v1, normed_one = project(
            token_pieces, after(w_self, source_chosen, pair_start[0]), 0, vectors, [6, None, 7], me, (0, 3),
            near_order, [width] * 3, [False, True, True], "project_self")
        source_pieces = source_join(None)
        mixed1, wide1, inv1 = attend(
            (self_first, self_last, index, stored), after(q1, source_start[3]), k1, v1, self_low, self_high,
            "attend_self")
        pair = pair_rest(q1)[2](mixed1)
        cot = lax.all_gather(after(cotangent[0], q1), "ctx", axis=0, tiled=False)
        mixed_one = exchange(mixed1.reshape(C, T, width))

        after_self, kept_self, q2_own = mix(
            mixed_one, pair, near, fixed, tokens[0],
            jnp.stack([outb[0], gains[1], shifts[1], vectors[8]]), 0, width, True, "mix_self")
        q2 = exchange(q2_own).reshape(L, width)
        k2, v2 = project(
            source_pieces, after(w_b, q2_own), 0, vectors, [None, 9], me, None, source_table,
            [width] * 2, [True, True], "project_cross")
        mixed2, wide2, inv2 = attend(
            (cross_first, cross_last, stored, stored), q2, k2, v2, cross_low, cross_high,
            "attend_cross")
        kept_self = lax.all_gather(kept_self, "ctx", axis=0, tiled=True)
        out_two = gather_rows(after(w_out, q2_own), mixed2)
        mixed_two = exchange(mixed2.reshape(C, T, width))
        after_cross, kept_cross, normed_three = mix(
            mixed_two, out_two, near, fixed, after(after_self, cot),
            jnp.stack([outb[1], gains[2], shifts[2]]), 0, width, False, "mix_cross")

        kept_cross = lax.all_gather(after(kept_cross, kept_self), "ctx", axis=0, tiled=True)

        n3 = gather_rows(normed_three)
        hidden, up_grad, upb_tp, *parts = feed(
            n3, cot, near, fixed, w_b, 3 * width, w_down, upb[None], cube, "feed")
        back_three, second, third = scatter_parts(parts)
        feed_dw = feed_weights(
            n3, cot, near, fixed, hidden, after(up_grad, third), Z, "feed_weights")
        feed_sum = lax.psum_scatter(feed_dw, "fsdp", scatter_dimension=0, tiled=False)


        cross_grad, m2_own, sums_three = unmix(
            back_three, None, None, out_two, near, fixed, (0, 0), after(cotangent[0], feed_dw), after_cross,
            gains[2:3], width, "unmix_cross")
        m2 = exchange(m2_own).reshape(L, 2 * width)
        out_parts = times_weight(
            hidden, after(w_down, m2_own), D, False, near, False, cube, C, "feed_out")
        out_terms, out_second, out_third = scatter_parts(out_parts)
        dq2, dkv2 = attend_back(
            (cross_first, cross_last, stored, stored, stored, near_source),
            q2, k2, v2, cross_low, cross_high, after(m2, out_parts[0]), wide2, inv2, False, "attend_cross_back")
        layer_out = (after_cross + (sum(t.astype(f32) for t in out_terms) + downb)).astype(bf16)
        dq2_own = exchange(dq2.reshape(C, T, width))
        (source_part,) = times_weight(dkv2, w_b, 2 * width, True, near, True, cube, C, "source_back")
        encoded_grad = lax.psum_scatter(source_part, "ctx", scatter_dimension=0, tiled=False).astype(f32)
        self_grad, m1_own, sums_two = unmix(
            [], dq2_own, pair, pair, near, fixed, (width, 0), after(cross_grad, source_part, out_third), after_self,
            gains[1:2], width, "unmix_self")


        m1 = exchange(m1_own).reshape(L, 2 * width)
        group_one = jnp.concatenate([
            contract_rows(kept_self[:, D:], after(dq2, m1_own)).astype(bf16),
            contract_rows(kept_cross, after(m2, m1_own)[:, width:]).astype(bf16),
            contract_pieces(source_pieces, after(dkv2, m1_own), "source_weights"),
        ], axis=1).reshape(Z, DZ, 4 * width)
        feed_all = lax.all_gather(after(feed_sum, m1_own), "ctx", axis=0, tiled=False)
        m1 = after(m1, group_one)
        group_one = zscatter(group_one).astype(bf16)
        (dqkv,) = attend_back(
            (self_first, self_last, index, stored, near_stored, near_stored),
            q1, k1, v1, self_low, self_high, m1, wide1, inv1, True, "attend_self_back")
        def placed(part, count):
            part = part.reshape(count, 1, -1)
            spot = lax.broadcasted_iota(i32, (count, C, part.shape[2]), 1) == me
            return jnp.where(spot, part, 0.0)

        dkv2_sum = placed(jnp.sum(dkv2[:, width:].astype(f32), axis=0), 1).reshape(D)
        upb_rows = placed(upb_tp, Z).reshape(Z, FZ // DZ, DZ)
        none = jnp.zeros((D,), f32)
        sums = jnp.stack([
            none, sums_two[0], sums_three[0], none, sums_two[1], sums_three[1],
            none, none, sums_two[3], dkv2_sum, sums_two[2], sums_three[2], sums_three[3],
        ])
        count = 13 + FZ // DZ
        sums = jnp.concatenate([
            sums.reshape(13, Z, DZ).transpose(1, 0, 2), upb_rows, jnp.zeros((Z, 32 - count, DZ), f32)], axis=1)
        sums = jnp.concatenate([sums[:, :16], sums[:, 16:]], axis=2)
        sums, *parts_one = self_back(
            token_pieces, dqkv, w_self, after(sums, m1), me, cube, "self_back")
        back_one, _, back_third = scatter_parts(parts_one)
        group_two = jnp.concatenate([
            contract_rows(kept_self[:, :D], m1[:, width:]).astype(bf16),
            contract_rows(normed_one, after(dqkv, encoded_grad)).astype(bf16),
        ], axis=1)
        group_two = jnp.concatenate([group_two.reshape(Z, DZ, 4 * width), sums], axis=1)
        group_two = zscatter(after(group_two, group_one), back_third).astype(bf16)
        one_start, one_chosen, one_join = gather_steps(after(group_one, parts_one[0]), back_third)
        group_one = one_join(None)
        upward_grad, down_grad = feed_outputs(after(feed_all, back_third), Z, D, "feed_outputs")
        tokens_grad, _ = unmix(
            back_one, None, None, None, near, fixed, (0, 0),
            after(self_grad, upward_grad, one_chosen, group_two), tokens[0], gains[0:1], width, "unmix_tokens")
        group_two = gather_rows(after(group_two, tokens_grad))
        part = tree_sum([g[DZ:].astype(f32) for g in group_two])
        part = jnp.concatenate([part[:, :DZ], part[:, DZ:]], axis=0)[:count]

        inward_grad, outward_grad = columns(
            [group_one, group_two],
            [(1, (k + 1) * width, width, 0, 0, k * D) for k in range(3)]
            + [(0, 0, width, 0, 1, 0)]
            + [(0, (k + 2) * width, width, 0, 1, (k + 1) * D) for k in range(2)]
            + [(1, 0, width, 1, 0, 0), (0, width, width, 1, 1, 0)],
            [(2, DZ, 3 * D), (2, DZ, D)], f32, "spread_rest")

        return (
            layer_out[None], tokens_grad[None], encoded_grad[None],
            part[0:3], part[3:6], inward_grad, part[6:10].reshape(2, 2, DZ), outward_grad,
            part[10:12], upward_grad, part[13:].reshape(FZ), down_grad, part[12],
        )

    return body


def solution(mesh):
    rows = P("fsdp", "ctx", None)
    placed = (
        rows, rows, rows, P("fsdp", None), P("fsdp", None), P("fsdp", None),
        P(None, "fsdp"), P(None, "fsdp"), P(None, "fsdp", None), P(None, None, "fsdp"),
        P(None, "fsdp", None), P(None, "fsdp"), P("fsdp", None), P("fsdp"), P("fsdp", None), P("fsdp"),
    )
    return jax.shard_map(
        make_body(mesh.shape["ctx"], mesh.shape["fsdp"]),
        mesh=mesh,
        in_specs=placed,
        out_specs=(
            rows, rows, rows, P(None, "fsdp"), P(None, "fsdp"), P(None, "fsdp", None),
            P(None, None, "fsdp"), P(None, "fsdp", None), P(None, "fsdp"), P("fsdp", None),
            P("fsdp"), P("fsdp", None), P("fsdp"),
        ),
        check_vma=False,
    )
```

```python
import jax
import jax.numpy as jnp
from jax import lax
from jax.experimental import pallas as pl
from jax.experimental.pallas import tpu as pltpu
from jax.sharding import PartitionSpec as P

HEADS = 16
HEAD_DIM = 64
BLOCK = 128
DOCS = 16
QB = 256
KB = 256

epsilon = 1e-05
f32 = jnp.float32
bf16 = jnp.bfloat16
i32 = jnp.int32
VMEM_BYTES = 56 << 20
TIMES = {
    "cut_weights": 20, "assemble_a": 20, "project_self": 90, "attend_self": 100, "project_cross": 5, "attend_cross": 11,
    "mix_self": 5, "mix_cross": 4, "feed": 16, "feed_weights": 11, "feed_out": 5, "unmix_cross": 5, "unmix_self": 6,
    "attend_cross_back": 15, "attend_self_back": 14, "source_back": 5, "source_weights": 5, "self_back": 8,
    "unmix_tokens": 4, "feed_outputs": 6, "spread_rest": 6,
}


def cost(name):
    return pl.CostEstimate(
        flops=int(1.1e9 * TIMES.get(name, 4)), transcendentals=0, bytes_accessed=int(3.5e6 * TIMES.get(name, 4)))


def product(left, right):
    return jnp.dot(left, right, preferred_element_type=f32)


def contract_rows(left, right):
    return lax.dot_general(left, right, (((0,), (0,)), ((), ())), preferred_element_type=f32)


def times_transpose(left, right):
    return lax.dot_general(left, right, (((1,), (1,)), ((), ())), preferred_element_type=f32)


def normalise(values):
    centre = jnp.mean(values, axis=-1, keepdims=True)
    centred = values - centre
    inverse = lax.rsqrt(jnp.mean(centred * centred, axis=-1, keepdims=True) + epsilon)
    return centred * inverse, inverse


def norm_backward(upstream, scaled, inverse, gain_row):
    weighted = upstream * gain_row
    first_mean = jnp.mean(weighted, axis=-1, keepdims=True)
    second_mean = jnp.mean(weighted * scaled, axis=-1, keepdims=True)
    return inverse * (weighted - first_mean - scaled * second_mean)


def vmem():
    return pl.BlockSpec(memory_space=pltpu.VMEM)


def smem():
    return pl.BlockSpec(memory_space=pltpu.SMEM)


def project(pieces, weight, first, vectors, biases, me, norm, table, widths, padded, name):
    counts = [p.shape[0] for p in pieces]
    rows = sum(counts)
    depth = weight.shape[0]
    extra = [BLOCK if pad else 0 for pad in padded]
    n_in = len(pieces)
    total = sum(widths)
    aligned = widths[0] % 128 == 0
    if not aligned:
        own = [
            jnp.zeros((w,), f32) if b is None else lax.dynamic_slice_in_dim(vectors[b], me * w, w)
            for b, w in zip(biases, widths)
        ]
        own = jnp.concatenate(own)[None]

    def kernel(*refs):
        table_ref, me_ref = refs[:2]
        x_refs = refs[2 : 2 + n_in]
        w_ref, v_ref = refs[2 + n_in], refs[3 + n_in]
        at = 4 + n_in
        if not aligned:
            own_ref = refs[at]
            at += 1
        outs = refs[at : at + len(widths)]
        if norm:
            normed_ref = refs[at + len(widths)]
        bias = []
        left = 0
        for b, w in zip(biases, widths):
            if not aligned:
                bias.append(own_ref[0:1, left : left + w])
            elif b is not None:
                bias.append(v_ref[b : b + 1, pl.ds(pl.multiple_of(me_ref[0] * w, 128), w)])
            else:
                bias.append(None)
            left += w
        base = 0
        for x_ref, count in zip(x_refs, counts):
            step = min(count, 256)
            for sub in range(0, count, step):
                x = x_ref[sub : sub + step, :depth]
                if norm:
                    scaled, _ = normalise(x.astype(f32))
                    x = (scaled * v_ref[norm[0] : norm[0] + 1, :] + v_ref[norm[1] : norm[1] + 1, :]).astype(bf16)
                    normed_ref[base + sub : base + sub + step, :] = x
                y = product(x, w_ref[:, first : first + total])
                left = 0
                for out, width, row in zip(outs, widths, bias):
                    cut = y[:, left : left + width]
                    cut = (cut if row is None else cut + row).astype(bf16)
                    for part in range(0, step, BLOCK):
                        place = pl.multiple_of(table_ref[(base + sub + part) // BLOCK] * BLOCK, BLOCK)
                        out[pl.ds(place, BLOCK), :] = cut[part : part + BLOCK, :]
                    left += width
            base += count
        for out, width, more in zip(outs, widths, extra):
            if more:
                out[rows : rows + more, :] = jnp.zeros((more, width), bf16)

    out_shape = [jax.ShapeDtypeStruct((rows + more, width), bf16) for width, more in zip(widths, extra)]
    if norm:
        out_shape.append(jax.ShapeDtypeStruct((rows, depth), bf16))
    args = [table, me.reshape(1), *pieces, weight, vectors] + ([] if aligned else [own])
    return call(kernel, args, out_shape, [], name)


def split_rows(rows, heads):
    if heads == 1:
        return rows
    lane = lax.broadcasted_iota(i32, rows.shape, 1)
    zero = jnp.zeros_like(rows)
    parts = [
        jnp.where((lane >= h * HEAD_DIM) & (lane < (h + 1) * HEAD_DIM), rows, zero)
        for h in range(heads)
    ]
    return jnp.concatenate(parts, axis=0)


def own_rows(stacked, heads):
    if heads == 1:
        return stacked
    width = stacked.shape[1] // heads
    return jnp.concatenate(
        [
            stacked[h * HEAD_DIM : (h + 1) * HEAD_DIM, h * width : (h + 1) * width]
            for h in range(heads)
        ],
        axis=0,
    )


def load_blocks(ref, table_ref, block):
    parts = []
    for k in range(QB // BLOCK):
        place = pl.multiple_of(table_ref[block * (QB // BLOCK) + k] * BLOCK, BLOCK)
        parts.append(ref[pl.ds(place, BLOCK), :])
    return jnp.concatenate(parts, axis=0)


def store_blocks(ref, table_ref, block, values, left):
    width = values.shape[1]
    for k in range(QB // BLOCK):
        place = pl.multiple_of(table_ref[block * (QB // BLOCK) + k] * BLOCK, BLOCK)
        ref[pl.ds(place, BLOCK), left : left + width] = values[k * BLOCK : (k + 1) * BLOCK, :]


def key_weights(keys, query_rows, low, high, start, heads):
    scores = times_transpose(keys, query_rows)
    place = start + lax.broadcasted_iota(i32, (KB, QB), 0)
    allowed = (place >= low) & (place < high)
    parts = [
        jnp.where(allowed, jnp.exp(scores[:, h * QB : (h + 1) * QB]), 0.0) for h in range(heads)
    ]
    return jnp.concatenate(parts, axis=1) if heads > 1 else parts[0]


def attend(tables, query, keys, values, low, high, name):
    first, last, query_table, out_table = tables
    rows, width = query.shape
    heads = width // HEAD_DIM
    key_rows = keys.shape[0]
    tall = width + 16

    def kernel(
        first_ref, last_ref, qt_ref, ot_ref, q_ref, k_ref, v_ref, lo_ref, hi_ref,
        mixed_ref, wide_ref, inv_ref, vt_ref, acc_ref,
    ):
        for c in range(0, key_rows, BLOCK):
            vt_ref[0:width, c : c + BLOCK] = v_ref[c : c + BLOCK, :].T
        vt_ref[width:tall, :] = jnp.ones((16, key_rows), bf16)

        def one(i, carry):
            q = split_rows(load_blocks(q_ref, qt_ref, i) * jnp.asarray(HEAD_DIM ** (-0.5), bf16), heads)
            lo = lo_ref[pl.ds(i, 1), :]
            hi = hi_ref[pl.ds(i, 1), :]
            acc_ref[...] = jnp.zeros_like(acc_ref)
            begin = first_ref[i]

            def step(j, c):
                start = pl.multiple_of((begin + j * (KB // BLOCK)) * BLOCK, BLOCK)
                w = key_weights(k_ref[pl.ds(start, KB), :], q, lo, hi, start, heads)
                acc_ref[...] += product(vt_ref[:, pl.ds(start, KB)], w.astype(bf16))
                return c

            lax.fori_loop(0, (last_ref[i] - begin + KB // BLOCK - 1) // (KB // BLOCK), step, 0)
            acc = acc_ref[...]
            inverse = 1.0 / acc[width : width + 1, :]
            mixed = own_rows(acc[0:width, :] * inverse, heads).T
            inv = own_rows(jnp.broadcast_to(inverse, (width, heads * QB)), heads).T
            wide_ref[pl.ds(pl.multiple_of(i * QB, QB), QB), :] = mixed
            inv_ref[pl.ds(pl.multiple_of(i * QB, QB), QB), :] = inv
            store_blocks(mixed_ref, ot_ref, i, mixed.astype(bf16), 0)
            return carry

        lax.fori_loop(0, rows // QB, one, 0)

    return pl.pallas_call(
        kernel,
        out_shape=[
            jax.ShapeDtypeStruct((rows, width), bf16),
            jax.ShapeDtypeStruct((rows, width), f32),
            jax.ShapeDtypeStruct((rows, width), f32),
        ],
        in_specs=[smem()] * 4 + [vmem()] * 5,
        out_specs=[vmem()] * 3,
        scratch_shapes=[pltpu.VMEM((tall, key_rows), bf16), pltpu.VMEM((tall, heads * QB), f32)],
        compiler_params=pltpu.CompilerParams(vmem_limit_bytes=VMEM_BYTES),
        cost_estimate=cost(name),
        name=name,
    )(first, last, query_table, out_table, query, keys, values, low, high)


def attend_back(tables, query, keys, values, low, high, upstream, wide, inverse, joined, name):
    first, last, query_table, up_table, dq_table, dk_table = tables
    rows, width = query.shape
    heads = width // HEAD_DIM
    key_rows = keys.shape[0]
    held = key_rows - BLOCK
    scale = HEAD_DIM ** (-0.5)

    def kernel(
        first_ref, last_ref, qt_ref, ut_ref, dqt_ref, dkt_ref,
        q_ref, k_ref, v_ref, lo_ref, hi_ref, up_ref, wide_ref, inv_ref, *rest,
    ):
        if joined:
            dq_ref, kt_ref, dk_acc, dv_acc, dq_acc = rest
            dkv_ref = dq_ref
            left = width
        else:
            dq_ref, dkv_ref, kt_ref, dk_acc, dv_acc, dq_acc = rest
            left = 0
        for c in range(0, key_rows, BLOCK):
            kt_ref[:, c : c + BLOCK] = k_ref[c : c + BLOCK, :].T
        dk_acc[...] = jnp.zeros_like(dk_acc)
        dv_acc[...] = jnp.zeros_like(dv_acc)

        def one(i, carry):
            here = pl.ds(pl.multiple_of(i * QB, QB), QB)
            q = split_rows(load_blocks(q_ref, qt_ref, i) * jnp.asarray(scale, bf16), heads)
            shared = load_blocks(up_ref, ut_ref, i)[:, :width].astype(f32) * inv_ref[here, :]
            total = -(shared * wide_ref[here, :]).T
            total = [
                jnp.sum(total[h * HEAD_DIM : (h + 1) * HEAD_DIM, :], axis=0, keepdims=True)
                for h in range(heads)
            ]
            total = jnp.concatenate(total, axis=1) if heads > 1 else total[0]
            shared = split_rows(shared.astype(bf16), heads)
            lo = lo_ref[pl.ds(i, 1), :]
            hi = hi_ref[pl.ds(i, 1), :]
            dq_acc[...] = jnp.zeros_like(dq_acc)
            begin = first_ref[i]

            def step(j, c):
                start = pl.multiple_of((begin + j * (KB // BLOCK)) * BLOCK, BLOCK)
                some = pl.ds(start, KB)
                w = key_weights(k_ref[some, :], q, lo, hi, start, heads)
                grad = times_transpose(v_ref[some, :], shared)
                ds = (w * (grad + total)).astype(bf16)
                dv_acc[some, :] += product(w.astype(bf16), shared)
                dk_acc[some, :] += product(ds, q)
                dq_acc[...] += product(kt_ref[:, some], ds)
                return c

            lax.fori_loop(0, (last_ref[i] - begin + KB // BLOCK - 1) // (KB // BLOCK), step, 0)
            dq = own_rows(dq_acc[...] * scale, heads).T.astype(bf16)
            store_blocks(dq_ref, dqt_ref, i, dq, 0)
            return carry

        lax.fori_loop(0, rows // QB, one, 0)

        def flush(b, carry):
            here = pl.ds(pl.multiple_of(b * BLOCK, BLOCK), BLOCK)
            there = pl.ds(pl.multiple_of(dkt_ref[b] * BLOCK, BLOCK), BLOCK)
            dkv_ref[there, left : left + width] = dk_acc[here, :].astype(bf16)
            dkv_ref[there, left + width : left + 2 * width] = dv_acc[here, :].astype(bf16)
            return carry

        lax.fori_loop(0, held // BLOCK, flush, 0)

    if joined:
        out_shape = [jax.ShapeDtypeStruct((rows, 3 * width), bf16)]
    else:
        out_shape = [
            jax.ShapeDtypeStruct((rows, width), bf16),
            jax.ShapeDtypeStruct((held, 2 * width), bf16),
        ]
    return pl.pallas_call(
        kernel,
        out_shape=out_shape,
        in_specs=[smem()] * 6 + [vmem()] * 8,
        out_specs=[vmem()] * len(out_shape),
        scratch_shapes=[
            pltpu.VMEM((width, key_rows), bf16),
            pltpu.VMEM((key_rows, width), f32),
            pltpu.VMEM((key_rows, width), f32),
            pltpu.VMEM((width, heads * QB), f32),
        ],
        compiler_params=pltpu.CompilerParams(vmem_limit_bytes=VMEM_BYTES),
        cost_estimate=cost(name),
        name=name,
    )(first, last, query_table, up_table, dq_table, dk_table,
      query, keys, values, low, high, upstream, wide, inverse)


def cut_weights(inward, outward, upward, downward, small, me, width, units, parts, name):
    depth, D = outward.shape[1:]
    stride = upward.shape[1] // parts

    F = parts * units
    tall, wide = small.shape

    def kernel(me_ref, small_ref, in_ref, out_ref, up_ref, down_ref, a_ref, b_ref, sems):
        at = pl.multiple_of(me_ref[0] * width, 128)
        unit = pl.multiple_of(me_ref[0] * units, 128)
        plan = []
        for k in range(3):
            plan.append((in_ref.at[0, :, pl.ds(k * D + at, width)], a_ref.at[0:depth, pl.ds(k * width, width)]))
        plan.append((out_ref.at[0, :, pl.ds(at, width)], a_ref.at[0:depth, pl.ds(3 * width, width)]))
        plan.append((in_ref.at[1, :, pl.ds(at, width)], a_ref.at[0:depth, pl.ds(4 * width, width)]))
        for k in range(2):
            plan.append((in_ref.at[1, :, pl.ds((k + 1) * D + at, width)], b_ref.at[:, pl.ds(k * width, width)]))
        plan.append((out_ref.at[1, :, pl.ds(at, width)], b_ref.at[:, pl.ds(2 * width, width)]))
        for k in range(parts):
            plan.append((up_ref.at[:, pl.ds(k * stride + unit, units)],
                         b_ref.at[:, pl.ds(3 * width + k * units, units)]))
        for q in range(D // F):
            plan.append((down_ref.at[pl.ds(unit, units), q * F : (q + 1) * F],
                         b_ref.at[q * units : (q + 1) * units, pl.ds(3 * width + F, F)]))
        copies = [pltpu.make_async_copy(src, dst, sems.at[k]) for k, (src, dst) in enumerate(plan)]
        for c in copies:
            c.start()
        a_ref[depth : depth + tall, 0:wide] = small_ref[...]
        a_ref[depth : depth + tall, wide : 5 * width] = jnp.zeros((tall, 5 * width - wide), bf16)
        for c in copies:
            c.wait()

    return pl.pallas_call(
        kernel,
        out_shape=[
            jax.ShapeDtypeStruct((depth + tall, 5 * width), bf16),
            jax.ShapeDtypeStruct((depth, 3 * width + 2 * F), bf16),
        ],
        in_specs=[smem(), vmem()] + [pl.BlockSpec(memory_space=pl.ANY)] * 4,
        out_specs=[vmem()] * 2,
        scratch_shapes=[pltpu.SemaphoreType.DMA((8 + parts + D // F,))],
        compiler_params=pltpu.CompilerParams(vmem_limit_bytes=VMEM_BYTES),
        cost_estimate=cost(name),
        name=name,
    )(me.reshape(1), small, inward, outward, upward, downward)


def assemble(pieces, places, widths, tall, name):
    depth = pieces[0].shape[0] - tall
    count = len(pieces)

    def kernel(*refs):
        place_ref, parts, outs = refs[0], refs[1 : 1 + count], refs[1 + count :]
        for d, part in enumerate(parts):
            at = pl.multiple_of(place_ref[d] * depth, depth)
            left = 0
            for out, width in zip(outs, widths):
                out[pl.ds(at, depth), :] = part[0:depth, left : left + width]
                left += width
            for k in range(2):
                outs[-1][k * tall : (k + 1) * tall, pl.ds(at, depth)] = part[
                    depth : depth + tall, k * depth : (k + 1) * depth].astype(f32)

    shapes = [jax.ShapeDtypeStruct((count * depth, w), bf16) for w in widths]
    shapes.append(jax.ShapeDtypeStruct((2 * tall, count * depth), f32))
    return call(kernel, [places, *pieces], shapes, [], name)


def spread_columns(pieces, near, plan, shapes, dtype, name):
    counts = [len(group) for group in pieces]
    flat = [p for group in pieces for p in group]
    slabs = []
    for item in plan:
        if item[3:5] not in slabs:
            slabs.append(item[3:5])

    def kernel(*refs):
        near_ref, parts = refs[0], refs[1 : 1 + len(flat)]
        outs = refs[1 + len(flat) : 1 + len(flat) + len(shapes)]
        bufs, sems = refs[1 + len(flat) + len(shapes) : -1], refs[-1]
        going = Copies(sems)
        for slab in slabs:
            for group, first, width, out, lead, base in plan:
                if (out, lead) != slab:
                    continue
                skip = sum(counts[:group])
                for r in range(near.shape[0]):
                    there = pl.ds(pl.multiple_of(base + near_ref[r] * width, 128), width)
                    value = parts[skip + r][: shapes[out][-2], first : first + width].astype(dtype)
                    if lead is None:
                        bufs[out][:, there] = value
                    else:
                        bufs[out][lead, :, there] = value
            out, lead = slab
            if lead is None:
                going.start(bufs[out], outs[out])
            else:
                going.start(bufs[out].at[lead], outs[out].at[lead])
        going.finish()

    return call(kernel, [near, *flat], [jax.ShapeDtypeStruct(shape, dtype) for shape in shapes],
                [pltpu.VMEM(shape, dtype) for shape in shapes] + [pltpu.SemaphoreType.DMA((len(slabs),))],
                name, (), range(len(shapes)))


def call(kernel, args, out_shape, scratch, name, far_args=(), far_outs=()):
    def spec(k, a, far):
        if k in far:
            return pl.BlockSpec(memory_space=pl.ANY)
        return smem() if a.ndim == 1 and a.dtype == i32 else vmem()

    return pl.pallas_call(
        kernel,
        out_shape=out_shape,
        in_specs=[spec(k, a, far_args) for k, a in enumerate(args)],
        out_specs=[pl.BlockSpec(memory_space=pl.ANY) if k in far_outs else vmem() for k in range(len(out_shape))],
        scratch_shapes=scratch,
        compiler_params=pltpu.CompilerParams(vmem_limit_bytes=VMEM_BYTES),
        cost_estimate=cost(name),
        name=name,
    )(*args)


class Copies:
    def __init__(self, sems):
        self.sems, self.used, self.open = sems, 0, []

    def start(self, source, target):
        copy = pltpu.make_async_copy(source, target, self.sems.at[self.used])
        copy.start()
        self.used += 1
        self.open.append(copy)
        return copy

    def finish(self):
        for copy in self.open:
            copy.wait()


def columns_at(order_ref, fixed, r, width):
    if fixed:
        return pl.ds(r * width, width)
    return pl.ds(pl.multiple_of(order_ref[r] * width, 128), width)


def block_at(order_ref, fixed, r):
    return r if fixed else order_ref[r]


def mix(received, pieces, order, fixed, residual, rows, first, width, query, name):
    C, T = received.shape[:2]
    D = residual.shape[1]
    stacked = len(pieces) == 1

    def kernel(*refs):
        order_ref, rec_ref = refs[:2]
        parts = refs[2 : 2 + len(pieces)]
        res_ref, rows_ref, after_ref, kept_ref, last_ref, y_ref = refs[2 + len(pieces) :]

        def weights(r, left):
            part = parts[0].at[r] if stacked else parts[r]
            return part[:, left : left + width]

        def pairs(x, left):
            for r in range(0, C, 2):
                both = product(x, jnp.concatenate([weights(r, left), weights(r + 1, left)], axis=1))
                yield r, both[:, :width]
                yield r + 1, both[:, width:]

        mixed = jnp.concatenate([rec_ref[c] for c in range(C)], axis=1)
        kept_ref[:, 0:D] = mixed
        for r, value in pairs(mixed, first):
            y_ref[:, columns_at(order_ref, fixed, r, width)] = value
        values = res_ref[...].astype(f32) + (y_ref[...] + rows_ref[0:1, :])
        after_ref[...] = values
        scaled, _ = normalise(values)
        normed = (scaled * rows_ref[1:2, :] + rows_ref[2:3, :]).astype(bf16)
        if not query:
            last_ref[...] = normed
        else:
            kept_ref[:, D : 2 * D] = normed
            for r, value in pairs(normed, first + width):
                bias = rows_ref[3:4, columns_at(order_ref, fixed, r, width)]
                last_ref[block_at(order_ref, fixed, r)] = (value + bias).astype(bf16)

    shapes = [
        jax.ShapeDtypeStruct((T, D), f32),
        jax.ShapeDtypeStruct((T, 2 * D if query else D), bf16),
        jax.ShapeDtypeStruct((C, T, width) if query else (T, D), bf16),
    ]
    return call(kernel, [order, received, *pieces, residual, rows], shapes,
                [pltpu.VMEM((T, D), f32)], name)


def unmix(grads, query_grads, query_pieces, pieces, order, fixed, firsts, upstream, values, gain, width, name):
    T, D = upstream.shape
    C = D // width
    joined = query_pieces is pieces and pieces is not None
    lists = [list(grads)]
    lists.append([query_grads] if query_grads is not None else [])
    lists.append(list(query_pieces) if query_pieces is not None and not joined else [])
    lists.append(list(pieces) if pieces is not None else [])
    flat = [a for part in lists for a in part]
    low_out = pieces is not None

    def kernel(*refs):
        order_ref = refs[0]
        at = 1
        got = []
        for part in lists:
            got.append(refs[at : at + len(part)])
            at += len(part)
        up_ref, val_ref, gain_ref = refs[at : at + 3]
        at += 3
        if low_out:
            grad_ref, m_ref, sums_ref = refs[at : at + 3]
        else:
            grad_ref, sums_ref = refs[at : at + 2]
        ws = got[3]
        qs = ws if joined else got[2]

        def weights(parts, r, left):
            part = parts[0].at[r] if len(parts) == 1 else parts[r]
            return part[:, left : left + width]

        def back(columns, parts, left):
            total = None
            for r in range(0, C, 2):
                cols = jnp.concatenate([columns(r), columns(r + 1)], axis=1)
                both = jnp.concatenate([weights(parts, r, left), weights(parts, r + 1, left)], axis=1)
                part = times_transpose(cols, both)
                total = part if total is None else total + part
            return total

        sums_ref[...] = jnp.zeros_like(sums_ref)
        if query_grads is not None:
            dq_ref = got[1][0]
            grad = back(lambda r: dq_ref[block_at(order_ref, fixed, r)], qs, firsts[0])
            for c in range(C):
                sums_ref[3:4, c * width : (c + 1) * width] = jnp.sum(
                    dq_ref[c].astype(f32), axis=0, keepdims=True)
        else:
            grad = got[0][0][...].astype(f32)
            for g in got[0][1:]:
                grad = grad + g[...].astype(f32)
        scaled, inverse = normalise(val_ref[...].astype(f32))
        sums_ref[0:1, :] = jnp.sum(grad * scaled, axis=0, keepdims=True)
        sums_ref[1:2, :] = jnp.sum(grad, axis=0, keepdims=True)
        upstream_values = up_ref[...].astype(f32)
        if query_grads is None:
            sums_ref[3:4, :] = jnp.sum(upstream_values, axis=0, keepdims=True)
        result = upstream_values + norm_backward(grad, scaled, inverse, gain_ref[...])
        grad_ref[...] = result
        if low_out:
            low = result.astype(bf16)
            for c in range(C):
                m_ref[c, :, width : 2 * width] = low[:, c * width : (c + 1) * width]
            sums_ref[2:3, :] = jnp.sum(low.astype(f32), axis=0, keepdims=True)
            m = back(lambda r: m_ref[block_at(order_ref, fixed, r), :, width : 2 * width], ws, firsts[1])
            for c in range(C):
                m_ref[c, :, 0:width] = m[:, c * width : (c + 1) * width].astype(bf16)

    shapes = [jax.ShapeDtypeStruct((T, D), f32)]
    if low_out:
        shapes.append(jax.ShapeDtypeStruct((C, T, 2 * width), bf16))
    shapes.append(jax.ShapeDtypeStruct((8, D), f32))
    return call(kernel, [order, *flat, upstream, values, gain], shapes, [], name)


def parts_shapes(cube, C, T, D):
    if cube:
        return [jax.ShapeDtypeStruct((T, D), bf16)] * 5 + [jax.ShapeDtypeStruct((3, T, D), bf16)]
    return [jax.ShapeDtypeStruct((C, T, D), bf16)]


def store_part(cube, refs, r, value):
    if not cube:
        refs[0][r] = value
    elif r < 4:
        refs[r][...] = value
    elif r == 7:
        refs[4][...] = value
    else:
        refs[5][r - 4] = value


def part_at(cube, refs, r):
    if not cube:
        return refs[0].at[r]
    if r < 4:
        return refs[r]
    return refs[4] if r == 7 else refs[5].at[r - 4]


ROOT = 0.7978845608028654


def feed(normed, cotangent, order, fixed, up, first, down, up_bias, cube, name):
    C = len(normed)
    T, D = normed[0].shape
    F = down.shape[0]

    def kernel(*refs):
        order_ref = refs[0]
        n_refs = refs[1 : 1 + C]
        cot_ref, up_ref, down_ref, bias_ref = refs[1 + C : 5 + C]
        hidden_ref, grad_ref, sum_ref = refs[5 + C : 8 + C]
        part_refs = refs[8 + C :]
        total = jnp.zeros((1, F), f32)
        for g in range(0, C, 4):
            group = range(g, g + 4)
            rows = slice(g * T, (g + 4) * T)
            normed_rows = jnp.concatenate([n_refs[r][...] for r in group], axis=0)
            pre = product(normed_rows, up_ref[:, first : first + F]) + bias_ref[...]
            square = pre * pre
            inner = jnp.tanh(ROOT * pre * (1.0 + 0.044715 * square))
            half = 0.5 * (1.0 + inner)
            hidden_ref[rows, :] = (pre * half).astype(bf16)
            slope = half + 0.5 * pre * (1.0 - inner * inner) * (ROOT * (1.0 + 3 * 0.044715 * square))
            cot = jnp.concatenate([cot_ref[block_at(order_ref, fixed, r)] for r in group], axis=0)
            low = (times_transpose(cot, down_ref[...]) * slope).astype(bf16)
            grad_ref[rows, :] = low
            total = total + jnp.sum(low.astype(f32), axis=0, keepdims=True)
            back = times_transpose(low, up_ref[:, first : first + F]).astype(bf16)
            for k, r in enumerate(group):
                store_part(cube, part_refs, r, back[k * T : (k + 1) * T, :])
        sum_ref[...] = total

    shapes = [
        jax.ShapeDtypeStruct((C * T, F), bf16),
        jax.ShapeDtypeStruct((C * T, F), bf16),
        jax.ShapeDtypeStruct((1, F), f32),
    ] + parts_shapes(cube, C, T, D)
    return call(kernel, [order, *normed, cotangent, up, down, up_bias], shapes, [], name)


def feed_weights(normed, cotangent, order, fixed, hidden, up_grad, parts, name):
    C = len(normed)
    T, D = normed[0].shape
    F = hidden.shape[1]
    depth, units = D // parts, F // parts

    def kernel(*refs):
        order_ref = refs[0]
        n_refs = refs[1 : 1 + C]
        cot_ref, hid_ref, grad_ref, out_ref, up_acc, down_acc = refs[1 + C :]
        for r in range(C):
            rows = slice(r * T, (r + 1) * T)
            up = contract_rows(n_refs[r][...], grad_ref[rows, :])
            down = contract_rows(hid_ref[rows, :], cot_ref[block_at(order_ref, fixed, r)])
            if r == 0:
                up_acc[...] = up
                down_acc[...] = down
            else:
                up_acc[...] += up
                down_acc[...] += down
        for z in range(parts):
            out_ref[z, 0:depth, :] = up_acc[z * depth : (z + 1) * depth, :].astype(bf16)
            for q in range(D // F):
                out_ref[z, depth + q * units : depth + (q + 1) * units, :] = down_acc[
                    z * units : (z + 1) * units, q * F : (q + 1) * F].astype(bf16)

    return call(kernel, [order, *normed, cotangent, hidden, up_grad],
                [jax.ShapeDtypeStruct((parts, 2 * depth, F), bf16)],
                [pltpu.VMEM((D, F), f32), pltpu.VMEM((F, D), f32)], name)[0]


def feed_outputs(gathered, parts, D, name):
    C, _, F = gathered.shape
    depth, units = D // parts, F // parts
    FF, FZ = C * F, C * units

    def kernel(x_ref, up_ref, down_ref):
        for c in range(C):
            for z in range(parts):
                at = z * FZ + c * units
                up_ref[:, at : at + units] = x_ref[c, 0:depth, z * units : (z + 1) * units].astype(f32)
            for q in range(D // F):
                down_ref[c * units : (c + 1) * units, q * F : (q + 1) * F] = x_ref[
                    c, depth + q * units : depth + (q + 1) * units, :].astype(f32)

    return call(kernel, [gathered], [
        jax.ShapeDtypeStruct((depth, FF), f32), jax.ShapeDtypeStruct((FZ, D), f32)], [], name)


def times_weight(x, weight, columns, turned, order, ordered, cube, C, name):
    T = x.shape[0] // C
    D = weight.shape[0] if turned else columns

    shapes = [jax.ShapeDtypeStruct((C, T, D), bf16)] if ordered else parts_shapes(cube, C, T, D)

    def kernel(order_ref, x_ref, w_ref, *refs):
        outs, buf, sems = refs[: len(shapes)], refs[-2], refs[-1]
        going = Copies(sems)
        for r in range(C):
            rows = x_ref[r * T : (r + 1) * T, :]
            some = w_ref[:, :columns]
            value = times_transpose(rows, some) if turned else product(rows, some)
            buf[r] = value.astype(bf16)
            going.start(buf.at[r], outs[0].at[order_ref[r]] if ordered else part_at(cube, outs, r))
        going.finish()

    return call(kernel, [order, x, weight], shapes,
                [pltpu.VMEM((C, T, D), bf16), pltpu.SemaphoreType.DMA((C,))], name, (), range(len(shapes)))


def self_back(tokens, grads, weight, sums, me, cube, name):
    C = len(tokens)
    T, D = tokens[0].shape
    Z = sums.shape[0]
    DZ = D // Z
    width = weight.shape[1] // 3

    def kernel(me_ref, *refs):
        x_refs, (g_ref, w_ref, sums_ref, out_ref), outs = refs[:C], refs[C : C + 4], refs[C + 4 :]
        first = jnp.zeros((1, D), f32)
        second = jnp.zeros((1, D), f32)
        bias = jnp.zeros((1, 3 * width), f32)
        for r in range(C):
            rows = g_ref[r * T : (r + 1) * T, :]
            grad = times_transpose(rows, w_ref[...])
            store_part(cube, outs, r, grad.astype(bf16))
            scaled, _ = normalise(x_refs[r][...].astype(f32))
            first = first + jnp.sum(grad * scaled, axis=0, keepdims=True)
            second = second + jnp.sum(grad, axis=0, keepdims=True)
            bias = bias + jnp.sum(rows.astype(f32), axis=0, keepdims=True)
        lane = lax.broadcasted_iota(i32, (1, D), 1)
        spot = (lane >= me_ref[0] * width) & (lane < (me_ref[0] + 1) * width)

        def at_own(row):
            return jnp.where(spot, jnp.concatenate([row] * C, axis=1), 0.0)

        late = {0: first, 3: second, 6: at_own(bias[:, :width]), 7: at_own(bias[:, 2 * width :])}
        for z in range(Z):
            block = sums_ref[z]
            place = lax.broadcasted_iota(i32, block.shape, 0)
            for k, row in late.items():
                cut = row[:, z * DZ : (z + 1) * DZ]
                cut = jnp.concatenate([cut, jnp.zeros_like(cut)], axis=1)
                block = block + jnp.where(place == k, cut, 0.0)
            out_ref[z] = block.astype(bf16)

    shapes = [jax.ShapeDtypeStruct(sums.shape, bf16)] + parts_shapes(cube, C, T, D)
    return call(kernel, [me.reshape(1), *tokens, grads, weight, sums], shapes, [], name)


def contract_pieces(pieces, grads, name):
    C = len(pieces)
    T, D = pieces[0].shape
    N = grads.shape[1]

    def kernel(*refs):
        x_refs, (g_ref, out_ref, acc_ref) = refs[:C], refs[C:]
        for r in range(C):
            part = contract_rows(x_refs[r][...], g_ref[r * T : (r + 1) * T, :])
            if r == 0:
                acc_ref[...] = part
            else:
                acc_ref[...] += part
        out_ref[...] = acc_ref[...].astype(bf16)

    return call(kernel, [*pieces, grads], [jax.ShapeDtypeStruct((D, N), bf16)],
                [pltpu.VMEM((D, N), f32)], name)[0]


def after(x, *others):
    return lax.optimization_barrier((x, *others))[0]


def together(many, *others):
    return lax.optimization_barrier((*many, *others))[: len(many)]


def make_body(C, Z):
    cube = C == 8
    relative = [0, 2, 4, 6, 1, 3, 5, 7] if cube else list(range(C))

    def hop(x, bit):
        return lax.ppermute(x, "ctx", [(i, i ^ bit) for i in range(C)])

    def hop_diag(x):
        return lax.ppermute(x, "ctx", [(i, i ^ (4 if i & 1 else 2)) for i in range(C)])

    def gather_halves(x):
        if not cube:
            return [x, x, x], lambda hold: gather_steps(x, hold)
        odd = lax.axis_index("ctx") & 1
        own, ex, wy = hop(x, 1), hop(x, 2), hop(x, 4)

        def rest(hold):
            one, two = (ex, wy) if hold is None else together((ex, wy), hold)
            chosen = jnp.where(odd == 1, one, two)
            diag = hop_diag(chosen)
            first = [x, ex, wy, diag, own, hop(one, 1), hop(two, 1)]
            return first, chosen, lambda held: first + [hop(diag if held is None else after(diag, held), 1)]

        return [own, ex, wy], rest

    def gather_steps(x, hold):
        if not cube:
            whole = lax.all_gather(x, "ctx", axis=0, tiled=False)
            blocks = [whole[r] for r in range(C)]
            return blocks, x, lambda held: blocks
        return gather_halves(x)[1](hold)

    def gather_rows(x, hold=None):
        return gather_steps(x, hold)[2](None)

    def scatter_parts(parts):
        if not cube:
            done = lax.psum_scatter(parts[0], "ctx", scatter_dimension=0, tiled=False)
            return [done], done, done
        odd = lax.axis_index("ctx") & 1
        even, other_diag, others = parts[:4], parts[4], parts[5]
        got_diag = hop(other_diag, 1)
        got = hop(others, 1)
        second = (even[3].astype(f32) + got_diag.astype(f32)).astype(bf16)
        passed = hop_diag(second).astype(f32)
        ex = even[1].astype(f32) + got[1].astype(f32) + jnp.where(odd == 1, passed, 0.0)
        wy = even[2].astype(f32) + got[2].astype(f32) + jnp.where(odd == 1, 0.0, passed)
        third = wy.astype(bf16)
        got_x = hop(ex.astype(bf16), 2)
        got_y = hop(third, 4)
        return [even[0], got[0], got_x, got_y], second, third

    def tree_sum(blocks):
        parts = [blocks[relative.index(r)] for r in range(C)]
        while len(parts) > 1:
            parts = [parts[k] + parts[k + 1] for k in range(0, len(parts), 2)]
        return parts[0]

    def exchange(x):
        return lax.all_to_all(x, "ctx", split_axis=0, concat_axis=0, tiled=True)

    def zhop(x, d):
        return lax.ppermute(x, "fsdp", [(i, (i + d) % Z) for i in range(Z)])

    far_first = sorted(range(1, Z), key=lambda d: -min(d, Z - d))

    def zgather(x):
        got = {d: zhop(x, d) for d in far_first}
        return [x] + [got[d] for d in range(1, Z)]

    def zscatter(blocks, hold=None):
        got = lax.all_to_all(blocks, "fsdp", split_axis=0, concat_axis=0, tiled=True)
        if hold is not None:
            got = after(got, hold)
        return jnp.sum(got.astype(f32), axis=0)

    def body(
        tokens, encoded, cotangent, target_segments, source_segments, block_order,
        norm_gain, norm_shift, inward, inbias, outward, outbias, upward, upbias, downward, downbias,
    ):
        T, D = tokens.shape[1:]
        S = encoded.shape[1]
        L = C * T
        DZ = norm_gain.shape[1]
        FZ = downward.shape[0]
        FF = FZ * Z
        U = FZ // C
        width = D // C
        lanes = width % 128 == 0 and U % 128 == 0
        me = lax.axis_index("ctx")
        zi = lax.axis_index("fsdp")
        near = jnp.array(relative, i32)
        if cube:
            near = near ^ me
        zplace = (zi - jnp.arange(Z, dtype=i32)) % Z
        fixed = not cube
        steady = jnp.arange(C, dtype=i32)

        def mine(x, dims, axis):
            return lax.dynamic_index_in_dim(x.reshape(dims), me, axis, keepdims=False)

        def columns(groups, plan, shapes, dtype, name):
            if lanes:
                return spread_columns(groups, near, plan, shapes, dtype, name)
            outs = [[None] * (shape[0] if len(shape) == 3 else 1) for shape in shapes]
            for group, first, w, out, lead, base in sorted(plan, key=lambda p: p[5]):
                stacked = jnp.stack(groups[group])[:, : shapes[out][-2], first : first + w].astype(dtype)
                part = stacked.transpose(1, 0, 2).reshape(stacked.shape[1], -1)
                k = lead or 0
                outs[out][k] = part if outs[out][k] is None else jnp.concatenate([outs[out][k], part], axis=1)
            return [o[0] if len(shape) == 2 else jnp.stack(o) for o, shape in zip(outs, shapes)]

        small = jnp.concatenate(
            [norm_gain, norm_shift, inbias.reshape(4, DZ), outbias, downbias.reshape(1, DZ),
             upbias.reshape(FZ // DZ, DZ), jnp.zeros((19 - FZ // DZ, DZ), bf16)], axis=0)
        small = jnp.concatenate([small[:16], small[16:]], axis=1)
        F = Z * U
        if lanes:
            cut_a, cut_b = cut_weights(
                inward, outward, upward, downward, small, me, width, U, Z, "cut_weights")
        else:
            in_one = mine(inward[0], (DZ, 3, C, width), 2).reshape(DZ, 3 * width)
            in_two = mine(inward[1], (DZ, 3, C, width), 2).reshape(DZ, 3 * width)
            outs = mine(outward, (2, DZ, C, width), 2)
            cut_a = jnp.concatenate([in_one, outs[0], in_two[:, :width]], axis=1)
            cut_a = jnp.concatenate([cut_a, jnp.pad(small, ((0, 0), (0, 5 * width - 2 * DZ)))], axis=0)
            cut_up = mine(upward, (DZ, Z, C, U), 2).reshape(DZ, F)
            cut_down = mine(downward, (C, U, D), 0).reshape(U, D // F, F).transpose(1, 0, 2).reshape(DZ, F)
            cut_b = jnp.concatenate([in_two[:, width:], outs[1], cut_up, cut_down], axis=1)

        pieces_a = zgather(cut_a)
        token_start, token_chosen, token_join = gather_steps(after(tokens[0], cut_a), None)
        source_start, source_chosen, source_join = gather_steps(after(encoded[0], token_chosen), None)
        w_self, w_pair, vectors = assemble(
            list(together(pieces_a, token_chosen)), zplace, [3 * width, 2 * width], 16, "assemble_a")
        token_pieces = token_join(w_self)
        pair_start, pair_rest = gather_halves(w_pair)
        w_b = lax.all_gather(after(cut_b, w_self), "fsdp", axis=0, tiled=True)
        w_down = w_b[:, 3 * width + F :].reshape(Z, D // F, U, F).transpose(0, 2, 1, 3).reshape(F, D)
        w_out = w_b[:, 2 * width : 3 * width]
        gains, shifts = vectors[0:3], vectors[3:6]
        outb, downb = vectors[10:12], vectors[12]
        upb = vectors[13 : 13 + FZ // DZ].reshape(FZ // DZ, Z, DZ).transpose(1, 0, 2)
        upb = mine(upb.reshape(FF), (Z, C, U), 1).reshape(F)

        blocks = T // BLOCK
        index = jnp.arange(C * blocks, dtype=i32)
        order = block_order[0]
        by_device = order.reshape(1, C, blocks)
        near_order = jnp.sum(
            jnp.where(near[:, None, None] == jnp.arange(C, dtype=i32)[None, :, None], by_device, 0), axis=1
        ).reshape(-1)

        def inverted(table):
            return jnp.sum(jnp.where(table[None, :] == index[:, None], index[None, :], 0), axis=1)

        source_table = (near[:, None] * blocks + jnp.arange(blocks, dtype=i32)).reshape(-1)
        near_source = inverted(source_table)
        stored = inverted(order)
        near_stored = inverted(near_order)
        seg = target_segments[0]
        docs = jnp.arange(DOCS, dtype=i32)[:, None]
        own_doc = seg[None, :] == docs
        t_start = jnp.sum((seg[None, :] < docs).astype(i32), axis=1)
        s_start = jnp.sum((source_segments[0][None, :] < docs).astype(i32), axis=1)
        s_end = jnp.sum((source_segments[0][None, :] <= docs).astype(i32), axis=1)

        def per_row(table):
            return jnp.sum(jnp.where(own_doc, table[:, None], 0), axis=0).reshape(L // QB, QB)

        self_low = per_row(t_start)
        self_high = jnp.arange(1, L + 1, dtype=i32).reshape(L // QB, QB)
        cross_low, cross_high = per_row(s_start), per_row(s_end)
        self_first = self_low[:, 0] // BLOCK
        self_last = self_high[:, -1] // BLOCK
        cross_first = cross_low[:, 0] // BLOCK
        cross_last = (cross_high[:, -1] + BLOCK - 1) // BLOCK

        q1, k1, v1, normed_one = project(
            token_pieces, after(w_self, source_chosen, pair_start[0]), 0, vectors, [6, None, 7], me, (0, 3),
            near_order, [width] * 3, [False, True, True], "project_self")
        source_pieces = source_join(None)
        mixed1, wide1, inv1 = attend(
            (self_first, self_last, index, stored), after(q1, source_start[3]), k1, v1, self_low, self_high,
            "attend_self")
        pair = pair_rest(q1)[2](mixed1)
        cot = lax.all_gather(after(cotangent[0], q1), "ctx", axis=0, tiled=False)
        mixed_one = exchange(mixed1.reshape(C, T, width))

        after_self, kept_self, q2_own = mix(
            mixed_one, pair, near, fixed, tokens[0],
            jnp.stack([outb[0], gains[1], shifts[1], vectors[8]]), 0, width, True, "mix_self")
        q2 = exchange(q2_own).reshape(L, width)
        k2, v2 = project(
            source_pieces, after(w_b, q2_own), 0, vectors, [None, 9], me, None, source_table,
            [width] * 2, [True, True], "project_cross")
        mixed2, wide2, inv2 = attend(
            (cross_first, cross_last, stored, stored), q2, k2, v2, cross_low, cross_high,
            "attend_cross")
        kept_self = lax.all_gather(kept_self, "ctx", axis=0, tiled=True)
        out_two = gather_rows(after(w_out, q2_own), mixed2)
        mixed_two = exchange(mixed2.reshape(C, T, width))
        after_cross, kept_cross, normed_three = mix(
            mixed_two, out_two, near, fixed, after_self,
            jnp.stack([outb[1], gains[2], shifts[2]]), 0, width, False, "mix_cross")

        kept_cross = lax.all_gather(after(kept_cross, kept_self), "ctx", axis=0, tiled=True)

        n3 = gather_rows(normed_three)
        hidden, up_grad, upb_tp, *parts = feed(
            n3, cot, near, fixed, w_b, 3 * width, w_down, upb[None], cube, "feed")
        back_three, second, third = scatter_parts(parts)
        feed_dw = feed_weights(
            n3, cot, near, fixed, hidden, after(up_grad, third), Z, "feed_weights")
        feed_sum = lax.psum_scatter(feed_dw, "fsdp", scatter_dimension=0, tiled=False)


        cross_grad, m2_own, sums_three = unmix(
            back_three, None, None, out_two, near, fixed, (0, 0), after(cotangent[0], feed_dw), after_cross,
            gains[2:3], width, "unmix_cross")
        m2 = exchange(m2_own).reshape(L, 2 * width)
        out_parts = times_weight(
            hidden, after(w_down, m2_own), D, False, near, False, cube, C, "feed_out")
        out_terms, out_second, out_third = scatter_parts(out_parts)
        dq2, dkv2 = attend_back(
            (cross_first, cross_last, stored, stored, stored, near_source),
            q2, k2, v2, cross_low, cross_high, after(m2, out_parts[0]), wide2, inv2, False, "attend_cross_back")
        layer_out = (after_cross + (sum(t.astype(f32) for t in out_terms) + downb)).astype(bf16)
        dq2_own = exchange(dq2.reshape(C, T, width))
        (source_part,) = times_weight(dkv2, w_b, 2 * width, True, near, True, cube, C, "source_back")
        encoded_grad = lax.psum_scatter(source_part, "ctx", scatter_dimension=0, tiled=False).astype(f32)
        self_grad, m1_own, sums_two = unmix(
            [], dq2_own, pair, pair, near, fixed, (width, 0), after(cross_grad, source_part, out_third), after_self,
            gains[1:2], width, "unmix_self")


        m1 = exchange(m1_own).reshape(L, 2 * width)
        group_one = jnp.concatenate([
            contract_rows(kept_self[:, D:], after(dq2, m1_own)).astype(bf16),
            contract_rows(kept_cross, after(m2, m1_own)[:, width:]).astype(bf16),
            contract_pieces(source_pieces, after(dkv2, m1_own), "source_weights"),
        ], axis=1).reshape(Z, DZ, 4 * width)
        feed_all = lax.all_gather(after(feed_sum, m1_own), "ctx", axis=0, tiled=False)
        m1 = after(m1, group_one)
        group_one = zscatter(group_one).astype(bf16)
        (dqkv,) = attend_back(
            (self_first, self_last, index, stored, near_stored, near_stored),
            q1, k1, v1, self_low, self_high, m1, wide1, inv1, True, "attend_self_back")
        def placed(part, count):
            part = part.reshape(count, 1, -1)
            spot = lax.broadcasted_iota(i32, (count, C, part.shape[2]), 1) == me
            return jnp.where(spot, part, 0.0)

        dkv2_sum = placed(jnp.sum(dkv2[:, width:].astype(f32), axis=0), 1).reshape(D)
        upb_rows = placed(upb_tp, Z).reshape(Z, FZ // DZ, DZ)
        none = jnp.zeros((D,), f32)
        sums = jnp.stack([
            none, sums_two[0], sums_three[0], none, sums_two[1], sums_three[1],
            none, none, sums_two[3], dkv2_sum, sums_two[2], sums_three[2], sums_three[3],
        ])
        count = 13 + FZ // DZ
        sums = jnp.concatenate([
            sums.reshape(13, Z, DZ).transpose(1, 0, 2), upb_rows, jnp.zeros((Z, 32 - count, DZ), f32)], axis=1)
        sums = jnp.concatenate([sums[:, :16], sums[:, 16:]], axis=2)
        sums, *parts_one = self_back(
            token_pieces, dqkv, w_self, after(sums, m1), me, cube, "self_back")
        back_one, _, back_third = scatter_parts(parts_one)
        group_two = jnp.concatenate([
            contract_rows(kept_self[:, :D], m1[:, width:]).astype(bf16),
            contract_rows(normed_one, after(dqkv, encoded_grad)).astype(bf16),
        ], axis=1)
        group_two = jnp.concatenate([group_two.reshape(Z, DZ, 4 * width), sums], axis=1)
        group_two = zscatter(after(group_two, group_one), back_third).astype(bf16)
        one_start, one_chosen, one_join = gather_steps(after(group_one, parts_one[0]), back_third)
        group_one = one_join(None)
        upward_grad, down_grad = feed_outputs(after(feed_all, back_third), Z, D, "feed_outputs")
        tokens_grad, _ = unmix(
            back_one, None, None, None, near, fixed, (0, 0),
            after(self_grad, upward_grad, one_chosen, group_two), tokens[0], gains[0:1], width, "unmix_tokens")
        group_two = gather_rows(after(group_two, tokens_grad))
        part = tree_sum([g[DZ:].astype(f32) for g in group_two])
        part = jnp.concatenate([part[:, :DZ], part[:, DZ:]], axis=0)[:count]

        inward_grad, outward_grad = columns(
            [group_one, group_two],
            [(1, (k + 1) * width, width, 0, 0, k * D) for k in range(3)]
            + [(0, 0, width, 0, 1, 0)]
            + [(0, (k + 2) * width, width, 0, 1, (k + 1) * D) for k in range(2)]
            + [(1, 0, width, 1, 0, 0), (0, width, width, 1, 1, 0)],
            [(2, DZ, 3 * D), (2, DZ, D)], f32, "spread_rest")

        return (
            layer_out[None], tokens_grad[None], encoded_grad[None],
            part[0:3], part[3:6], inward_grad, part[6:10].reshape(2, 2, DZ), outward_grad,
            part[10:12], upward_grad, part[13:].reshape(FZ), down_grad, part[12],
        )

    return body


def solution(mesh):
    rows = P("fsdp", "ctx", None)
    placed = (
        rows, rows, rows, P("fsdp", None), P("fsdp", None), P("fsdp", None),
        P(None, "fsdp"), P(None, "fsdp"), P(None, "fsdp", None), P(None, None, "fsdp"),
        P(None, "fsdp", None), P(None, "fsdp"), P("fsdp", None), P("fsdp"), P("fsdp", None), P("fsdp"),
    )
    return jax.shard_map(
        make_body(mesh.shape["ctx"], mesh.shape["fsdp"]),
        mesh=mesh,
        in_specs=placed,
        out_specs=(
            rows, rows, rows, P(None, "fsdp"), P(None, "fsdp"), P(None, "fsdp", None),
            P(None, None, "fsdp"), P(None, "fsdp", None), P(None, "fsdp"), P("fsdp", None),
            P("fsdp"), P("fsdp", None), P("fsdp"),
        ),
        check_vma=False,
    )
```

```python
import jax
import jax.numpy as jnp
from jax import lax
from jax.experimental import pallas as pl
from jax.experimental.pallas import tpu as pltpu
from jax.sharding import PartitionSpec as P

HEADS = 16
HEAD_DIM = 64
BLOCK = 128
DOCS = 16
QB = 256
KB = 256

epsilon = 1e-05
f32 = jnp.float32
bf16 = jnp.bfloat16
i32 = jnp.int32
VMEM_BYTES = 56 << 20
TIMES = {
    "cut_weights": 20, "assemble_a": 20, "project_self": 90, "attend_self": 100, "project_cross": 5, "attend_cross": 11,
    "mix_self": 5, "mix_cross": 4, "feed": 16, "feed_weights": 11, "feed_out": 5, "unmix_cross": 5, "unmix_self": 6,
    "attend_cross_back": 15, "attend_self_back": 14, "source_back": 5, "source_weights": 5, "self_back": 8,
    "unmix_tokens": 4, "feed_outputs": 6, "spread_rest": 6,
}


def cost(name):
    return pl.CostEstimate(
        flops=int(1.1e9 * TIMES.get(name, 4)), transcendentals=0, bytes_accessed=int(3.5e6 * TIMES.get(name, 4)))


def product(left, right):
    return jnp.dot(left, right, preferred_element_type=f32)


def contract_rows(left, right):
    return lax.dot_general(left, right, (((0,), (0,)), ((), ())), preferred_element_type=f32)


def times_transpose(left, right):
    return lax.dot_general(left, right, (((1,), (1,)), ((), ())), preferred_element_type=f32)


def normalise(values):
    centre = jnp.mean(values, axis=-1, keepdims=True)
    centred = values - centre
    inverse = lax.rsqrt(jnp.mean(centred * centred, axis=-1, keepdims=True) + epsilon)
    return centred * inverse, inverse


def norm_backward(upstream, scaled, inverse, gain_row):
    weighted = upstream * gain_row
    first_mean = jnp.mean(weighted, axis=-1, keepdims=True)
    second_mean = jnp.mean(weighted * scaled, axis=-1, keepdims=True)
    return inverse * (weighted - first_mean - scaled * second_mean)


def vmem():
    return pl.BlockSpec(memory_space=pltpu.VMEM)


def smem():
    return pl.BlockSpec(memory_space=pltpu.SMEM)


def project(pieces, weight, first, vectors, biases, me, norm, table, widths, padded, name):
    counts = [p.shape[0] for p in pieces]
    rows = sum(counts)
    depth = weight.shape[0]
    extra = [BLOCK if pad else 0 for pad in padded]
    n_in = len(pieces)
    total = sum(widths)
    aligned = widths[0] % 128 == 0
    if not aligned:
        own = [
            jnp.zeros((w,), f32) if b is None else lax.dynamic_slice_in_dim(vectors[b], me * w, w)
            for b, w in zip(biases, widths)
        ]
        own = jnp.concatenate(own)[None]

    def kernel(*refs):
        table_ref, me_ref = refs[:2]
        x_refs = refs[2 : 2 + n_in]
        w_ref, v_ref = refs[2 + n_in], refs[3 + n_in]
        at = 4 + n_in
        if not aligned:
            own_ref = refs[at]
            at += 1
        outs = refs[at : at + len(widths)]
        if norm:
            normed_ref = refs[at + len(widths)]
        bias = []
        left = 0
        for b, w in zip(biases, widths):
            if not aligned:
                bias.append(own_ref[0:1, left : left + w])
            elif b is not None:
                bias.append(v_ref[b : b + 1, pl.ds(pl.multiple_of(me_ref[0] * w, 128), w)])
            else:
                bias.append(None)
            left += w
        base = 0
        for x_ref, count in zip(x_refs, counts):
            step = min(count, 256)
            for sub in range(0, count, step):
                x = x_ref[sub : sub + step, :depth]
                if norm:
                    scaled, _ = normalise(x.astype(f32))
                    x = (scaled * v_ref[norm[0] : norm[0] + 1, :] + v_ref[norm[1] : norm[1] + 1, :]).astype(bf16)
                    normed_ref[base + sub : base + sub + step, :] = x
                y = product(x, w_ref[:, first : first + total])
                left = 0
                for out, width, row in zip(outs, widths, bias):
                    cut = y[:, left : left + width]
                    cut = (cut if row is None else cut + row).astype(bf16)
                    for part in range(0, step, BLOCK):
                        place = pl.multiple_of(table_ref[(base + sub + part) // BLOCK] * BLOCK, BLOCK)
                        out[pl.ds(place, BLOCK), :] = cut[part : part + BLOCK, :]
                    left += width
            base += count
        for out, width, more in zip(outs, widths, extra):
            if more:
                out[rows : rows + more, :] = jnp.zeros((more, width), bf16)

    out_shape = [jax.ShapeDtypeStruct((rows + more, width), bf16) for width, more in zip(widths, extra)]
    if norm:
        out_shape.append(jax.ShapeDtypeStruct((rows, depth), bf16))
    args = [table, me.reshape(1), *pieces, weight, vectors] + ([] if aligned else [own])
    return call(kernel, args, out_shape, [], name)


def split_rows(rows, heads):
    if heads == 1:
        return rows
    lane = lax.broadcasted_iota(i32, rows.shape, 1)
    zero = jnp.zeros_like(rows)
    parts = [
        jnp.where((lane >= h * HEAD_DIM) & (lane < (h + 1) * HEAD_DIM), rows, zero)
        for h in range(heads)
    ]
    return jnp.concatenate(parts, axis=0)


def own_rows(stacked, heads):
    if heads == 1:
        return stacked
    width = stacked.shape[1] // heads
    return jnp.concatenate(
        [
            stacked[h * HEAD_DIM : (h + 1) * HEAD_DIM, h * width : (h + 1) * width]
            for h in range(heads)
        ],
        axis=0,
    )


def load_blocks(ref, table_ref, block):
    parts = []
    for k in range(QB // BLOCK):
        place = pl.multiple_of(table_ref[block * (QB // BLOCK) + k] * BLOCK, BLOCK)
        parts.append(ref[pl.ds(place, BLOCK), :])
    return jnp.concatenate(parts, axis=0)


def store_blocks(ref, table_ref, block, values, left):
    width = values.shape[1]
    for k in range(QB // BLOCK):
        place = pl.multiple_of(table_ref[block * (QB // BLOCK) + k] * BLOCK, BLOCK)
        ref[pl.ds(place, BLOCK), left : left + width] = values[k * BLOCK : (k + 1) * BLOCK, :]


def key_weights(keys, query_rows, low, high, start, heads):
    scores = times_transpose(keys, query_rows)
    place = start + lax.broadcasted_iota(i32, (KB, QB), 0)
    allowed = (place >= low) & (place < high)
    parts = [
        jnp.where(allowed, jnp.exp(scores[:, h * QB : (h + 1) * QB]), 0.0) for h in range(heads)
    ]
    return jnp.concatenate(parts, axis=1) if heads > 1 else parts[0]


def attend(tables, query, keys, values, low, high, name):
    first, last, query_table, out_table = tables
    rows, width = query.shape
    heads = width // HEAD_DIM
    key_rows = keys.shape[0]
    tall = width + 16

    def kernel(
        first_ref, last_ref, qt_ref, ot_ref, q_ref, k_ref, v_ref, lo_ref, hi_ref,
        mixed_ref, wide_ref, inv_ref, vt_ref, acc_ref,
    ):
        for c in range(0, key_rows, BLOCK):
            vt_ref[0:width, c : c + BLOCK] = v_ref[c : c + BLOCK, :].T
        vt_ref[width:tall, :] = jnp.ones((16, key_rows), bf16)

        def one(i, carry):
            q = split_rows(load_blocks(q_ref, qt_ref, i) * jnp.asarray(HEAD_DIM ** (-0.5), bf16), heads)
            lo = lo_ref[pl.ds(i, 1), :]
            hi = hi_ref[pl.ds(i, 1), :]
            acc_ref[...] = jnp.zeros_like(acc_ref)
            begin = first_ref[i]

            def step(j, c):
                start = pl.multiple_of((begin + j * (KB // BLOCK)) * BLOCK, BLOCK)
                w = key_weights(k_ref[pl.ds(start, KB), :], q, lo, hi, start, heads)
                acc_ref[...] += product(vt_ref[:, pl.ds(start, KB)], w.astype(bf16))
                return c

            lax.fori_loop(0, (last_ref[i] - begin + KB // BLOCK - 1) // (KB // BLOCK), step, 0)
            acc = acc_ref[...]
            inverse = 1.0 / acc[width : width + 1, :]
            mixed = own_rows(acc[0:width, :] * inverse, heads).T
            inv = own_rows(jnp.broadcast_to(inverse, (width, heads * QB)), heads).T
            wide_ref[pl.ds(pl.multiple_of(i * QB, QB), QB), :] = mixed
            inv_ref[pl.ds(pl.multiple_of(i * QB, QB), QB), :] = inv
            store_blocks(mixed_ref, ot_ref, i, mixed.astype(bf16), 0)
            return carry

        lax.fori_loop(0, rows // QB, one, 0)

    return pl.pallas_call(
        kernel,
        out_shape=[
            jax.ShapeDtypeStruct((rows, width), bf16),
            jax.ShapeDtypeStruct((rows, width), f32),
            jax.ShapeDtypeStruct((rows, width), f32),
        ],
        in_specs=[smem()] * 4 + [vmem()] * 5,
        out_specs=[vmem()] * 3,
        scratch_shapes=[pltpu.VMEM((tall, key_rows), bf16), pltpu.VMEM((tall, heads * QB), f32)],
        compiler_params=pltpu.CompilerParams(vmem_limit_bytes=VMEM_BYTES),
        cost_estimate=cost(name),
        name=name,
    )(first, last, query_table, out_table, query, keys, values, low, high)


def attend_back(tables, query, keys, values, low, high, upstream, wide, inverse, joined, name):
    first, last, query_table, up_table, dq_table, dk_table = tables
    rows, width = query.shape
    heads = width // HEAD_DIM
    key_rows = keys.shape[0]
    held = key_rows - BLOCK
    scale = HEAD_DIM ** (-0.5)

    def kernel(
        first_ref, last_ref, qt_ref, ut_ref, dqt_ref, dkt_ref,
        q_ref, k_ref, v_ref, lo_ref, hi_ref, up_ref, wide_ref, inv_ref, *rest,
    ):
        if joined:
            dq_ref, kt_ref, dk_acc, dv_acc, dq_acc = rest
            dkv_ref = dq_ref
            left = width
        else:
            dq_ref, dkv_ref, kt_ref, dk_acc, dv_acc, dq_acc = rest
            left = 0
        for c in range(0, key_rows, BLOCK):
            kt_ref[:, c : c + BLOCK] = k_ref[c : c + BLOCK, :].T
        dk_acc[...] = jnp.zeros_like(dk_acc)
        dv_acc[...] = jnp.zeros_like(dv_acc)

        def one(i, carry):
            here = pl.ds(pl.multiple_of(i * QB, QB), QB)
            q = split_rows(load_blocks(q_ref, qt_ref, i) * jnp.asarray(scale, bf16), heads)
            shared = load_blocks(up_ref, ut_ref, i)[:, :width].astype(f32) * inv_ref[here, :]
            total = -(shared * wide_ref[here, :]).T
            total = [
                jnp.sum(total[h * HEAD_DIM : (h + 1) * HEAD_DIM, :], axis=0, keepdims=True)
                for h in range(heads)
            ]
            total = jnp.concatenate(total, axis=1) if heads > 1 else total[0]
            shared = split_rows(shared.astype(bf16), heads)
            lo = lo_ref[pl.ds(i, 1), :]
            hi = hi_ref[pl.ds(i, 1), :]
            dq_acc[...] = jnp.zeros_like(dq_acc)
            begin = first_ref[i]

            def step(j, c):
                start = pl.multiple_of((begin + j * (KB // BLOCK)) * BLOCK, BLOCK)
                some = pl.ds(start, KB)
                w = key_weights(k_ref[some, :], q, lo, hi, start, heads)
                grad = times_transpose(v_ref[some, :], shared)
                ds = (w * (grad + total)).astype(bf16)
                dv_acc[some, :] += product(w.astype(bf16), shared)
                dk_acc[some, :] += product(ds, q)
                dq_acc[...] += product(kt_ref[:, some], ds)
                return c

            lax.fori_loop(0, (last_ref[i] - begin + KB // BLOCK - 1) // (KB // BLOCK), step, 0)
            dq = own_rows(dq_acc[...] * scale, heads).T.astype(bf16)
            store_blocks(dq_ref, dqt_ref, i, dq, 0)
            return carry

        lax.fori_loop(0, rows // QB, one, 0)

        def flush(b, carry):
            here = pl.ds(pl.multiple_of(b * BLOCK, BLOCK), BLOCK)
            there = pl.ds(pl.multiple_of(dkt_ref[b] * BLOCK, BLOCK), BLOCK)
            dkv_ref[there, left : left + width] = dk_acc[here, :].astype(bf16)
            dkv_ref[there, left + width : left + 2 * width] = dv_acc[here, :].astype(bf16)
            return carry

        lax.fori_loop(0, held // BLOCK, flush, 0)

    if joined:
        out_shape = [jax.ShapeDtypeStruct((rows, 3 * width), bf16)]
    else:
        out_shape = [
            jax.ShapeDtypeStruct((rows, width), bf16),
            jax.ShapeDtypeStruct((held, 2 * width), bf16),
        ]
    return pl.pallas_call(
        kernel,
        out_shape=out_shape,
        in_specs=[smem()] * 6 + [vmem()] * 8,
        out_specs=[vmem()] * len(out_shape),
        scratch_shapes=[
            pltpu.VMEM((width, key_rows), bf16),
            pltpu.VMEM((key_rows, width), f32),
            pltpu.VMEM((key_rows, width), f32),
            pltpu.VMEM((width, heads * QB), f32),
        ],
        compiler_params=pltpu.CompilerParams(vmem_limit_bytes=VMEM_BYTES),
        cost_estimate=cost(name),
        name=name,
    )(first, last, query_table, up_table, dq_table, dk_table,
      query, keys, values, low, high, upstream, wide, inverse)


def cut_weights(inward, outward, upward, downward, small, me, width, units, parts, name):
    depth, D = outward.shape[1:]
    stride = upward.shape[1] // parts

    F = parts * units
    tall, wide = small.shape

    def kernel(me_ref, small_ref, in_ref, out_ref, up_ref, down_ref, a_ref, b_ref, sems):
        at = pl.multiple_of(me_ref[0] * width, 128)
        unit = pl.multiple_of(me_ref[0] * units, 128)
        plan = []
        for k in range(3):
            plan.append((in_ref.at[0, :, pl.ds(k * D + at, width)], a_ref.at[0:depth, pl.ds(k * width, width)]))
        plan.append((out_ref.at[0, :, pl.ds(at, width)], a_ref.at[0:depth, pl.ds(3 * width, width)]))
        plan.append((in_ref.at[1, :, pl.ds(at, width)], a_ref.at[0:depth, pl.ds(4 * width, width)]))
        for k in range(2):
            plan.append((in_ref.at[1, :, pl.ds((k + 1) * D + at, width)], b_ref.at[:, pl.ds(k * width, width)]))
        plan.append((out_ref.at[1, :, pl.ds(at, width)], b_ref.at[:, pl.ds(2 * width, width)]))
        for k in range(parts):
            plan.append((up_ref.at[:, pl.ds(k * stride + unit, units)],
                         b_ref.at[:, pl.ds(3 * width + k * units, units)]))
        for q in range(D // F):
            plan.append((down_ref.at[pl.ds(unit, units), q * F : (q + 1) * F],
                         b_ref.at[q * units : (q + 1) * units, pl.ds(3 * width + F, F)]))
        copies = [pltpu.make_async_copy(src, dst, sems.at[k]) for k, (src, dst) in enumerate(plan)]
        for c in copies:
            c.start()
        a_ref[depth : depth + tall, 0:wide] = small_ref[...]
        a_ref[depth : depth + tall, wide : 5 * width] = jnp.zeros((tall, 5 * width - wide), bf16)
        for c in copies:
            c.wait()

    return pl.pallas_call(
        kernel,
        out_shape=[
            jax.ShapeDtypeStruct((depth + tall, 5 * width), bf16),
            jax.ShapeDtypeStruct((depth, 3 * width + 2 * F), bf16),
        ],
        in_specs=[smem(), vmem()] + [pl.BlockSpec(memory_space=pl.ANY)] * 4,
        out_specs=[vmem()] * 2,
        scratch_shapes=[pltpu.SemaphoreType.DMA((8 + parts + D // F,))],
        compiler_params=pltpu.CompilerParams(vmem_limit_bytes=VMEM_BYTES),
        cost_estimate=cost(name),
        name=name,
    )(me.reshape(1), small, inward, outward, upward, downward)


def assemble(pieces, places, widths, tall, name):
    depth = pieces[0].shape[0] - tall
    count = len(pieces)

    def kernel(*refs):
        place_ref, parts, outs = refs[0], refs[1 : 1 + count], refs[1 + count :]
        for d, part in enumerate(parts):
            at = pl.multiple_of(place_ref[d] * depth, depth)
            left = 0
            for out, width in zip(outs, widths):
                out[pl.ds(at, depth), :] = part[0:depth, left : left + width]
                left += width
            for k in range(2):
                outs[-1][k * tall : (k + 1) * tall, pl.ds(at, depth)] = part[
                    depth : depth + tall, k * depth : (k + 1) * depth].astype(f32)

    shapes = [jax.ShapeDtypeStruct((count * depth, w), bf16) for w in widths]
    shapes.append(jax.ShapeDtypeStruct((2 * tall, count * depth), f32))
    return call(kernel, [places, *pieces], shapes, [], name)


def spread_columns(pieces, near, plan, shapes, dtype, name):
    counts = [len(group) for group in pieces]
    flat = [p for group in pieces for p in group]
    slabs = []
    for item in plan:
        if item[3:5] not in slabs:
            slabs.append(item[3:5])

    def kernel(*refs):
        near_ref, parts = refs[0], refs[1 : 1 + len(flat)]
        outs = refs[1 + len(flat) : 1 + len(flat) + len(shapes)]
        bufs, sems = refs[1 + len(flat) + len(shapes) : -1], refs[-1]
        going = Copies(sems)
        for slab in slabs:
            for group, first, width, out, lead, base in plan:
                if (out, lead) != slab:
                    continue
                skip = sum(counts[:group])
                for r in range(near.shape[0]):
                    there = pl.ds(pl.multiple_of(base + near_ref[r] * width, 128), width)
                    value = parts[skip + r][: shapes[out][-2], first : first + width].astype(dtype)
                    if lead is None:
                        bufs[out][:, there] = value
                    else:
                        bufs[out][lead, :, there] = value
            out, lead = slab
            if lead is None:
                going.start(bufs[out], outs[out])
            else:
                going.start(bufs[out].at[lead], outs[out].at[lead])
        going.finish()

    return call(kernel, [near, *flat], [jax.ShapeDtypeStruct(shape, dtype) for shape in shapes],
                [pltpu.VMEM(shape, dtype) for shape in shapes] + [pltpu.SemaphoreType.DMA((len(slabs),))],
                name, (), range(len(shapes)))


def call(kernel, args, out_shape, scratch, name, far_args=(), far_outs=()):
    def spec(k, a, far):
        if k in far:
            return pl.BlockSpec(memory_space=pl.ANY)
        return smem() if a.ndim == 1 and a.dtype == i32 else vmem()

    return pl.pallas_call(
        kernel,
        out_shape=out_shape,
        in_specs=[spec(k, a, far_args) for k, a in enumerate(args)],
        out_specs=[pl.BlockSpec(memory_space=pl.ANY) if k in far_outs else vmem() for k in range(len(out_shape))],
        scratch_shapes=scratch,
        compiler_params=pltpu.CompilerParams(vmem_limit_bytes=VMEM_BYTES),
        cost_estimate=cost(name),
        name=name,
    )(*args)


class Copies:
    def __init__(self, sems):
        self.sems, self.used, self.open = sems, 0, []

    def start(self, source, target):
        copy = pltpu.make_async_copy(source, target, self.sems.at[self.used])
        copy.start()
        self.used += 1
        self.open.append(copy)
        return copy

    def finish(self):
        for copy in self.open:
            copy.wait()


def columns_at(order_ref, fixed, r, width):
    if fixed:
        return pl.ds(r * width, width)
    return pl.ds(pl.multiple_of(order_ref[r] * width, 128), width)


def block_at(order_ref, fixed, r):
    return r if fixed else order_ref[r]


def mix(received, pieces, order, fixed, residual, rows, first, width, query, name):
    C, T = received.shape[:2]
    D = residual.shape[1]
    stacked = len(pieces) == 1

    def kernel(*refs):
        order_ref, rec_ref = refs[:2]
        parts = refs[2 : 2 + len(pieces)]
        res_ref, rows_ref, after_ref, kept_ref, last_ref, y_ref = refs[2 + len(pieces) :]

        def weights(r, left):
            part = parts[0].at[r] if stacked else parts[r]
            return part[:, left : left + width]

        def pairs(x, left):
            for r in range(0, C, 2):
                both = product(x, jnp.concatenate([weights(r, left), weights(r + 1, left)], axis=1))
                yield r, both[:, :width]
                yield r + 1, both[:, width:]

        mixed = jnp.concatenate([rec_ref[c] for c in range(C)], axis=1)
        kept_ref[:, 0:D] = mixed
        for r, value in pairs(mixed, first):
            y_ref[:, columns_at(order_ref, fixed, r, width)] = value
        values = res_ref[...].astype(f32) + (y_ref[...] + rows_ref[0:1, :])
        after_ref[...] = values
        scaled, _ = normalise(values)
        normed = (scaled * rows_ref[1:2, :] + rows_ref[2:3, :]).astype(bf16)
        if not query:
            last_ref[...] = normed
        else:
            kept_ref[:, D : 2 * D] = normed
            for r, value in pairs(normed, first + width):
                bias = rows_ref[3:4, columns_at(order_ref, fixed, r, width)]
                last_ref[block_at(order_ref, fixed, r)] = (value + bias).astype(bf16)

    shapes = [
        jax.ShapeDtypeStruct((T, D), f32),
        jax.ShapeDtypeStruct((T, 2 * D if query else D), bf16),
        jax.ShapeDtypeStruct((C, T, width) if query else (T, D), bf16),
    ]
    return call(kernel, [order, received, *pieces, residual, rows], shapes,
                [pltpu.VMEM((T, D), f32)], name)


def unmix(grads, query_grads, query_pieces, pieces, order, fixed, firsts, upstream, values, gain, width, name):
    T, D = upstream.shape
    C = D // width
    joined = query_pieces is pieces and pieces is not None
    lists = [list(grads)]
    lists.append([query_grads] if query_grads is not None else [])
    lists.append(list(query_pieces) if query_pieces is not None and not joined else [])
    lists.append(list(pieces) if pieces is not None else [])
    flat = [a for part in lists for a in part]
    low_out = pieces is not None

    def kernel(*refs):
        order_ref = refs[0]
        at = 1
        got = []
        for part in lists:
            got.append(refs[at : at + len(part)])
            at += len(part)
        up_ref, val_ref, gain_ref = refs[at : at + 3]
        at += 3
        if low_out:
            grad_ref, m_ref, sums_ref = refs[at : at + 3]
        else:
            grad_ref, sums_ref = refs[at : at + 2]
        ws = got[3]
        qs = ws if joined else got[2]

        def weights(parts, r, left):
            part = parts[0].at[r] if len(parts) == 1 else parts[r]
            return part[:, left : left + width]

        def back(columns, parts, left):
            total = None
            for r in range(0, C, 2):
                cols = jnp.concatenate([columns(r), columns(r + 1)], axis=1)
                both = jnp.concatenate([weights(parts, r, left), weights(parts, r + 1, left)], axis=1)
                part = times_transpose(cols, both)
                total = part if total is None else total + part
            return total

        sums_ref[...] = jnp.zeros_like(sums_ref)
        if query_grads is not None:
            dq_ref = got[1][0]
            grad = back(lambda r: dq_ref[block_at(order_ref, fixed, r)], qs, firsts[0])
            for c in range(C):
                sums_ref[3:4, c * width : (c + 1) * width] = jnp.sum(
                    dq_ref[c].astype(f32), axis=0, keepdims=True)
        else:
            grad = got[0][0][...].astype(f32)
            for g in got[0][1:]:
                grad = grad + g[...].astype(f32)
        scaled, inverse = normalise(val_ref[...].astype(f32))
        sums_ref[0:1, :] = jnp.sum(grad * scaled, axis=0, keepdims=True)
        sums_ref[1:2, :] = jnp.sum(grad, axis=0, keepdims=True)
        upstream_values = up_ref[...].astype(f32)
        if query_grads is None:
            sums_ref[3:4, :] = jnp.sum(upstream_values, axis=0, keepdims=True)
        result = upstream_values + norm_backward(grad, scaled, inverse, gain_ref[...])
        grad_ref[...] = result
        if low_out:
            low = result.astype(bf16)
            for c in range(C):
                m_ref[c, :, width : 2 * width] = low[:, c * width : (c + 1) * width]
            sums_ref[2:3, :] = jnp.sum(low.astype(f32), axis=0, keepdims=True)
            m = back(lambda r: m_ref[block_at(order_ref, fixed, r), :, width : 2 * width], ws, firsts[1])
            for c in range(C):
                m_ref[c, :, 0:width] = m[:, c * width : (c + 1) * width].astype(bf16)

    shapes = [jax.ShapeDtypeStruct((T, D), f32)]
    if low_out:
        shapes.append(jax.ShapeDtypeStruct((C, T, 2 * width), bf16))
    shapes.append(jax.ShapeDtypeStruct((8, D), f32))
    return call(kernel, [order, *flat, upstream, values, gain], shapes, [], name)


def parts_shapes(cube, C, T, D):
    if cube:
        return [jax.ShapeDtypeStruct((T, D), bf16)] * 5 + [jax.ShapeDtypeStruct((3, T, D), bf16)]
    return [jax.ShapeDtypeStruct((C, T, D), bf16)]


def store_part(cube, refs, r, value):
    if not cube:
        refs[0][r] = value
    elif r < 4:
        refs[r][...] = value
    elif r == 7:
        refs[4][...] = value
    else:
        refs[5][r - 4] = value


def part_at(cube, refs, r):
    if not cube:
        return refs[0].at[r]
    if r < 4:
        return refs[r]
    return refs[4] if r == 7 else refs[5].at[r - 4]


ROOT = 0.7978845608028654


def feed(normed, cotangent, order, fixed, up, first, down, up_bias, cube, name):
    C = len(normed)
    T, D = normed[0].shape
    F = down.shape[0]

    def kernel(*refs):
        order_ref = refs[0]
        n_refs = refs[1 : 1 + C]
        cot_ref, up_ref, down_ref, bias_ref = refs[1 + C : 5 + C]
        hidden_ref, grad_ref, sum_ref = refs[5 + C : 8 + C]
        part_refs = refs[8 + C :]
        total = jnp.zeros((1, F), f32)
        for g in range(0, C, 4):
            group = range(g, g + 4)
            rows = slice(g * T, (g + 4) * T)
            normed_rows = jnp.concatenate([n_refs[r][...] for r in group], axis=0)
            pre = product(normed_rows, up_ref[:, first : first + F]) + bias_ref[...]
            square = pre * pre
            inner = jnp.tanh(ROOT * pre * (1.0 + 0.044715 * square))
            half = 0.5 * (1.0 + inner)
            hidden_ref[rows, :] = (pre * half).astype(bf16)
            slope = half + 0.5 * pre * (1.0 - inner * inner) * (ROOT * (1.0 + 3 * 0.044715 * square))
            cot = jnp.concatenate([cot_ref[block_at(order_ref, fixed, r)] for r in group], axis=0)
            low = (times_transpose(cot, down_ref[...]) * slope).astype(bf16)
            grad_ref[rows, :] = low
            total = total + jnp.sum(low.astype(f32), axis=0, keepdims=True)
            back = times_transpose(low, up_ref[:, first : first + F]).astype(bf16)
            for k, r in enumerate(group):
                store_part(cube, part_refs, r, back[k * T : (k + 1) * T, :])
        sum_ref[...] = total

    shapes = [
        jax.ShapeDtypeStruct((C * T, F), bf16),
        jax.ShapeDtypeStruct((C * T, F), bf16),
        jax.ShapeDtypeStruct((1, F), f32),
    ] + parts_shapes(cube, C, T, D)
    return call(kernel, [order, *normed, cotangent, up, down, up_bias], shapes, [], name)


def feed_weights(normed, cotangent, order, fixed, hidden, up_grad, parts, name):
    C = len(normed)
    T, D = normed[0].shape
    F = hidden.shape[1]
    depth, units = D // parts, F // parts

    def kernel(*refs):
        order_ref = refs[0]
        n_refs = refs[1 : 1 + C]
        cot_ref, hid_ref, grad_ref, out_ref, up_acc, down_acc = refs[1 + C :]
        for r in range(C):
            rows = slice(r * T, (r + 1) * T)
            up = contract_rows(n_refs[r][...], grad_ref[rows, :])
            down = contract_rows(hid_ref[rows, :], cot_ref[block_at(order_ref, fixed, r)])
            if r == 0:
                up_acc[...] = up
                down_acc[...] = down
            else:
                up_acc[...] += up
                down_acc[...] += down
        for z in range(parts):
            out_ref[z, 0:depth, :] = up_acc[z * depth : (z + 1) * depth, :].astype(bf16)
            for q in range(D // F):
                out_ref[z, depth + q * units : depth + (q + 1) * units, :] = down_acc[
                    z * units : (z + 1) * units, q * F : (q + 1) * F].astype(bf16)

    return call(kernel, [order, *normed, cotangent, hidden, up_grad],
                [jax.ShapeDtypeStruct((parts, 2 * depth, F), bf16)],
                [pltpu.VMEM((D, F), f32), pltpu.VMEM((F, D), f32)], name)[0]


def feed_outputs(gathered, parts, D, name):
    C, _, F = gathered.shape
    depth, units = D // parts, F // parts
    FF, FZ = C * F, C * units

    def kernel(x_ref, up_ref, down_ref):
        for c in range(C):
            for z in range(parts):
                at = z * FZ + c * units
                up_ref[:, at : at + units] = x_ref[c, 0:depth, z * units : (z + 1) * units].astype(f32)
            for q in range(D // F):
                down_ref[c * units : (c + 1) * units, q * F : (q + 1) * F] = x_ref[
                    c, depth + q * units : depth + (q + 1) * units, :].astype(f32)

    return call(kernel, [gathered], [
        jax.ShapeDtypeStruct((depth, FF), f32), jax.ShapeDtypeStruct((FZ, D), f32)], [], name)


def times_weight(x, weight, columns, turned, order, ordered, cube, C, name):
    T = x.shape[0] // C
    D = weight.shape[0] if turned else columns

    shapes = [jax.ShapeDtypeStruct((C, T, D), bf16)] if ordered else parts_shapes(cube, C, T, D)

    def kernel(order_ref, x_ref, w_ref, *refs):
        outs, buf, sems = refs[: len(shapes)], refs[-2], refs[-1]
        going = Copies(sems)
        for r in range(C):
            rows = x_ref[r * T : (r + 1) * T, :]
            some = w_ref[:, :columns]
            value = times_transpose(rows, some) if turned else product(rows, some)
            buf[r] = value.astype(bf16)
            going.start(buf.at[r], outs[0].at[order_ref[r]] if ordered else part_at(cube, outs, r))
        going.finish()

    return call(kernel, [order, x, weight], shapes,
                [pltpu.VMEM((C, T, D), bf16), pltpu.SemaphoreType.DMA((C,))], name, (), range(len(shapes)))


def self_back(tokens, grads, weight, sums, me, cube, name):
    C = len(tokens)
    T, D = tokens[0].shape
    Z = sums.shape[0]
    DZ = D // Z
    width = weight.shape[1] // 3

    def kernel(me_ref, *refs):
        x_refs, (g_ref, w_ref, sums_ref, out_ref), outs = refs[:C], refs[C : C + 4], refs[C + 4 :]
        first = jnp.zeros((1, D), f32)
        second = jnp.zeros((1, D), f32)
        bias = jnp.zeros((1, 3 * width), f32)
        for r in range(C):
            rows = g_ref[r * T : (r + 1) * T, :]
            grad = times_transpose(rows, w_ref[...])
            store_part(cube, outs, r, grad.astype(bf16))
            scaled, _ = normalise(x_refs[r][...].astype(f32))
            first = first + jnp.sum(grad * scaled, axis=0, keepdims=True)
            second = second + jnp.sum(grad, axis=0, keepdims=True)
            bias = bias + jnp.sum(rows.astype(f32), axis=0, keepdims=True)
        lane = lax.broadcasted_iota(i32, (1, D), 1)
        spot = (lane >= me_ref[0] * width) & (lane < (me_ref[0] + 1) * width)

        def at_own(row):
            return jnp.where(spot, jnp.concatenate([row] * C, axis=1), 0.0)

        late = {0: first, 3: second, 6: at_own(bias[:, :width]), 7: at_own(bias[:, 2 * width :])}
        for z in range(Z):
            block = sums_ref[z]
            place = lax.broadcasted_iota(i32, block.shape, 0)
            for k, row in late.items():
                cut = row[:, z * DZ : (z + 1) * DZ]
                cut = jnp.concatenate([cut, jnp.zeros_like(cut)], axis=1)
                block = block + jnp.where(place == k, cut, 0.0)
            out_ref[z] = block.astype(bf16)

    shapes = [jax.ShapeDtypeStruct(sums.shape, bf16)] + parts_shapes(cube, C, T, D)
    return call(kernel, [me.reshape(1), *tokens, grads, weight, sums], shapes, [], name)


def contract_pieces(pieces, grads, name):
    C = len(pieces)
    T, D = pieces[0].shape
    N = grads.shape[1]

    def kernel(*refs):
        x_refs, (g_ref, out_ref, acc_ref) = refs[:C], refs[C:]
        for r in range(C):
            part = contract_rows(x_refs[r][...], g_ref[r * T : (r + 1) * T, :])
            if r == 0:
                acc_ref[...] = part
            else:
                acc_ref[...] += part
        out_ref[...] = acc_ref[...].astype(bf16)

    return call(kernel, [*pieces, grads], [jax.ShapeDtypeStruct((D, N), bf16)],
                [pltpu.VMEM((D, N), f32)], name)[0]


def after(x, *others):
    return lax.optimization_barrier((x, *others))[0]


def together(many, *others):
    return lax.optimization_barrier((*many, *others))[: len(many)]


def make_body(C, Z):
    cube = C == 8
    relative = [0, 2, 4, 6, 1, 3, 5, 7] if cube else list(range(C))

    def hop(x, bit):
        return lax.ppermute(x, "ctx", [(i, i ^ bit) for i in range(C)])

    def hop_diag(x):
        return lax.ppermute(x, "ctx", [(i, i ^ (4 if i & 1 else 2)) for i in range(C)])

    def gather_halves(x):
        if not cube:
            return [x, x, x], lambda hold: gather_steps(x, hold)
        odd = lax.axis_index("ctx") & 1
        own, ex, wy = hop(x, 1), hop(x, 2), hop(x, 4)

        def rest(hold):
            one, two = (ex, wy) if hold is None else together((ex, wy), hold)
            chosen = jnp.where(odd == 1, one, two)
            diag = hop_diag(chosen)
            first = [x, ex, wy, diag, own, hop(one, 1), hop(two, 1)]
            return first, chosen, lambda held: first + [hop(diag if held is None else after(diag, held), 1)]

        return [own, ex, wy], rest

    def gather_steps(x, hold):
        if not cube:
            whole = lax.all_gather(x, "ctx", axis=0, tiled=False)
            blocks = [whole[r] for r in range(C)]
            return blocks, x, lambda held: blocks
        return gather_halves(x)[1](hold)

    def gather_rows(x, hold=None):
        return gather_steps(x, hold)[2](None)

    def scatter_parts(parts):
        if not cube:
            done = lax.psum_scatter(parts[0], "ctx", scatter_dimension=0, tiled=False)
            return [done], done, done
        odd = lax.axis_index("ctx") & 1
        even, other_diag, others = parts[:4], parts[4], parts[5]
        got_diag = hop(other_diag, 1)
        got = hop(others, 1)
        second = (even[3].astype(f32) + got_diag.astype(f32)).astype(bf16)
        passed = hop_diag(second).astype(f32)
        ex = even[1].astype(f32) + got[1].astype(f32) + jnp.where(odd == 1, passed, 0.0)
        wy = even[2].astype(f32) + got[2].astype(f32) + jnp.where(odd == 1, 0.0, passed)
        third = wy.astype(bf16)
        got_x = hop(ex.astype(bf16), 2)
        got_y = hop(third, 4)
        return [even[0], got[0], got_x, got_y], second, third

    def tree_sum(blocks):
        parts = [blocks[relative.index(r)] for r in range(C)]
        while len(parts) > 1:
            parts = [parts[k] + parts[k + 1] for k in range(0, len(parts), 2)]
        return parts[0]

    def exchange(x):
        return lax.all_to_all(x, "ctx", split_axis=0, concat_axis=0, tiled=True)

    def zhop(x, d):
        return lax.ppermute(x, "fsdp", [(i, (i + d) % Z) for i in range(Z)])

    far_first = sorted(range(1, Z), key=lambda d: -min(d, Z - d))

    def zgather(x):
        got = {d: zhop(x, d) for d in far_first}
        return [x] + [got[d] for d in range(1, Z)]

    def zscatter(blocks, hold=None):
        got = lax.all_to_all(blocks, "fsdp", split_axis=0, concat_axis=0, tiled=True)
        if hold is not None:
            got = after(got, hold)
        return jnp.sum(got.astype(f32), axis=0)

    def body(
        tokens, encoded, cotangent, target_segments, source_segments, block_order,
        norm_gain, norm_shift, inward, inbias, outward, outbias, upward, upbias, downward, downbias,
    ):
        T, D = tokens.shape[1:]
        S = encoded.shape[1]
        L = C * T
        DZ = norm_gain.shape[1]
        FZ = downward.shape[0]
        FF = FZ * Z
        U = FZ // C
        width = D // C
        lanes = width % 128 == 0 and U % 128 == 0
        me = lax.axis_index("ctx")
        zi = lax.axis_index("fsdp")
        near = jnp.array(relative, i32)
        if cube:
            near = near ^ me
        zplace = (zi - jnp.arange(Z, dtype=i32)) % Z
        fixed = not cube
        steady = jnp.arange(C, dtype=i32)

        def mine(x, dims, axis):
            return lax.dynamic_index_in_dim(x.reshape(dims), me, axis, keepdims=False)

        def columns(groups, plan, shapes, dtype, name):
            if lanes:
                return spread_columns(groups, near, plan, shapes, dtype, name)
            outs = [[None] * (shape[0] if len(shape) == 3 else 1) for shape in shapes]
            for group, first, w, out, lead, base in sorted(plan, key=lambda p: p[5]):
                stacked = jnp.stack(groups[group])[:, : shapes[out][-2], first : first + w].astype(dtype)
                part = stacked.transpose(1, 0, 2).reshape(stacked.shape[1], -1)
                k = lead or 0
                outs[out][k] = part if outs[out][k] is None else jnp.concatenate([outs[out][k], part], axis=1)
            return [o[0] if len(shape) == 2 else jnp.stack(o) for o, shape in zip(outs, shapes)]

        small = jnp.concatenate(
            [norm_gain, norm_shift, inbias.reshape(4, DZ), outbias, downbias.reshape(1, DZ),
             upbias.reshape(FZ // DZ, DZ), jnp.zeros((19 - FZ // DZ, DZ), bf16)], axis=0)
        small = jnp.concatenate([small[:16], small[16:]], axis=1)
        F = Z * U
        if lanes:
            cut_a, cut_b = cut_weights(
                inward, outward, upward, downward, small, me, width, U, Z, "cut_weights")
        else:
            in_one = mine(inward[0], (DZ, 3, C, width), 2).reshape(DZ, 3 * width)
            in_two = mine(inward[1], (DZ, 3, C, width), 2).reshape(DZ, 3 * width)
            outs = mine(outward, (2, DZ, C, width), 2)
            cut_a = jnp.concatenate([in_one, outs[0], in_two[:, :width]], axis=1)
            cut_a = jnp.concatenate([cut_a, jnp.pad(small, ((0, 0), (0, 5 * width - 2 * DZ)))], axis=0)
            cut_up = mine(upward, (DZ, Z, C, U), 2).reshape(DZ, F)
            cut_down = mine(downward, (C, U, D), 0).reshape(U, D // F, F).transpose(1, 0, 2).reshape(DZ, F)
            cut_b = jnp.concatenate([in_two[:, width:], outs[1], cut_up, cut_down], axis=1)

        pieces_a = zgather(cut_a)
        token_start, token_chosen, token_join = gather_steps(after(tokens[0], cut_a), None)
        source_start, source_chosen, source_join = gather_steps(after(encoded[0], token_chosen), None)
        w_self, w_pair, vectors = assemble(
            list(together(pieces_a, token_chosen)), zplace, [3 * width, 2 * width], 16, "assemble_a")
        token_pieces = token_join(w_self)
        pair_start, pair_rest = gather_halves(w_pair)
        w_b = lax.all_gather(after(cut_b, w_self), "fsdp", axis=0, tiled=True)
        w_down = w_b[:, 3 * width + F :].reshape(Z, D // F, U, F).transpose(0, 2, 1, 3).reshape(F, D)
        w_out = w_b[:, 2 * width : 3 * width]
        gains, shifts = vectors[0:3], vectors[3:6]
        outb, downb = vectors[10:12], vectors[12]
        upb = vectors[13 : 13 + FZ // DZ].reshape(FZ // DZ, Z, DZ).transpose(1, 0, 2)
        upb = mine(upb.reshape(FF), (Z, C, U), 1).reshape(F)

        blocks = T // BLOCK
        index = jnp.arange(C * blocks, dtype=i32)
        order = block_order[0]
        by_device = order.reshape(1, C, blocks)
        near_order = jnp.sum(
            jnp.where(near[:, None, None] == jnp.arange(C, dtype=i32)[None, :, None], by_device, 0), axis=1
        ).reshape(-1)

        def inverted(table):
            return jnp.sum(jnp.where(table[None, :] == index[:, None], index[None, :], 0), axis=1)

        source_table = (near[:, None] * blocks + jnp.arange(blocks, dtype=i32)).reshape(-1)
        near_source = inverted(source_table)
        stored = inverted(order)
        near_stored = inverted(near_order)
        seg = target_segments[0]
        docs = jnp.arange(DOCS, dtype=i32)[:, None]
        own_doc = seg[None, :] == docs
        t_start = jnp.sum((seg[None, :] < docs).astype(i32), axis=1)
        s_start = jnp.sum((source_segments[0][None, :] < docs).astype(i32), axis=1)
        s_end = jnp.sum((source_segments[0][None, :] <= docs).astype(i32), axis=1)

        def per_row(table):
            return jnp.sum(jnp.where(own_doc, table[:, None], 0), axis=0).reshape(L // QB, QB)

        self_low = per_row(t_start)
        self_high = jnp.arange(1, L + 1, dtype=i32).reshape(L // QB, QB)
        cross_low, cross_high = per_row(s_start), per_row(s_end)
        self_first = self_low[:, 0] // BLOCK
        self_last = self_high[:, -1] // BLOCK
        cross_first = cross_low[:, 0] // BLOCK
        cross_last = (cross_high[:, -1] + BLOCK - 1) // BLOCK

        q1, k1, v1, normed_one = project(
            token_pieces, after(w_self, source_chosen, pair_start[0]), 0, vectors, [6, None, 7], me, (0, 3),
            near_order, [width] * 3, [False, True, True], "project_self")
        source_pieces = source_join(None)
        mixed1, wide1, inv1 = attend(
            (self_first, self_last, index, stored), after(q1, source_start[3]), k1, v1, self_low, self_high,
            "attend_self")
        pair = pair_rest(q1)[2](mixed1)
        cot = lax.all_gather(after(cotangent[0], q1), "ctx", axis=0, tiled=False)
        mixed_one = exchange(mixed1.reshape(C, T, width))

        after_self, kept_self, q2_own = mix(
            mixed_one, pair, near, fixed, tokens[0],
            jnp.stack([outb[0], gains[1], shifts[1], vectors[8]]), 0, width, True, "mix_self")
        q2 = exchange(q2_own).reshape(L, width)
        k2, v2 = project(
            source_pieces, after(w_b, q2_own), 0, vectors, [None, 9], me, None, source_table,
            [width] * 2, [True, True], "project_cross")
        mixed2, wide2, inv2 = attend(
            (cross_first, cross_last, stored, stored), q2, k2, v2, cross_low, cross_high,
            "attend_cross")
        kept_self = lax.all_gather(kept_self, "ctx", axis=0, tiled=True)
        out_two = gather_rows(after(w_out, q2_own), mixed2)
        mixed_two = exchange(mixed2.reshape(C, T, width))
        after_cross, kept_cross, normed_three = mix(
            mixed_two, out_two, near, fixed, after_self,
            jnp.stack([outb[1], gains[2], shifts[2]]), 0, width, False, "mix_cross")

        kept_cross = lax.all_gather(after(kept_cross, kept_self), "ctx", axis=0, tiled=True)

        n3 = gather_rows(normed_three)
        hidden, up_grad, upb_tp, *parts = feed(
            n3, cot, near, fixed, w_b, 3 * width, w_down, upb[None], cube, "feed")
        back_three, second, third = scatter_parts(parts)
        feed_dw = feed_weights(
            n3, cot, near, fixed, hidden, after(up_grad, third), Z, "feed_weights")
        feed_sum = lax.psum_scatter(feed_dw, "fsdp", scatter_dimension=0, tiled=False)


        cross_grad, m2_own, sums_three = unmix(
            back_three, None, None, out_two, near, fixed, (0, 0), after(cotangent[0], feed_dw), after_cross,
            gains[2:3], width, "unmix_cross")
        m2 = exchange(m2_own).reshape(L, 2 * width)
        out_parts = times_weight(
            hidden, after(w_down, m2_own), D, False, near, False, cube, C, "feed_out")
        out_terms, out_second, out_third = scatter_parts(out_parts)
        dq2, dkv2 = attend_back(
            (cross_first, cross_last, stored, stored, stored, near_source),
            q2, k2, v2, cross_low, cross_high, after(m2, out_parts[0]), wide2, inv2, False, "attend_cross_back")
        layer_out = (after_cross + (sum(t.astype(f32) for t in out_terms) + downb)).astype(bf16)
        dq2_own = exchange(dq2.reshape(C, T, width))
        (source_part,) = times_weight(dkv2, w_b, 2 * width, True, near, True, cube, C, "source_back")
        encoded_grad = lax.psum_scatter(source_part, "ctx", scatter_dimension=0, tiled=False).astype(f32)
        self_grad, m1_own, sums_two = unmix(
            [], dq2_own, pair, pair, near, fixed, (width, 0), after(cross_grad, source_part, out_third), after_self,
            gains[1:2], width, "unmix_self")


        m1 = exchange(m1_own).reshape(L, 2 * width)
        group_one = jnp.concatenate([
            contract_rows(kept_self[:, D:], after(dq2, m1_own)).astype(bf16),
            contract_rows(kept_cross, after(m2, m1_own)[:, width:]).astype(bf16),
            contract_pieces(source_pieces, after(dkv2, m1_own), "source_weights"),
        ], axis=1).reshape(Z, DZ, 4 * width)
        feed_all = lax.all_gather(after(feed_sum, m1_own), "ctx", axis=0, tiled=False)
        m1 = after(m1, group_one)
        group_one = zscatter(group_one).astype(bf16)
        (dqkv,) = attend_back(
            (self_first, self_last, index, stored, near_stored, near_stored),
            q1, k1, v1, self_low, self_high, m1, wide1, inv1, True, "attend_self_back")
        def placed(part, count):
            part = part.reshape(count, 1, -1)
            spot = lax.broadcasted_iota(i32, (count, C, part.shape[2]), 1) == me
            return jnp.where(spot, part, 0.0)

        dkv2_sum = placed(jnp.sum(dkv2[:, width:].astype(f32), axis=0), 1).reshape(D)
        upb_rows = placed(upb_tp, Z).reshape(Z, FZ // DZ, DZ)
        none = jnp.zeros((D,), f32)
        sums = jnp.stack([
            none, sums_two[0], sums_three[0], none, sums_two[1], sums_three[1],
            none, none, sums_two[3], dkv2_sum, sums_two[2], sums_three[2], sums_three[3],
        ])
        count = 13 + FZ // DZ
        sums = jnp.concatenate([
            sums.reshape(13, Z, DZ).transpose(1, 0, 2), upb_rows, jnp.zeros((Z, 32 - count, DZ), f32)], axis=1)
        sums = jnp.concatenate([sums[:, :16], sums[:, 16:]], axis=2)
        sums, *parts_one = self_back(
            token_pieces, dqkv, w_self, after(sums, m1), me, cube, "self_back")
        back_one, _, back_third = scatter_parts(parts_one)
        group_two = jnp.concatenate([
            contract_rows(kept_self[:, :D], m1[:, width:]).astype(bf16),
            contract_rows(normed_one, after(dqkv, encoded_grad)).astype(bf16),
        ], axis=1)
        group_two = jnp.concatenate([group_two.reshape(Z, DZ, 4 * width), sums], axis=1)
        group_two = zscatter(after(group_two, group_one), back_third).astype(bf16)
        one_start, one_chosen, one_join = gather_steps(after(group_one, parts_one[0]), back_third)
        group_one = one_join(None)
        upward_grad, down_grad = feed_outputs(after(feed_all, back_third), Z, D, "feed_outputs")
        tokens_grad, _ = unmix(
            back_one, None, None, None, near, fixed, (0, 0),
            after(self_grad, upward_grad, one_chosen, group_two, layer_out), tokens[0], gains[0:1], width, "unmix_tokens")
        group_two = gather_rows(after(group_two, tokens_grad))
        part = tree_sum([g[DZ:].astype(f32) for g in group_two])
        part = jnp.concatenate([part[:, :DZ], part[:, DZ:]], axis=0)[:count]

        inward_grad, outward_grad = columns(
            [group_one, group_two],
            [(1, (k + 1) * width, width, 0, 0, k * D) for k in range(3)]
            + [(0, 0, width, 0, 1, 0)]
            + [(0, (k + 2) * width, width, 0, 1, (k + 1) * D) for k in range(2)]
            + [(1, 0, width, 1, 0, 0), (0, width, width, 1, 1, 0)],
            [(2, DZ, 3 * D), (2, DZ, D)], f32, "spread_rest")

        return (
            layer_out[None], tokens_grad[None], encoded_grad[None],
            part[0:3], part[3:6], inward_grad, part[6:10].reshape(2, 2, DZ), outward_grad,
            part[10:12], upward_grad, part[13:].reshape(FZ), down_grad, part[12],
        )

    return body


def solution(mesh):
    rows = P("fsdp", "ctx", None)
    placed = (
        rows, rows, rows, P("fsdp", None), P("fsdp", None), P("fsdp", None),
        P(None, "fsdp"), P(None, "fsdp"), P(None, "fsdp", None), P(None, None, "fsdp"),
        P(None, "fsdp", None), P(None, "fsdp"), P("fsdp", None), P("fsdp"), P("fsdp", None), P("fsdp"),
    )
    return jax.shard_map(
        make_body(mesh.shape["ctx"], mesh.shape["fsdp"]),
        mesh=mesh,
        in_specs=placed,
        out_specs=(
            rows, rows, rows, P(None, "fsdp"), P(None, "fsdp"), P(None, "fsdp", None),
            P(None, None, "fsdp"), P(None, "fsdp", None), P(None, "fsdp"), P("fsdp", None),
            P("fsdp"), P("fsdp", None), P("fsdp"),
        ),
        check_vma=False,
    )
```
